32 devices in a mesh: dp: 2 (over y), row: 4 (over x, core), col: 4 (over z).
Axes of the slice: x: 2, y: 2, z: 4, core: 2. Of those that a mesh axis runs over, the one named last changes fastest.
Arguments:
- features: bfloat16 [2, 32, 512, 256], P('dp', 'row', 'col'), may hold values from -6 to 6
- reduce_weight: bfloat16 [256, 128], replicated, may hold values from -0.375 to 0.375
- scale_one: float32 [128], replicated, may hold values from 0.25 to 1.75
- shift_one: float32 [128], replicated, may hold values from -3 to 3
- group_weight: bfloat16 [3, 3, 4, 128], replicated, may hold values from -1 to 1
- scale_two: float32 [128], replicated, may hold values from 0.25 to 1.75
- shift_two: float32 [128], replicated, may hold values from -3 to 3
- expand_weight: bfloat16 [128, 256], replicated, may hold values from -0.5 to 0.5
- scale_three: float32 [256], replicated, may hold values from 0.25 to 1.75
- shift_three: float32 [256], replicated, may hold values from -3 to 3
- cotangent: bfloat16 [2, 32, 512, 256], P('dp', 'row', 'col'), may hold values from -6 to 6
Outputs:
- input_grad: bfloat16 [2, 32, 512, 256], P('dp', 'row', 'col')
- reduce_grad: float32 [256, 128], P('dp')
- group_grad: float32 [128, 3, 3, 4], P('dp')
- expand_grad: float32 [128, 256], P('dp')
The draws below stay inside these ranges and needn't reach their ends.
All inputs are finite; a program needn't handle non-finite values.
Results may differ from the reference program's by a relative error of at most 0.0069.
Values may be sent and summed in bfloat16 or wider, within the bound.
No kernel may reach another device: no remote copies, remote signals or barrier semaphores. Data moves between devices by JAX's collectives and lax.ppermute only.
A program may use at most 128 MiB of HBM per device.

```python
import jax
import jax.numpy as jnp
from jax import lax

C = 256
WIDTH = 128
GROUPS = 32
GROUP_CH = 4
BANDS = 2
HEIGHT = 32
BAND_W = 512
PIXELS = 32768


def with_spikes(drawn, stream_key, source, target, shards_of, factor):
    owner, partner = [(jnp.arange(drawn.shape[dim]) // (drawn.shape[dim] // shards_of)).reshape([-1 if axis == dim else 1 for axis in range(drawn.ndim)]) for dim in (source, target)]
    chosen = jax.random.permutation(stream_key, shards_of)[partner]
    strong = (owner == chosen) | (owner == (partner + shards_of // 2) % shards_of)
    return jnp.where(strong, factor * drawn, drawn)


def block_scale(rng, shape, cuts, smallest, largest):
    factor_of = 1.0
    for dim, parts in cuts:
        steps = jax.random.uniform(jax.random.fold_in(jax.random.fold_in(rng, 6), dim), (parts,), jnp.float32, smallest / len(cuts), largest / len(cuts))
        factor_of = factor_of * jnp.repeat(jnp.exp(steps), shape[dim] // parts).reshape((-1,) + (1,) * (len(shape) - 1 - dim))
    return factor_of


def gaussian(stream_key, extent, width, bound, split=(), dtype=jnp.bfloat16):
    values = jax.random.normal(stream_key, extent, jnp.float32) * width
    if len(split) > 0:
        values = block_scale(stream_key, extent, split, -0.22, 0.18) * values
    return jnp.clip(values, min=-bound, max=bound).astype(dtype)


def gaussian_with(stream_key, dims, spread, limit, pieces, heavy, dtype=jnp.bfloat16):
    entries = spread * jax.random.normal(stream_key, dims, jnp.float32)
    if pieces:
        entries = entries * block_scale(stream_key, dims, pieces, -0.22, 0.18)
    return jnp.clip(with_spikes(entries, jax.random.fold_in(stream_key, 3), *heavy), -limit, limit).astype(dtype)


def setup_inputs(seed: int = 0) -> dict:
    key_list = jax.random.split(jax.random.key(seed), 12)
    features = gaussian_with(key_list[0], (BANDS, HEIGHT, BAND_W, C), 1.0, 6.0, ((0, 2), (1, 4), (2, 4)), (0, 3, 2, 2.0))
    reduce_weight = gaussian(key_list[1], (C, WIDTH), C ** -0.5, 0.375)
    scale_one = jnp.clip(1.0 + 0.15 * jax.random.normal(key_list[2], (WIDTH,), jnp.float32), 0.25, 1.75)
    shift_one = gaussian(key_list[3], (WIDTH,), 0.5, 3.0, (), jnp.float32)
    group_weight = gaussian(key_list[4], (3, 3, GROUP_CH, WIDTH), (9 * GROUP_CH) ** -0.5, 1.0)
    scale_two = jnp.clip(1.0 + 0.15 * jax.random.normal(key_list[5], (WIDTH,), jnp.float32), 0.25, 1.75)
    shift_two = gaussian(key_list[6], (WIDTH,), 0.5, 3.0, (), jnp.float32)
    expand_weight = gaussian(key_list[7], (WIDTH, C), WIDTH ** -0.5, 0.5)
    scale_three = jnp.clip(1.0 + 0.15 * jax.random.normal(key_list[8], (C,), jnp.float32), 0.25, 1.75)
    shift_three = gaussian(key_list[9], (C,), 0.5, 3.0, (), jnp.float32)
    cotangent = gaussian(key_list[10], (BANDS, HEIGHT, BAND_W, C), 1.0, 6.0, ((0, 2), (1, 4), (2, 4)))
    return {"features": features, "reduce_weight": reduce_weight, "scale_one": scale_one, "shift_one": shift_one, "group_weight": group_weight, "scale_two": scale_two, "shift_two": shift_two, "expand_weight": expand_weight, "scale_three": scale_three, "shift_three": shift_three, "cotangent": cotangent}


def dsilu(value):
    sg = jax.nn.sigmoid(value)
    return sg * (1.0 + value * (1.0 - sg))

def group_conv(inputs, kernel, pads, exact):
    return lax.conv_general_dilated(inputs, kernel, (1, 1), pads, dimension_numbers=('NHWC', 'HWIO', 'NHWC'), feature_group_count=GROUPS, preferred_element_type=jnp.float32, precision=lax.Precision.HIGHEST if exact else None)

def one_band(band, cot_band, reduce_weight, scale_one, shift_one, group_weight, scale_two, shift_two, expand_weight, scale_three, shift_three):
    flat = band.reshape(-1, C)
    pre_one = jnp.dot(flat, reduce_weight, preferred_element_type=jnp.float32) * scale_one + shift_one
    act_one = jax.nn.silu(pre_one).astype(jnp.bfloat16)
    img_one = act_one.reshape(1, HEIGHT, BAND_W, WIDTH)
    pre_two = group_conv(img_one, group_weight, ((1, 1), (1, 1)), False).reshape(-1, WIDTH) * scale_two + shift_two
    act_two = jax.nn.silu(pre_two).astype(jnp.bfloat16)
    pre_three = jnp.dot(act_two, expand_weight, preferred_element_type=jnp.float32) * scale_three + shift_three + flat.astype(jnp.float32)
    back_three = cot_band.reshape(-1, C).astype(jnp.float32) * dsilu(pre_three)
    grad_three = (back_three * scale_three).astype(jnp.bfloat16)
    grad_two = (jnp.dot(grad_three, expand_weight.T, preferred_element_type=jnp.float32) * dsilu(pre_two) * scale_two).astype(jnp.bfloat16)
    gimg = grad_two.reshape(1, HEIGHT, BAND_W, WIDTH).astype(jnp.float32)
    kernel32 = group_weight.astype(jnp.float32)
    act32 = img_one.astype(jnp.float32)
    back_one = jax.vjp(lambda u: group_conv(u, kernel32, ((1, 1), (1, 1)), True), act32)[1](gimg)[0]
    gw_two = jax.vjp(lambda k: group_conv(act32, k, ((1, 1), (1, 1)), True), kernel32)[1](gimg)[0]
    grad_one = (back_one.reshape(-1, WIDTH) * dsilu(pre_one) * scale_one).astype(jnp.bfloat16)
    input_grad = (jnp.dot(grad_one, reduce_weight.T, preferred_element_type=jnp.float32) + back_three).astype(jnp.bfloat16)
    gw_three = lax.dot_general(act_two, grad_three, (((0,), (0,)), ((), ())), preferred_element_type=jnp.float32)
    gw_one = lax.dot_general(flat, grad_one, (((0,), (0,)), ((), ())), preferred_element_type=jnp.float32)
    return (input_grad.reshape(HEIGHT, BAND_W, C), gw_one, gw_two, gw_three)

def reference(features, reduce_weight, scale_one, shift_one, group_weight, scale_two, shift_two, expand_weight, scale_three, shift_three, cotangent):

    def step(pair):
        return one_band(pair[0], pair[1], reduce_weight, scale_one, shift_one, group_weight, scale_two, shift_two, expand_weight, scale_three, shift_three)
    input_grad, gw_one, gw_two, gw_three = lax.map(step, (features, cotangent))
    factor = 1.0 / jnp.sqrt(jnp.float32(PIXELS))
    reduce_grad = lax.optimization_barrier(jnp.sum(gw_one, axis=0)) * factor
    group_grad = jnp.transpose(lax.optimization_barrier(jnp.sum(gw_two, axis=0)), (3, 0, 1, 2)) * factor
    expand_grad = lax.optimization_barrier(jnp.sum(gw_three, axis=0)) * factor
    return (input_grad, reduce_grad, group_grad, expand_grad)
```

```python
import functools

import jax
import jax.numpy as jnp
from jax import lax
from jax.experimental import pallas as pl
from jax.experimental.pallas import tpu as pltpu
from jax.sharding import PartitionSpec as P

BF = jnp.bfloat16
F32 = jnp.float32
SIDE = 8
GROUP_ROWS = 40


def pairings(count):
    out = []
    for start in (0, 1):
        perm = []
        for i in range(count):
            other = ((i - start) ^ 1) + start
            perm.append((i, other if i >= start and other < count else i))
        out.append(perm)
    return out


def swap_edges(pick, axis):
    even, odd = pairings(lax.axis_size(axis))
    is_odd = lax.axis_index(axis) % 2
    got_even = lax.ppermute(pick(is_odd == 0), axis, even)
    got_odd = lax.ppermute(pick(is_odd == 1), axis, odd)
    return got_even, got_odd


def dot(a, b):
    return jnp.dot(a, b, preferred_element_type=F32)


def gate(v):
    return 0.5 + 0.5 * jnp.tanh(0.5 * v)


def unit_kernel(
    pos, x_ref, c_ref, row_even, row_odd, col_even, col_odd, w1_ref, s1_ref, b1_ref, gw_ref, s2_ref, b2_ref,
    w3_ref, s3_ref, b3_ref, out_ref, share_ref, xs, cs, acts, gcat, d1, back, act2, g3, w2, w2t,
    *, rows, cols, chans, inner, group_ch,
):
    wide = cols + 2 * SIDE
    row_odd_p, col_odd_p = pos[0], pos[1]
    has_low_row, has_high_row, has_low_col, has_high_col = (pos[i].astype(F32) for i in range(2, 6))
    sub = lax.broadcasted_iota(jnp.int32, (inner, inner), 0)
    lane = lax.broadcasted_iota(jnp.int32, (inner, inner), 1)
    diag = jnp.where(sub // group_ch == lane // group_ch, 1.0, 0.0).astype(F32)
    for t in range(9):
        four = gw_ref[t * group_ch : (t + 1) * group_ch, :]
        eight = jnp.concatenate([four, four], axis=0)
        tiled = jnp.broadcast_to(eight[None], (inner // 8, 8, inner)).reshape(inner, inner)
        dense = tiled * diag
        w2[t * inner : (t + 1) * inner, :] = dense.astype(BF)
        w2t[(8 - t) * inner : (9 - t) * inner, :] = dense.T.astype(BF)
    def row_halo(i, low):
        a, b = row_even[i].astype(F32), row_odd[i].astype(F32)
        take_odd = (row_odd_p == 0) if low else (row_odd_p == 1)
        return jnp.where(take_odd, b, a).astype(BF)

    def col_halo(i):
        a, b = col_even[i].astype(F32), col_odd[i].astype(F32)
        odd = col_odd_p == 1
        return jnp.concatenate([jnp.where(odd, b, a), jnp.where(odd, a, b)], axis=0).astype(BF)

    for r in range(rows + 4):
        if r < 2:
            main = row_halo(r, True)
        elif r < rows + 2:
            main = x_ref[r - 2]
        else:
            main = row_halo(r - rows - 2, False)
        xs[r, 0:cols, :] = main
        xs[r, cols:wide, :] = col_halo(r)
    for r in range(rows + 2):
        if r < 1:
            main = row_halo(2, True)
        elif r < rows + 1:
            main = c_ref[r - 1]
        else:
            main = row_halo(2, False)
        cs[r, 0:cols, :] = main
        cs[r, cols:wide, :] = col_halo(rows + 4 + r)
    spot = lax.broadcasted_iota(jnp.int32, (wide, inner), 0)
    col_ok = jnp.where(spot < cols, 1.0, jnp.where(spot < cols + SIDE, has_high_col, has_low_col))

    def spread(ref, r, v):
        ref[r, :, 0:inner] = pltpu.roll(v, 1, 0).astype(BF)
        ref[r, :, inner : 2 * inner] = v.astype(BF)
        ref[r, :, 2 * inner :] = pltpu.roll(v, wide - 1, 0).astype(BF)

    s1, b1, w1 = s1_ref[...], b1_ref[...], w1_ref[...]
    step = 2
    for r0 in range(0, rows + 4, step):
        pre = dot(xs[r0 : r0 + step].reshape(step * wide, chans), w1) * s1 + b1
        sg = gate(pre)
        act = pre * sg
        for k in range(step):
            r = r0 + k
            a = act[k * wide : (k + 1) * wide] * col_ok
            if r < 2:
                a = a * has_low_row
            if r >= rows + 2:
                a = a * has_high_row
            spread(acts, r, a)
            if 2 <= r < rows + 2:
                at = slice(k * wide, k * wide + cols)
                d1[(r - 2) * cols : (r - 1) * cols, :] = (sg[at] + act[at] * (1.0 - sg[at])) * s1
    s2, b2, w3, s3, b3 = s2_ref[...], b2_ref[...], w3_ref[...], s3_ref[...], b3_ref[...]
    w3t = w3.T
    for q0 in range(0, rows + 2, step):
        conv = jnp.zeros((step * wide, inner), F32)
        for dh in range(3):
            conv = conv + dot(
                acts[q0 + dh : q0 + dh + step].reshape(step * wide, 3 * inner),
                w2[dh * 3 * inner : (dh + 1) * 3 * inner, :],
            )
        pre2 = conv * s2 + b2
        sg2 = gate(pre2)
        silu2 = pre2 * sg2
        a2 = silu2.astype(BF)
        dd2 = (sg2 + silu2 * (1.0 - sg2)) * s2
        skip = xs[q0 + 1 : q0 + 1 + step].reshape(step * wide, chans).astype(F32)
        pre3 = dot(a2, w3) * s3 + b3 + skip
        sg3 = gate(pre3)
        ct = cs[q0 : q0 + step].reshape(step * wide, chans).astype(F32)
        back3 = ct * (sg3 + pre3 * sg3 * (1.0 - sg3))
        grad3 = (back3 * s3).astype(BF)
        grad2 = dot(grad3, w3t) * dd2
        for k in range(step):
            q = q0 + k
            g = grad2[k * wide : (k + 1) * wide] * col_ok
            if q < 1:
                g = g * has_low_row
            if q >= rows + 1:
                g = g * has_high_row
            spread(gcat, q, g)
            if 1 <= q < rows + 1:
                at = slice(k * wide, k * wide + cols)
                to = slice((q - 1) * cols, q * cols)
                back[to, :] = back3[at]
                act2[to, :] = a2[at]
                g3[to, :] = grad3[at]
    n_dp = share_ref.shape[0]
    gw3 = dot(act2[...].T, g3[...])
    own_g = gcat[1 : rows + 1, 0:cols, inner : 2 * inner].reshape(rows * cols, inner)
    own_gt = own_g.T
    pick_sub = lax.broadcasted_iota(jnp.int32, (3 * inner, inner), 0)
    pick_lane = lax.broadcasted_iota(jnp.int32, (3 * inner, inner), 1)
    compact = jnp.zeros((inner, inner), F32)
    diag3 = jnp.concatenate([diag, diag, diag], axis=1)
    for dh in range(3):
        near = acts[dh + 1 : dh + 1 + rows, 0:cols, :].reshape(rows * cols, 3 * inner)
        full = (dot(own_gt, near) * diag3).astype(BF)
        place = (dh * 3 + pick_sub // inner) * group_ch + pick_sub % group_ch
        compact = compact + dot(full, jnp.where(pick_lane == place, 1.0, 0.0).astype(BF))
    gw2 = compact.T[0:GROUP_ROWS]
    w1t = w1.T
    gw1t = jnp.zeros((inner, chans), F32)
    for p0 in range(0, rows, step):
        conv = jnp.zeros((step * cols, inner), F32)
        for dh in range(3):
            conv = conv + dot(
                gcat[p0 + dh : p0 + dh + step, 0:cols, :].reshape(step * cols, 3 * inner),
                w2t[dh * 3 * inner : (dh + 1) * 3 * inner, :],
            )
        at = slice(p0 * cols, (p0 + step) * cols)
        g1 = (conv * d1[at, :]).astype(BF)
        gw1t = gw1t + dot(g1.T, x_ref[p0 : p0 + step].reshape(step * cols, chans))
        out = dot(g1, w1t) + back[at, :]
        out_ref[p0 : p0 + step] = out.astype(BF).reshape(step, cols, chans)
    gw1 = gw1t.T
    one, three = chans // n_dp, inner // n_dp
    for h in range(n_dp):
        share_ref[h, 0:one, :] = gw1[h * one : (h + 1) * one].astype(BF)
        for k in range(chans // inner):
            share_ref[h, one + k * three : one + (k + 1) * three, :] = gw3[
                h * three : (h + 1) * three, k * inner : (k + 1) * inner
            ].astype(BF)
        base = one + three * (chans // inner)
        share_ref[h, base : base + GROUP_ROWS, :] = gw2.astype(BF)


def swap_sum(value, axis, bit):
    count = lax.axis_size(axis)
    other = lax.ppermute(value, axis, [(i, i ^ bit) for i in range(count)])
    return (value.astype(F32) + other.astype(F32)).astype(value.dtype)


def body(
    features, reduce_weight, scale_one, shift_one, group_weight, scale_two, shift_two, expand_weight, scale_three,
    shift_three, cotangent,
):
    _, rows, cols, chans = features.shape
    inner = reduce_weight.shape[1]
    group_ch = group_weight.shape[2]
    x, c = features[0], cotangent[0]
    n_dp, n_row, n_col = (lax.axis_size(a) for a in ("dp", "row", "col"))
    dp, row, col = (lax.axis_index(a) for a in ("dp", "row", "col"))

    def row_edge(high):
        edge = lax.dynamic_slice_in_dim(x, jnp.where(high, rows - 2, 0), 2, axis=0)
        cot = lax.dynamic_slice_in_dim(c, jnp.where(high, rows - 1, 0), 1, axis=0)
        return jnp.concatenate([edge, cot], axis=0)

    row_even, row_odd = swap_edges(row_edge, "row")

    def col_edge(high):
        def cut(v):
            return lax.dynamic_slice_in_dim(v, jnp.where(high, cols - SIDE, 0), SIDE, axis=1)

        even, odd = cut(row_even), cut(row_odd)
        low = jnp.where(row % 2 == 0, odd, even)
        top = jnp.where(row % 2 == 0, even, odd)
        return jnp.concatenate([low[0:2], cut(x), top[0:2], low[2:3], cut(c), top[2:3]], axis=0)

    col_even, col_odd = swap_edges(col_edge, "col")
    pos = jnp.stack([row % 2, col % 2, row > 0, row < n_row - 1, col > 0, col < n_col - 1]).astype(jnp.int32)
    wide = cols + 2 * SIDE
    share_rows = chans // n_dp + (inner // n_dp) * (chans // inner) + GROUP_ROWS
    vmem = pl.BlockSpec(memory_space=pltpu.VMEM)
    input_grad, shares = pl.pallas_call(
        functools.partial(unit_kernel, rows=rows, cols=cols, chans=chans, inner=inner, group_ch=group_ch),
        out_shape=(
            jax.ShapeDtypeStruct((rows, cols, chans), BF),
            jax.ShapeDtypeStruct((n_dp, share_rows, inner), BF),
        ),
        in_specs=[pl.BlockSpec(memory_space=pltpu.SMEM)] + [vmem] * 15,
        out_specs=(vmem, vmem),
        scratch_shapes=[
            pltpu.VMEM((rows + 4, wide, chans), BF),
            pltpu.VMEM((rows + 2, wide, chans), BF),
            pltpu.VMEM((rows + 4, wide, 3 * inner), BF),
            pltpu.VMEM((rows + 2, wide, 3 * inner), BF),
            pltpu.VMEM((rows * cols, inner), F32),
            pltpu.VMEM((rows * cols, chans), F32),
            pltpu.VMEM((rows * cols, inner), BF),
            pltpu.VMEM((rows * cols, chans), BF),
            pltpu.VMEM((9 * inner, inner), BF),
            pltpu.VMEM((9 * inner, inner), BF),
        ],
        compiler_params=pltpu.CompilerParams(vmem_limit_bytes=40 << 20),
        name="unit",
    )(
        pos, x, c, row_even, row_odd, col_even, col_odd, reduce_weight, scale_one[None], shift_one[None],
        group_weight.astype(F32).reshape(9 * group_ch, inner), scale_two[None], shift_two[None], expand_weight,
        scale_three[None], shift_three[None],
    )
    held = n_dp
    while held > 1:
        half = held // 2
        bit = (dp // half) % 2
        mine = lax.dynamic_slice_in_dim(shares, bit * half, half, axis=0)
        theirs = lax.dynamic_slice_in_dim(shares, (1 - bit) * half, half, axis=0)
        other = lax.ppermute(theirs, "dp", [(i, i ^ half) for i in range(n_dp)])
        shares = (mine.astype(F32) + other.astype(F32)).astype(BF)
        held = half
    total = shares[0]
    steps = [(a, 1 << k) for a, n in (("row", n_row), ("col", n_col)) for k in range(n.bit_length() - 1)]
    for axis, bit in steps[:-1]:
        total = swap_sum(total, axis, bit)
    axis, bit = steps[-1]
    other = lax.ppermute(total, axis, [(i, i ^ bit) for i in range(lax.axis_size(axis))])
    pixels = rows * cols * n_dp * n_row * n_col
    total = (total.astype(F32) + other.astype(F32)) * (1.0 / jnp.sqrt(F32(pixels)))
    one, three = chans // n_dp, inner // n_dp
    base = one + three * (chans // inner)
    expand_grad = jnp.concatenate(
        [total[one + k * three : one + (k + 1) * three] for k in range(chans // inner)], axis=1
    )
    group = lax.dynamic_slice_in_dim(total[base : base + 9 * group_ch], dp * three, three, axis=1)
    group_grad = jnp.transpose(group.reshape(3, 3, group_ch, three), (3, 0, 1, 2))
    return input_grad[None], total[0:one], group_grad, expand_grad


def solution(mesh):
    image = P("dp", "row", "col", None)
    return jax.shard_map(
        body,
        mesh=mesh,
        in_specs=(image,) + (P(),) * 9 + (image,),
        out_specs=(image, P("dp", None), P("dp", None, None, None), P("dp", None)),
        check_vma=False,
    )
```

```python
import functools

import jax
import jax.numpy as jnp
from jax import lax
from jax.experimental import pallas as pl
from jax.experimental.pallas import tpu as pltpu
from jax.sharding import PartitionSpec as P

BF = jnp.bfloat16
F32 = jnp.float32
EDGE = 2
STRIP = 16
GROUP_ROWS = 24


def pairings(count):
    out = []
    for start in (0, 1):
        perm = []
        for i in range(count):
            other = ((i - start) ^ 1) + start
            perm.append((i, other if i >= start and other < count else i))
        out.append(perm)
    return out


def swap_edges(pick, axis):
    even, odd = pairings(lax.axis_size(axis))
    is_odd = lax.axis_index(axis) % 2
    got_even = lax.ppermute(pick(is_odd == 0), axis, even)
    got_odd = lax.ppermute(pick(is_odd == 1), axis, odd)
    return got_even, got_odd


def dot(a, b):
    return jnp.dot(a, b, preferred_element_type=F32)


def gate(v):
    return 0.5 + 0.5 * jnp.tanh(0.5 * v)


def column_mask(pos, wide, cols, inner):
    spot = lax.broadcasted_iota(jnp.int32, (wide, inner), 0)
    has_low, has_high = pos[3].astype(F32), pos[4].astype(F32)
    return jnp.where(spot < cols, 1.0, jnp.where(spot < cols + STRIP // 2, has_high, has_low))


def vectors(ref, inner):
    return [ref[i : i + 1, 0:inner] for i in range(4)] + [ref[4:5, :], ref[5:6, :]]


def spread(ref, r, v):
    wide, inner = v.shape
    ref[r, :, 0:inner] = pltpu.roll(v, 1, 0).astype(BF)
    ref[r, :, inner : 2 * inner] = v.astype(BF)
    ref[r, :, 2 * inner :] = pltpu.roll(v, wide - 1, 0).astype(BF)


def conv3(windows, w_ref):
    n = w_ref.shape[0] // 3
    out = dot(windows(0), w_ref[0:n, :])
    for dh in (1, 2):
        out = out + dot(windows(dh), w_ref[dh * n : (dh + 1) * n, :])
    return out


def reduce_act(x, w1, s1, b1):
    pre = dot(x, w1) * s1 + b1
    sg = gate(pre)
    return pre * sg, sg


def through(conv, skip, ct, s2, b2, w3, w3t, s3, b3):
    pre2 = conv * s2 + b2
    sg2 = gate(pre2)
    silu2 = pre2 * sg2
    a2 = silu2.astype(BF)
    pre3 = dot(a2, w3) * s3 + b3 + skip.astype(F32)
    sg3 = gate(pre3)
    back3 = ct.astype(F32) * (sg3 + pre3 * sg3 * (1.0 - sg3))
    grad3 = (back3 * s3).astype(BF)
    grad2 = dot(grad3, w3t) * ((sg2 + silu2 * (1.0 - sg2)) * s2)
    return a2, grad3, back3, grad2


def weights_kernel(gw_ref, w3_ref, w2, w2t, w3t, *, inner, group_ch):
    sub = lax.broadcasted_iota(jnp.int32, (inner, inner), 0)
    lane = lax.broadcasted_iota(jnp.int32, (inner, inner), 1)
    diag = jnp.where(sub // group_ch == lane // group_ch, 1.0, 0.0).astype(F32)
    for t in range(9):
        four = gw_ref[t * group_ch : (t + 1) * group_ch, :]
        eight = jnp.concatenate([four, four], axis=0)
        tiled = jnp.broadcast_to(eight[None], (inner // 8, 8, inner)).reshape(inner, inner)
        dense = tiled * diag
        w2[t * inner : (t + 1) * inner, :] = dense.astype(BF)
        w2t[(8 - t) * inner : (9 - t) * inner, :] = dense.T.astype(BF)
    w3t[...] = w3_ref[...].T


def inner_kernel(
    pos, x_ref, c_ref, strip_ref, w1_ref, vec_ref, w2, w2t, w3_ref, w3t_ref,
    acts, gcat, d1, back, g1, gw3_ref, full_ref, gw1t_ref, xs, cs,
    *, rows, cols, chans, inner,
):
    wide = cols + STRIP
    step = 2
    col_ok = column_mask(pos, wide, cols, inner)
    s1, b1, s2, b2, s3, b3 = vectors(vec_ref, inner)
    w1 = w1_ref[...]
    for r in range(rows):
        xs[r, 0:cols, :] = x_ref[r]
        xs[r, cols:wide, :] = strip_ref[r]
        cs[r, 0:cols, :] = c_ref[r]
        cs[r, cols:wide, :] = strip_ref[rows + r]
    for r0 in range(0, rows, step):
        act, sg = reduce_act(xs[r0 : r0 + step].reshape(step * wide, chans), w1, s1, b1)
        slope = (sg + act * (1.0 - sg)) * s1
        for k in range(step):
            r = r0 + k
            spread(acts, r, act[k * wide : (k + 1) * wide] * col_ok)
            d1[r * cols : (r + 1) * cols, :] = slope[k * wide : k * wide + cols]
    rest = (s2, b2, w3_ref[...], w3t_ref[...], s3, b3)
    gw3 = jnp.zeros((inner, chans), F32)
    for p0 in range(1, rows - 1, step):
        conv = conv3(lambda dh: acts[p0 - 1 + dh : p0 - 1 + dh + step].reshape(step * wide, 3 * inner), w2)
        skip = xs[p0 : p0 + step].reshape(step * wide, chans)
        ct = cs[p0 : p0 + step].reshape(step * wide, chans)
        a2, grad3, back3, grad2 = through(conv, skip, ct, *rest)
        for k in range(step):
            spread(gcat, p0 - 1 + k, grad2[k * wide : (k + 1) * wide] * col_ok)
            back[(p0 - 1 + k) * cols : (p0 + k) * cols, :] = back3[k * wide : k * wide + cols]
        own = [slice(k * wide, k * wide + cols) for k in range(step)]
        gw3 = gw3 + dot(
            jnp.concatenate([a2[at] for at in own], axis=0).T, jnp.concatenate([grad3[at] for at in own], axis=0)
        )
    gw3_ref[...] = gw3
    n = (rows - 2) * cols
    own_gt = gcat[:, 0:cols, inner : 2 * inner].reshape(n, inner).T
    for dh in range(3):
        full_ref[dh] = dot(own_gt, acts[dh : dh + rows - 2, 0:cols, :].reshape(n, 3 * inner))
    gw1t = jnp.zeros((inner, chans), F32)
    for p0 in range(2, rows - 2, step):
        conv = conv3(lambda dh: gcat[p0 - 2 + dh : p0 - 2 + dh + step, 0:cols, :].reshape(step * cols, 3 * inner), w2t)
        g = (conv * d1[p0 * cols : (p0 + step) * cols, :]).astype(BF)
        g1[(p0 - 2) * cols : (p0 - 2 + step) * cols, :] = g
        gw1t = gw1t + dot(g.T, x_ref[p0 : p0 + step].reshape(step * cols, chans))
    gw1t_ref[...] = gw1t


def rim_kernel(
    pos, x_ref, c_ref, strip_ref, row_even, row_odd, w1_ref, vec_ref, w2, w2t, w3_ref, w3t_ref,
    acts, gcat, d1, gw3_ref, full_ref, gw1t_ref,
    share_ref, g1, back, hacts, hgrad,
    *, rows, cols, chans, inner, group_ch,
):
    wide = cols + STRIP
    col_ok = column_mask(pos, wide, cols, inner)
    s1, b1, s2, b2, s3, b3 = vectors(vec_ref, inner)
    row_is_odd = pos[0]
    has_low, has_high = pos[1].astype(F32), pos[2].astype(F32)

    def halo(i, low):
        a, b = row_even[i].astype(F32), row_odd[i].astype(F32)
        take_odd = (row_is_odd == 0) if low else (row_is_odd == 1)
        return jnp.where(take_odd, b, a).astype(BF)

    def wider(ref, r, base):
        return jnp.concatenate([ref[r], strip_ref[base + r]], axis=0)

    far = [halo(0, True), halo(1, True), halo(0, False), halo(1, False)]
    act, _ = reduce_act(jnp.concatenate(far, axis=0), w1_ref[...], s1, b1)
    for k in range(4):
        spread(hacts, k, act[k * wide : (k + 1) * wide] * (col_ok * (has_low if k < 2 else has_high)))
    def act_row(r):
        return hacts[r] if r < 2 else acts[r - 2] if r < rows + 2 else hacts[r - rows]

    mids = (0, 1, rows, rows + 1)
    conv = conv3(lambda dh: jnp.concatenate([act_row(q + dh) for q in mids], axis=0), w2)
    skip = jnp.concatenate([far[1], wider(x_ref, 0, 0), wider(x_ref, rows - 1, 0), far[2]], axis=0)
    ct = jnp.concatenate([halo(2, True), wider(c_ref, 0, rows), wider(c_ref, rows - 1, rows), halo(2, False)], axis=0)
    a2, grad3, back3, grad2 = through(conv, skip, ct, s2, b2, w3_ref[...], w3t_ref[...], s3, b3)
    for k in range(4):
        g = grad2[k * wide : (k + 1) * wide] * col_ok
        spread(hgrad, k, g * has_low if k == 0 else g * has_high if k == 3 else g)
    own = [slice(k * wide, k * wide + cols) for k in (1, 2)]
    for k in range(2):
        back[k * cols : (k + 1) * cols, :] = back3[own[k]]
    gw3 = gw3_ref[...] + dot(
        jnp.concatenate([a2[at] for at in own], axis=0).T, jnp.concatenate([grad3[at] for at in own], axis=0)
    )
    own_gt = jnp.concatenate([hgrad[k, 0:cols, inner : 2 * inner] for k in (1, 2)], axis=0).T
    sub = lax.broadcasted_iota(jnp.int32, (inner, 3 * inner), 0)
    lane = lax.broadcasted_iota(jnp.int32, (inner, 3 * inner), 1)
    same = jnp.where(sub // group_ch == (lane % inner) // group_ch, 1.0, 0.0).astype(F32)
    pick_sub = lax.broadcasted_iota(jnp.int32, (3 * inner, inner), 0)
    pick_lane = lax.broadcasted_iota(jnp.int32, (3 * inner, inner), 1)
    compact = jnp.zeros((inner, inner), F32)
    for dh in range(3):
        near = jnp.concatenate([act_row(q + dh)[0:cols] for q in (1, rows)], axis=0)
        full = ((full_ref[dh] + dot(own_gt, near)) * same).astype(BF)
        place = (dh * 3 + pick_sub // inner) * group_ch + pick_sub % group_ch
        compact = compact + dot(full, jnp.where(pick_lane == place, 1.0, 0.0).astype(BF))
    gw2 = compact.T

    def grad_row(q):
        return (hgrad[q] if q < 2 else gcat[q - 2] if q < rows else hgrad[q - rows + 2])[0:cols]

    outs = (0, 1, rows - 2, rows - 1)
    conv = conv3(lambda dh: jnp.concatenate([grad_row(p + dh) for p in outs], axis=0), w2t)
    slope = jnp.concatenate([d1[0 : 2 * cols, :], d1[(rows - 2) * cols :, :]], axis=0)
    g = (conv * slope).astype(BF)
    g1[...] = g
    gw1 = (gw1t_ref[...] + dot(g.T, jnp.concatenate([x_ref[p] for p in outs], axis=0))).T
    n_dp = share_ref.shape[1]
    one, three = chans // n_dp, inner // n_dp
    for h in range(n_dp):
        share_ref[0, h, 0:one, :] = gw1[h * one : (h + 1) * one]
        for k in range(chans // inner):
            share_ref[1, h, k * three : (k + 1) * three, :] = gw3[
                h * three : (h + 1) * three, k * inner : (k + 1) * inner
            ]
        group = gw2 if h == 0 else pltpu.roll(gw2, inner - h * three, 1)
        share_ref[0, h, one : one + GROUP_ROWS, :] = group[0:GROUP_ROWS]
        share_ref[1, h, one : one + GROUP_ROWS, :] = group[GROUP_ROWS : 2 * GROUP_ROWS]


def out_kernel(g1_in, g1_rim, back_in, back_rim, w1_ref, out_ref, *, rows, cols, chans):
    w1t = w1_ref[...].T
    for p in range(rows):
        if 2 <= p < rows - 2:
            g = g1_in[(p - 2) * cols : (p - 1) * cols, :]
        else:
            k = p if p < 2 else p - rows + 4
            g = g1_rim[k * cols : (k + 1) * cols, :]
        if 1 <= p < rows - 1:
            b = back_in[(p - 1) * cols : p * cols, :]
        else:
            b = back_rim[0:cols, :] if p == 0 else back_rim[cols:, :]
        out_ref[p] = (dot(g, w1t) + b).astype(BF)


def last_kernel(
    pos, a_ref, b_ref, r_out, g_out, e_out, r_ref, g_ref, e_ref, sems, *, scale, one, three, chans, inner, group_ch
):
    other_first = pos[5] == 1
    first = jnp.where(other_first, b_ref[...], a_ref[...]) * scale
    second = jnp.where(other_first, a_ref[...], b_ref[...]) * scale
    r_ref[...] = first[0:one]
    for k in range(chans // inner):
        e_ref[:, k * inner : (k + 1) * inner] = second[k * three : (k + 1) * three]
    for t in range(9):
        at = t * group_ch
        part = first[one + at : one + at + group_ch] if at < GROUP_ROWS else second[
            one + at - GROUP_ROWS : one + at - GROUP_ROWS + group_ch]
        g_ref[t // 3, t % 3] = part[:, 0:three]
    copies = [
        pltpu.make_async_copy(src, dst, sems.at[i])
        for i, (src, dst) in enumerate(((r_ref, r_out), (e_ref, e_out), (g_ref, g_out)))
    ]
    for copy in copies:
        copy.start()
    for copy in copies:
        copy.wait()


def crossed(value, axis, bit):
    n_row = lax.axis_size("row")
    if axis == "row":
        return lax.ppermute(value, "row", [(i, i ^ bit ^ 1) for i in range(n_row)])
    count = lax.axis_size(axis)
    pairs = [(i, j, i ^ bit, j ^ 1) for i in range(count) for j in range(n_row)]
    if axis == "dp":
        return lax.ppermute(value, ("dp", "row"), [(i * n_row + j, k * n_row + m) for i, j, k, m in pairs])
    return lax.ppermute(value, ("row", "col"), [(j * count + i, m * count + k) for i, j, k, m in pairs])


def body(
    features, reduce_weight, scale_one, shift_one, group_weight, scale_two, shift_two, expand_weight, scale_three,
    shift_three, cotangent,
):
    _, rows, cols, chans = features.shape
    inner = reduce_weight.shape[1]
    group_ch = group_weight.shape[2]
    x, c = features[0], cotangent[0]
    n_dp, n_row, n_col = (lax.axis_size(a) for a in ("dp", "row", "col"))
    dp, row, col = (lax.axis_index(a) for a in ("dp", "row", "col"))

    def col_edge(high):
        start = jnp.where(high, cols - EDGE, 0)
        return jnp.concatenate([lax.dynamic_slice_in_dim(v, start, EDGE, axis=1) for v in (x, c)], axis=0)

    col_even, col_odd = swap_edges(col_edge, "col")
    from_high = jnp.where(col % 2 == 0, col_even, col_odd)
    from_low = jnp.where(col % 2 == 0, col_odd, col_even)
    gap = jnp.zeros((2 * rows, STRIP - 2 * EDGE, chans), BF)
    strip = jnp.concatenate([from_high, gap, from_low], axis=1)

    def row_edge(high):
        def cut(v, at, n, base=0):
            return lax.dynamic_slice_in_dim(v, base + jnp.where(high, rows - n, 0), n, axis=0)

        main = jnp.concatenate([cut(x, 0, 2), cut(c, 0, 1)], axis=0)
        side = jnp.concatenate([cut(strip, 0, 2), cut(strip, 0, 1, rows)], axis=0)
        return jnp.concatenate([main, side], axis=1)

    row_even, row_odd = swap_edges(row_edge, "row")
    parity = (dp ^ (dp >> 1) ^ (dp >> 2) ^ (dp >> 3) ^ row ^ (row >> 1) ^ (row >> 2) ^ col ^ (col >> 1) ^ (col >> 2)) & 1
    pos = jnp.stack([row % 2, row > 0, row < n_row - 1, col > 0, col < n_col - 1, parity]).astype(jnp.int32)
    wide = cols + STRIP
    one, three = chans // n_dp, inner // n_dp
    half_rows = one + GROUP_ROWS
    vmem = pl.BlockSpec(memory_space=pltpu.VMEM)
    smem = pl.BlockSpec(memory_space=pltpu.SMEM)
    params = pltpu.CompilerParams(vmem_limit_bytes=8 << 20)
    sizes = dict(rows=rows, cols=cols, chans=chans)
    shape = jax.ShapeDtypeStruct
    w2, w2t, w3t = pl.pallas_call(
        functools.partial(weights_kernel, inner=inner, group_ch=group_ch),
        out_shape=(shape((9 * inner, inner), BF), shape((9 * inner, inner), BF), shape((chans, inner), BF)),
        in_specs=[vmem] * 2,
        out_specs=(vmem,) * 3,
        compiler_params=params,
        name="weights",
    )(group_weight.astype(F32).reshape(9 * group_ch, inner), expand_weight)
    narrow = jnp.stack([scale_one, shift_one, scale_two, shift_two])
    vecs = jnp.concatenate(
        [jnp.pad(narrow, ((0, 0), (0, chans - inner))), scale_three[None], shift_three[None]], axis=0
    )
    shared = (reduce_weight, vecs, w2, w2t, expand_weight, w3t)
    acts, gcat, d1, back_in, g1_in, gw3, full, gw1t = pl.pallas_call(
        functools.partial(inner_kernel, inner=inner, **sizes),
        out_shape=(
            shape((rows, wide, 3 * inner), BF),
            shape((rows - 2, wide, 3 * inner), BF),
            shape((rows * cols, inner), F32),
            shape(((rows - 2) * cols, chans), F32),
            shape(((rows - 4) * cols, inner), BF),
            shape((inner, chans), F32),
            shape((3, inner, 3 * inner), F32),
            shape((inner, chans), F32),
        ),
        in_specs=[smem] + [vmem] * 9,
        out_specs=(vmem,) * 8,
        scratch_shapes=[pltpu.VMEM((rows, wide, chans), BF), pltpu.VMEM((rows, wide, chans), BF)],
        compiler_params=params,
        name="inner",
    )(pos, x, c, strip, *shared)
    shares, g1_rim, back_rim = pl.pallas_call(
        functools.partial(rim_kernel, inner=inner, group_ch=group_ch, **sizes),
        out_shape=(
            shape((2, n_dp, half_rows, inner), F32),
            shape((4 * cols, inner), BF),
            shape((2 * cols, chans), F32),
        ),
        in_specs=[smem] + [vmem] * 17,
        out_specs=(vmem,) * 3,
        scratch_shapes=[pltpu.VMEM((4, wide, 3 * inner), BF), pltpu.VMEM((4, wide, 3 * inner), BF)],
        compiler_params=params,
        name="rim",
    )(pos, x, c, strip, row_even, row_odd, *shared, acts, gcat, d1, gw3, full, gw1t)
    mine = lax.dynamic_index_in_dim(shares, parity, axis=0, keepdims=False)
    theirs = lax.dynamic_index_in_dim(shares, 1 - parity, axis=0, keepdims=False)
    near = [(i, i ^ 1) for i in range(n_row)]
    shares = (mine + lax.ppermute(theirs, "row", near)).astype(BF)
    g1_rim, shares = lax.optimization_barrier((g1_rim, shares))
    input_grad = pl.pallas_call(
        functools.partial(out_kernel, **sizes),
        out_shape=shape((rows, cols, chans), BF),
        in_specs=[vmem] * 5,
        out_specs=vmem,
        compiler_params=params,
        name="out",
    )(g1_in, g1_rim, back_in, back_rim, reduce_weight)
    held = n_dp
    while held > 1:
        half = held // 2
        bit = (dp // half) % 2
        mine = lax.dynamic_slice_in_dim(shares, bit * half, half, axis=0)
        theirs = lax.dynamic_slice_in_dim(shares, (1 - bit) * half, half, axis=0)
        shares = (mine.astype(F32) + crossed(theirs, "dp", half).astype(F32)).astype(BF)
        held = half
    total = shares[0]
    steps = [("row", 1 << k) for k in range(1, n_row.bit_length() - 1)]
    steps += [("col", 1 << k) for k in range(n_col.bit_length() - 1)]
    for axis, bit in steps:
        other = crossed(total, axis, bit)
        if (axis, bit) == steps[0]:
            input_grad, other = lax.optimization_barrier((input_grad, other))
        summed = total.astype(F32) + other.astype(F32)
        total = summed.astype(BF)
    pixels = rows * cols * n_dp * n_row * n_col
    reduce_grad, group_grad, expand_grad = pl.pallas_call(
        functools.partial(
            last_kernel, scale=pixels**-0.5, one=one, three=three, chans=chans, inner=inner, group_ch=group_ch
        ),
        out_shape=(
            jax.ShapeDtypeStruct((one, inner), F32),
            jax.ShapeDtypeStruct((3, 3, group_ch, three), F32),
            jax.ShapeDtypeStruct((three, chans), F32),
        ),
        in_specs=[smem, vmem, vmem],
        out_specs=(pl.BlockSpec(memory_space=pl.ANY),) * 3,
        scratch_shapes=[
            pltpu.VMEM((one, inner), F32),
            pltpu.VMEM((3, 3, group_ch, three), F32),
            pltpu.VMEM((three, chans), F32),
            pltpu.SemaphoreType.DMA((3,)),
        ],
        compiler_params=pltpu.CompilerParams(vmem_limit_bytes=2 << 20),
        name="last",
    )(pos, summed, lax.ppermute(summed, "row", near))
    return input_grad[None], reduce_grad, jnp.transpose(group_grad, (3, 0, 1, 2)), expand_grad


def solution(mesh):
    image = P("dp", "row", "col", None)
    return jax.shard_map(
        body,
        mesh=mesh,
        in_specs=(image,) + (P(),) * 9 + (image,),
        out_specs=(image, P("dp", None), P("dp", None, None, None), P("dp", None)),
        check_vma=False,
    )
```

```python
import functools
import itertools

import jax
import jax.numpy as jnp
from jax import lax
from jax.experimental import pallas as pl
from jax.experimental.pallas import tpu as pltpu
from jax.sharding import PartitionSpec as P

BF = jnp.bfloat16
F32 = jnp.float32
EDGE = 2
STRIP = 16
GROUP_ROWS = 24


def swap_edges(to_even, to_odd, axis):
    count, bands = lax.axis_size(axis), lax.axis_size("dp")
    got_even = lax.ppermute(to_even, axis, [(i, i ^ 1) for i in range(count)])
    names = ("dp", "row", "col")
    sizes = [lax.axis_size(a) for a in names]
    which = names.index(axis)
    perm = []
    for at in itertools.product(*(range(n) for n in sizes)):
        to = list(at)
        if 0 < at[which] < count - 1:
            to[which] = ((at[which] - 1) ^ 1) + 1
        elif bands > 1:
            to[0] ^= 1
        perm.append(tuple(functools.reduce(lambda v, k: v * sizes[k] + p[k], range(3), 0) for p in (at, to)))
    got_odd = lax.ppermute(to_odd, names, perm)
    return got_even, got_odd


def dot(a, b):
    return jnp.dot(a, b, preferred_element_type=F32)


def gate(v):
    return 0.5 + 0.5 * jnp.tanh(0.5 * v)


def column_mask(pos, wide, cols, inner):
    spot = lax.broadcasted_iota(jnp.int32, (wide, inner), 0)
    has_low, has_high = pos[3].astype(F32), pos[4].astype(F32)
    return jnp.where(spot < cols, 1.0, jnp.where(spot < cols + STRIP // 2, has_high, has_low))


def spread(ref, r, v):
    wide, inner = v.shape
    ref[r, :, 0:inner] = pltpu.roll(v, 1, 0).astype(BF)
    ref[r, :, inner : 2 * inner] = v.astype(BF)
    ref[r, :, 2 * inner :] = pltpu.roll(v, wide - 1, 0).astype(BF)


def conv3(windows, w_ref):
    n = w_ref.shape[0] // 3
    out = dot(windows(0), w_ref[0:n, :])
    for dh in (1, 2):
        out = out + dot(windows(dh), w_ref[dh * n : (dh + 1) * n, :])
    return out


def reduce_act(x, w1, s1, b1):
    pre = dot(x, w1) * s1 + b1
    sg = gate(pre)
    return pre * sg, sg


def through(conv, skip, ct, s2, b2, w3, w3t, s3, b3):
    pre2 = conv * s2 + b2
    sg2 = gate(pre2)
    silu2 = pre2 * sg2
    a2 = silu2.astype(BF)
    pre3 = dot(a2, w3) * s3 + b3 + skip.astype(F32)
    sg3 = gate(pre3)
    back3 = ct.astype(F32) * (sg3 + pre3 * sg3 * (1.0 - sg3))
    grad3 = (back3 * s3).astype(BF)
    grad2 = dot(grad3, w3t) * ((sg2 + silu2 * (1.0 - sg2)) * s2)
    return a2, grad3, back3, grad2


def load_kernel(*refs, inner, group_ch):
    sources, targets, (w2, w2t, w3t, gw_ref, sems) = refs[:11], refs[11:21], refs[21:]
    gw_hbm, sources = sources[0], sources[1:]
    copies = [pltpu.make_async_copy(gw_hbm, gw_ref, sems.at[10])]
    copies += [pltpu.make_async_copy(src, dst, sems.at[i]) for i, (src, dst) in enumerate(zip(sources, targets))]
    for copy in copies:
        copy.start()
    copies[0].wait()
    sub = lax.broadcasted_iota(jnp.int32, (inner, inner), 0)
    lane = lax.broadcasted_iota(jnp.int32, (inner, inner), 1)
    diag = jnp.where(sub // group_ch == lane // group_ch, 1.0, 0.0).astype(F32)
    for t in range(9):
        four = gw_ref[t // 3, t % 3].astype(F32)
        eight = jnp.concatenate([four, four], axis=0)
        tiled = jnp.broadcast_to(eight[None], (inner // 8, 8, inner)).reshape(inner, inner)
        dense = tiled * diag
        w2[t * inner : (t + 1) * inner, :] = dense.astype(BF)
        w2t[(8 - t) * inner : (9 - t) * inner, :] = dense.T.astype(BF)
    copies[1].wait()
    w3t[...] = targets[0][...].T
    for copy in copies[2:]:
        copy.wait()


def edges_kernel(pos, x_ref, c_ref, col_even, col_odd, strip, even_ref, odd_ref, *, rows, cols):
    col_is_odd = pos[6] == 1
    chans = x_ref.shape[2]
    gap = jnp.zeros((STRIP - 2 * EDGE, chans), F32)
    for r in range(2 * rows):
        a, b = col_even[r].astype(F32), col_odd[r].astype(F32)
        high, low = jnp.where(col_is_odd, b, a), jnp.where(col_is_odd, a, b)
        strip[r] = jnp.concatenate([high, gap, low], axis=0).astype(BF)
    for ref, sends_high in ((even_ref, pos[0] == 0), (odd_ref, pos[0] == 1)):
        at = jnp.where(sends_high, rows - 2, 0)
        cot_at = jnp.where(sends_high, rows - 1, 0)
        for i in range(2):
            ref[i, 0:cols, :] = x_ref[at + i]
            ref[i, cols:, :] = strip[at + i]
        ref[2, 0:cols, :] = c_ref[cot_at]
        ref[2, cols:, :] = strip[rows + cot_at]


def inner_kernel(
    pos, x_ref, c_ref, strip_ref, w1_ref, s1_ref, b1_ref, s2_ref, b2_ref, s3_ref, b3_ref, w2, w2t, w3_ref, w3t_ref,
    acts, gcat, d1, back, g1, gw3_ref, full_ref, gw1t_ref, xs, cs,
    *, rows, cols, chans, inner,
):
    wide = cols + STRIP
    step = 2
    col_ok = column_mask(pos, wide, cols, inner)
    s1, b1, s2, b2, s3, b3 = (v[...] for v in (s1_ref, b1_ref, s2_ref, b2_ref, s3_ref, b3_ref))
    w1 = w1_ref[...]
    for r in range(rows):
        xs[r, 0:cols, :] = x_ref[r]
        xs[r, cols:wide, :] = strip_ref[r]
        cs[r, 0:cols, :] = c_ref[r]
        cs[r, cols:wide, :] = strip_ref[rows + r]
    for r0 in range(0, rows, step):
        act, sg = reduce_act(xs[r0 : r0 + step].reshape(step * wide, chans), w1, s1, b1)
        slope = (sg + act * (1.0 - sg)) * s1
        for k in range(step):
            r = r0 + k
            spread(acts, r, act[k * wide : (k + 1) * wide] * col_ok)
            d1[r * cols : (r + 1) * cols, :] = slope[k * wide : k * wide + cols]
    rest = (s2, b2, w3_ref[...], w3t_ref[...], s3, b3)
    gw3 = jnp.zeros((inner, chans), F32)
    for p0 in range(1, rows - 1, step):
        conv = conv3(lambda dh: acts[p0 - 1 + dh : p0 - 1 + dh + step].reshape(step * wide, 3 * inner), w2)
        skip = xs[p0 : p0 + step].reshape(step * wide, chans)
        ct = cs[p0 : p0 + step].reshape(step * wide, chans)
        a2, grad3, back3, grad2 = through(conv, skip, ct, *rest)
        for k in range(step):
            spread(gcat, p0 - 1 + k, grad2[k * wide : (k + 1) * wide] * col_ok)
            back[(p0 - 1 + k) * cols : (p0 + k) * cols, :] = back3[k * wide : k * wide + cols]
        own = [slice(k * wide, k * wide + cols) for k in range(step)]
        gw3 = gw3 + dot(
            jnp.concatenate([a2[at] for at in own], axis=0).T, jnp.concatenate([grad3[at] for at in own], axis=0)
        )
    gw3_ref[...] = gw3
    n = (rows - 2) * cols
    own_gt = gcat[:, 0:cols, inner : 2 * inner].reshape(n, inner).T
    for dh in range(3):
        full_ref[dh] = dot(own_gt, acts[dh : dh + rows - 2, 0:cols, :].reshape(n, 3 * inner))
    gw1t = jnp.zeros((inner, chans), F32)
    for p0 in range(2, rows - 2, step):
        conv = conv3(lambda dh: gcat[p0 - 2 + dh : p0 - 2 + dh + step, 0:cols, :].reshape(step * cols, 3 * inner), w2t)
        g = (conv * d1[p0 * cols : (p0 + step) * cols, :]).astype(BF)
        g1[(p0 - 2) * cols : (p0 - 2 + step) * cols, :] = g
        gw1t = gw1t + dot(g.T, x_ref[p0 : p0 + step].reshape(step * cols, chans))
    gw1t_ref[...] = gw1t


def rim_kernel(
    pos, x_ref, c_ref, strip_ref, row_even, row_odd, w1_ref, s1_ref, b1_ref, s2_ref, b2_ref, s3_ref, b3_ref, w2, w2t, w3_ref, w3t_ref,
    acts, gcat, d1, gw3_ref, full_ref, gw1t_ref,
    share_ref, g1, back, hacts, hgrad,
    *, rows, cols, chans, inner, group_ch,
):
    wide = cols + STRIP
    col_ok = column_mask(pos, wide, cols, inner)
    s1, b1, s2, b2, s3, b3 = (v[...] for v in (s1_ref, b1_ref, s2_ref, b2_ref, s3_ref, b3_ref))
    row_is_odd = pos[0]
    has_low, has_high = pos[1].astype(F32), pos[2].astype(F32)

    def halo(i, low):
        a, b = row_even[i].astype(F32), row_odd[i].astype(F32)
        take_odd = (row_is_odd == 0) if low else (row_is_odd == 1)
        return jnp.where(take_odd, b, a).astype(BF)

    def wider(ref, r, base):
        return jnp.concatenate([ref[r], strip_ref[base + r]], axis=0)

    far = [halo(0, True), halo(1, True), halo(0, False), halo(1, False)]
    act, _ = reduce_act(jnp.concatenate(far, axis=0), w1_ref[...], s1, b1)
    for k in range(4):
        spread(hacts, k, act[k * wide : (k + 1) * wide] * (col_ok * (has_low if k < 2 else has_high)))
    def act_row(r):
        return hacts[r] if r < 2 else acts[r - 2] if r < rows + 2 else hacts[r - rows]

    mids = (0, 1, rows, rows + 1)
    conv = conv3(lambda dh: jnp.concatenate([act_row(q + dh) for q in mids], axis=0), w2)
    skip = jnp.concatenate([far[1], wider(x_ref, 0, 0), wider(x_ref, rows - 1, 0), far[2]], axis=0)
    ct = jnp.concatenate([halo(2, True), wider(c_ref, 0, rows), wider(c_ref, rows - 1, rows), halo(2, False)], axis=0)
    a2, grad3, back3, grad2 = through(conv, skip, ct, s2, b2, w3_ref[...], w3t_ref[...], s3, b3)
    for k in range(4):
        g = grad2[k * wide : (k + 1) * wide] * col_ok
        spread(hgrad, k, g * has_low if k == 0 else g * has_high if k == 3 else g)
    own = [slice(k * wide, k * wide + cols) for k in (1, 2)]
    for k in range(2):
        back[k * cols : (k + 1) * cols, :] = back3[own[k]]
    gw3 = gw3_ref[...] + dot(
        jnp.concatenate([a2[at] for at in own], axis=0).T, jnp.concatenate([grad3[at] for at in own], axis=0)
    )
    own_gt = jnp.concatenate([hgrad[k, 0:cols, inner : 2 * inner] for k in (1, 2)], axis=0).T
    sub = lax.broadcasted_iota(jnp.int32, (inner, 3 * inner), 0)
    lane = lax.broadcasted_iota(jnp.int32, (inner, 3 * inner), 1)
    same = jnp.where(sub // group_ch == (lane % inner) // group_ch, 1.0, 0.0).astype(F32)
    pick_sub = lax.broadcasted_iota(jnp.int32, (3 * inner, inner), 0)
    pick_lane = lax.broadcasted_iota(jnp.int32, (3 * inner, inner), 1)
    compact = jnp.zeros((inner, inner), F32)
    for dh in range(3):
        near = jnp.concatenate([act_row(q + dh)[0:cols] for q in (1, rows)], axis=0)
        full = ((full_ref[dh] + dot(own_gt, near)) * same).astype(BF)
        place = (dh * 3 + pick_sub // inner) * group_ch + pick_sub % group_ch
        compact = compact + dot(full, jnp.where(pick_lane == place, 1.0, 0.0).astype(BF))
    gw2 = compact.T

    def grad_row(q):
        return (hgrad[q] if q < 2 else gcat[q - 2] if q < rows else hgrad[q - rows + 2])[0:cols]

    outs = (0, 1, rows - 2, rows - 1)
    conv = conv3(lambda dh: jnp.concatenate([grad_row(p + dh) for p in outs], axis=0), w2t)
    slope = jnp.concatenate([d1[0 : 2 * cols, :], d1[(rows - 2) * cols :, :]], axis=0)
    g = (conv * slope).astype(BF)
    g1[...] = g
    gw1 = (gw1t_ref[...] + dot(g.T, jnp.concatenate([x_ref[p] for p in outs], axis=0))).T
    n_dp = share_ref.shape[1]
    one, three = chans // n_dp, inner // n_dp
    at = (pos[5], 1 - pos[5])
    for h in range(n_dp):
        slot = h ^ pos[7]
        share_ref[at[0], slot, 0:one, :] = gw1[h * one : (h + 1) * one]
        for k in range(chans // inner):
            share_ref[at[1], slot, k * three : (k + 1) * three, :] = gw3[
                h * three : (h + 1) * three, k * inner : (k + 1) * inner
            ]
        group = gw2 if h == 0 else pltpu.roll(gw2, inner - h * three, 1)
        share_ref[at[0], slot, one : one + GROUP_ROWS, :] = group[0:GROUP_ROWS]
        share_ref[at[1], slot, one : one + GROUP_ROWS, :] = group[GROUP_ROWS : 2 * GROUP_ROWS]


def out_kernel(g1_in, g1_rim, back_in, back_rim, w1_ref, out_ref, *, rows, cols, chans):
    w1t = w1_ref[...].T
    for p in range(rows):
        if 2 <= p < rows - 2:
            g = g1_in[(p - 2) * cols : (p - 1) * cols, :]
        else:
            k = p if p < 2 else p - rows + 4
            g = g1_rim[k * cols : (k + 1) * cols, :]
        if 1 <= p < rows - 1:
            b = back_in[(p - 1) * cols : p * cols, :]
        else:
            b = back_rim[0:cols, :] if p == 0 else back_rim[cols:, :]
        out_ref[p] = (dot(g, w1t) + b).astype(BF)


def last_kernel(
    pos, a_ref, b_ref, r_out, g_out, e_out, r_ref, g_ref, e_ref, sems, *, scale, one, three, chans, inner, group_ch
):
    other_first = pos[5] == 1
    first = jnp.where(other_first, b_ref[...], a_ref[...]) * scale
    second = jnp.where(other_first, a_ref[...], b_ref[...]) * scale
    r_ref[...] = first[0:one]
    for k in range(chans // inner):
        e_ref[:, k * inner : (k + 1) * inner] = second[k * three : (k + 1) * three]
    for t in range(9):
        at = t * group_ch
        part = first[one + at : one + at + group_ch] if at < GROUP_ROWS else second[
            one + at - GROUP_ROWS : one + at - GROUP_ROWS + group_ch]
        g_ref[t // 3, t % 3] = part[:, 0:three]
    copies = [
        pltpu.make_async_copy(src, dst, sems.at[i])
        for i, (src, dst) in enumerate(((r_ref, r_out), (e_ref, e_out), (g_ref, g_out)))
    ]
    for copy in copies:
        copy.start()
    for copy in copies:
        copy.wait()


def crossed(value, axis, bit):
    n_row = lax.axis_size("row")
    if axis == "row":
        return lax.ppermute(value, "row", [(i, i ^ bit ^ 1) for i in range(n_row)])
    count = lax.axis_size(axis)
    pairs = [(i, j, i ^ bit, j ^ 1) for i in range(count) for j in range(n_row)]
    if axis == "dp":
        return lax.ppermute(value, ("dp", "row"), [(i * n_row + j, k * n_row + m) for i, j, k, m in pairs])
    return lax.ppermute(value, ("row", "col"), [(j * count + i, m * count + k) for i, j, k, m in pairs])


def body(
    features, reduce_weight, scale_one, shift_one, group_weight, scale_two, shift_two, expand_weight, scale_three,
    shift_three, cotangent,
):
    _, rows, cols, chans = features.shape
    inner = reduce_weight.shape[1]
    group_ch = group_weight.shape[2]
    x, c = features[0], cotangent[0]
    n_dp, n_row, n_col = (lax.axis_size(a) for a in ("dp", "row", "col"))
    dp, row, col = (lax.axis_index(a) for a in ("dp", "row", "col"))

    parity = (dp ^ (dp >> 1) ^ (dp >> 2) ^ (dp >> 3) ^ row ^ (row >> 1) ^ (row >> 2) ^ col ^ (col >> 1) ^ (col >> 2)) & 1
    pos = jnp.stack(
        [row % 2, row > 0, row < n_row - 1, col > 0, col < n_col - 1, parity, col % 2, dp]
    ).astype(jnp.int32)
    wide = cols + STRIP
    one, three = chans // n_dp, inner // n_dp
    half_rows = one + GROUP_ROWS
    vmem = pl.BlockSpec(memory_space=pltpu.VMEM)
    smem = pl.BlockSpec(memory_space=pltpu.SMEM)
    params = pltpu.CompilerParams(vmem_limit_bytes=8 << 20)
    sizes = dict(rows=rows, cols=cols, chans=chans)
    shape = jax.ShapeDtypeStruct

    def col_edge(high):
        start = jnp.where(high, cols - EDGE, 0)
        return jnp.concatenate([lax.dynamic_slice_in_dim(v, start, EDGE, axis=1) for v in (x, c)], axis=0)

    to_even, to_odd = col_edge(col % 2 == 0), col_edge(col % 2 == 1)
    to_even, to_odd, pos = lax.optimization_barrier((to_even, to_odd, pos))
    col_even, col_odd = swap_edges(to_even, to_odd, "col")
    sources = (
        expand_weight, reduce_weight, x, c, scale_one[None], shift_one[None], scale_two[None], shift_two[None],
        scale_three[None], shift_three[None],
    )
    w3, w1, x, c, *vecs, w2, w2t, w3t = pl.pallas_call(
        functools.partial(load_kernel, inner=inner, group_ch=group_ch),
        out_shape=tuple(shape(v.shape, v.dtype) for v in sources)
        + (shape((9 * inner, inner), BF), shape((9 * inner, inner), BF), shape((chans, inner), BF)),
        in_specs=[pl.BlockSpec(memory_space=pltpu.HBM)] * 11,
        out_specs=(vmem,) * 13,
        scratch_shapes=[pltpu.VMEM(group_weight.shape, BF), pltpu.SemaphoreType.DMA((11,))],
        compiler_params=params,
        name="load",
    )(*(pltpu.with_memory_space_constraint(v, pltpu.HBM) for v in (group_weight, *sources)))
    shared = (w1, *vecs, w2, w2t, w3, w3t)
    col_even, col_odd, shared, x, c = lax.optimization_barrier((col_even, col_odd, shared, x, c))
    strip, to_even, to_odd = pl.pallas_call(
        functools.partial(edges_kernel, rows=rows, cols=cols),
        out_shape=(shape((2 * rows, STRIP, chans), BF),) + (shape((3, wide, chans), BF),) * 2,
        in_specs=[smem] + [vmem] * 4,
        out_specs=(vmem,) * 3,
        compiler_params=params,
        name="edges",
    )(pos, x, c, col_even, col_odd)
    row_even, row_odd = swap_edges(to_even, to_odd, "row")
    acts, gcat, d1, back_in, g1_in, gw3, full, gw1t = pl.pallas_call(
        functools.partial(inner_kernel, inner=inner, **sizes),
        out_shape=(
            shape((rows, wide, 3 * inner), BF),
            shape((rows - 2, wide, 3 * inner), BF),
            shape((rows * cols, inner), F32),
            shape(((rows - 2) * cols, chans), F32),
            shape(((rows - 4) * cols, inner), BF),
            shape((inner, chans), F32),
            shape((3, inner, 3 * inner), F32),
            shape((inner, chans), F32),
        ),
        in_specs=[smem] + [vmem] * 14,
        out_specs=(vmem,) * 8,
        scratch_shapes=[pltpu.VMEM((rows, wide, chans), BF), pltpu.VMEM((rows, wide, chans), BF)],
        compiler_params=params,
        name="inner",
    )(pos, x, c, strip, *shared)
    shares, g1_rim, back_rim = pl.pallas_call(
        functools.partial(rim_kernel, inner=inner, group_ch=group_ch, **sizes),
        out_shape=(
            shape((2, n_dp, half_rows, inner), F32),
            shape((4 * cols, inner), BF),
            shape((2 * cols, chans), F32),
        ),
        in_specs=[smem] + [vmem] * 22,
        out_specs=(vmem,) * 3,
        scratch_shapes=[pltpu.VMEM((4, wide, 3 * inner), BF), pltpu.VMEM((4, wide, 3 * inner), BF)],
        compiler_params=params,
        name="rim",
    )(pos, x, c, strip, row_even, row_odd, *shared, acts, gcat, d1, gw3, full, gw1t)
    near = [(i, i ^ 1) for i in range(n_row)]
    shares = (shares[0] + lax.ppermute(shares[1], "row", near)).astype(BF)
    g1_rim, shares = lax.optimization_barrier((g1_rim, shares))
    input_grad = pl.pallas_call(
        functools.partial(out_kernel, **sizes),
        out_shape=shape((rows, cols, chans), BF),
        in_specs=[vmem] * 5,
        out_specs=vmem,
        compiler_params=params,
        name="out",
    )(g1_in, g1_rim, back_in, back_rim, w1)
    held = n_dp
    while held > 1:
        held //= 2
        other = crossed(shares[held:], "dp", held)
        shares = (shares[:held].astype(F32) + other.astype(F32)).astype(BF)
    total = shares[0]
    steps = [("row", 1 << k) for k in range(1, n_row.bit_length() - 1)]
    steps += [("col", 1 << k) for k in range(n_col.bit_length() - 1)]
    for axis, bit in steps:
        other = crossed(total, axis, bit)
        if (axis, bit) == steps[0]:
            input_grad, other = lax.optimization_barrier((input_grad, other))
        summed = total.astype(F32) + other.astype(F32)
        total = summed.astype(BF)
    pixels = rows * cols * n_dp * n_row * n_col
    reduce_grad, group_grad, expand_grad = pl.pallas_call(
        functools.partial(
            last_kernel, scale=pixels**-0.5, one=one, three=three, chans=chans, inner=inner, group_ch=group_ch
        ),
        out_shape=(
            jax.ShapeDtypeStruct((one, inner), F32),
            jax.ShapeDtypeStruct((3, 3, group_ch, three), F32),
            jax.ShapeDtypeStruct((three, chans), F32),
        ),
        in_specs=[smem, vmem, vmem],
        out_specs=(pl.BlockSpec(memory_space=pl.ANY),) * 3,
        scratch_shapes=[
            pltpu.VMEM((one, inner), F32),
            pltpu.VMEM((3, 3, group_ch, three), F32),
            pltpu.VMEM((three, chans), F32),
            pltpu.SemaphoreType.DMA((3,)),
        ],
        compiler_params=pltpu.CompilerParams(vmem_limit_bytes=2 << 20),
        name="last",
    )(pos, summed, lax.ppermute(summed, "row", near))
    return input_grad[None], reduce_grad, jnp.transpose(group_grad, (3, 0, 1, 2)), expand_grad


def solution(mesh):
    image = P("dp", "row", "col", None)
    return jax.shard_map(
        body,
        mesh=mesh,
        in_specs=(image,) + (P(),) * 9 + (image,),
        out_specs=(image, P("dp", None), P("dp", None, None, None), P("dp", None)),
        check_vma=False,
    )
```

```python
import functools
import itertools

import jax
import jax.numpy as jnp
from jax import lax
from jax.experimental import pallas as pl
from jax.experimental.pallas import tpu as pltpu
from jax.sharding import PartitionSpec as P

BF = jnp.bfloat16
F32 = jnp.float32
EDGE = 2
STRIP = 16
GROUP_ROWS = 24


def swap_edges(to_even, to_odd, axis):
    count, bands = lax.axis_size(axis), lax.axis_size("dp")
    got_even = lax.ppermute(to_even, axis, [(i, i ^ 1) for i in range(count)])
    names = ("dp", "row", "col")
    sizes = [lax.axis_size(a) for a in names]
    which = names.index(axis)
    perm = []
    for at in itertools.product(*(range(n) for n in sizes)):
        to = list(at)
        if 0 < at[which] < count - 1:
            to[which] = ((at[which] - 1) ^ 1) + 1
        elif bands > 1:
            to[0] ^= 1
        perm.append(tuple(functools.reduce(lambda v, k: v * sizes[k] + p[k], range(3), 0) for p in (at, to)))
    got_odd = lax.ppermute(to_odd, names, perm)
    return got_even, got_odd


def dot(a, b):
    return jnp.dot(a, b, preferred_element_type=F32)


def gate(v):
    return 0.5 + 0.5 * jnp.tanh(0.5 * v)


def parity_of_place():
    bits = 0
    for axis in ("dp", "row", "col"):
        at = lax.axis_index(axis)
        for k in range((lax.axis_size(axis) - 1).bit_length()):
            bits = bits + (at >> k)
    return bits % 2


def has_neighbours(axis):
    at = lax.axis_index(axis)
    return jnp.where(at > 0, 1.0, 0.0).astype(F32), jnp.where(at < lax.axis_size(axis) - 1, 1.0, 0.0).astype(F32)


def column_mask(wide, cols, inner):
    spot = lax.broadcasted_iota(jnp.int32, (wide, inner), 0)
    has_low, has_high = has_neighbours("col")
    return jnp.where(spot < cols, 1.0, jnp.where(spot < cols + STRIP // 2, has_high, has_low))


def spread(ref, r, v):
    wide, inner = v.shape
    ref[r, :, 0:inner] = pltpu.roll(v, 1, 0).astype(BF)
    ref[r, :, inner : 2 * inner] = v.astype(BF)
    ref[r, :, 2 * inner :] = pltpu.roll(v, wide - 1, 0).astype(BF)


def conv3(windows, w_ref):
    n = w_ref.shape[0] // 3
    out = dot(windows(0), w_ref[0:n, :])
    for dh in (1, 2):
        out = out + dot(windows(dh), w_ref[dh * n : (dh + 1) * n, :])
    return out


def reduce_act(x, w1, s1, b1):
    pre = dot(x, w1) * s1 + b1
    sg = gate(pre)
    return pre * sg, sg


def through(conv, skip, ct, s2, b2, w3, w3t, s3, b3):
    pre2 = conv * s2 + b2
    sg2 = gate(pre2)
    silu2 = pre2 * sg2
    a2 = silu2.astype(BF)
    pre3 = dot(a2, w3) * s3 + b3 + skip.astype(F32)
    sg3 = gate(pre3)
    back3 = ct.astype(F32) * (sg3 + pre3 * sg3 * (1.0 - sg3))
    grad3 = (back3 * s3).astype(BF)
    grad2 = dot(grad3, w3t) * ((sg2 + silu2 * (1.0 - sg2)) * s2)
    return a2, grad3, back3, grad2


def load_kernel(*refs, inner, group_ch):
    sources, targets, (w2, w2t, w3t, gw_ref, sems) = refs[:11], refs[11:21], refs[21:]
    gw_hbm, sources = sources[0], sources[1:]
    copies = [pltpu.make_async_copy(gw_hbm, gw_ref, sems.at[10])]
    copies += [pltpu.make_async_copy(src, dst, sems.at[i]) for i, (src, dst) in enumerate(zip(sources, targets))]
    for copy in copies:
        copy.start()
    copies[0].wait()
    sub = lax.broadcasted_iota(jnp.int32, (inner, inner), 0)
    lane = lax.broadcasted_iota(jnp.int32, (inner, inner), 1)
    diag = jnp.where(sub // group_ch == lane // group_ch, 1.0, 0.0).astype(F32)
    for t in range(9):
        four = gw_ref[t // 3, t % 3].astype(F32)
        eight = jnp.concatenate([four, four], axis=0)
        tiled = jnp.broadcast_to(eight[None], (inner // 8, 8, inner)).reshape(inner, inner)
        dense = tiled * diag
        w2[t * inner : (t + 1) * inner, :] = dense.astype(BF)
        w2t[(8 - t) * inner : (9 - t) * inner, :] = dense.T.astype(BF)
    copies[1].wait()
    w3t[...] = targets[0][...].T
    for copy in copies[2:]:
        copy.wait()


def edges_kernel(x_ref, c_ref, col_even, col_odd, strip, even_ref, odd_ref, *, rows, cols):
    col_is_odd = lax.axis_index("col") % 2 == 1
    row_is_odd = lax.axis_index("row") % 2
    chans = x_ref.shape[2]
    gap = jnp.zeros((STRIP - 2 * EDGE, chans), F32)
    for r in range(2 * rows):
        a, b = col_even[r].astype(F32), col_odd[r].astype(F32)
        high, low = jnp.where(col_is_odd, b, a), jnp.where(col_is_odd, a, b)
        strip[r] = jnp.concatenate([high, gap, low], axis=0).astype(BF)
    for ref, sends_high in ((even_ref, row_is_odd == 0), (odd_ref, row_is_odd == 1)):
        at = jnp.where(sends_high, rows - 2, 0)
        cot_at = jnp.where(sends_high, rows - 1, 0)
        for i in range(2):
            ref[i, 0:cols, :] = x_ref[at + i]
            ref[i, cols:, :] = strip[at + i]
        ref[2, 0:cols, :] = c_ref[cot_at]
        ref[2, cols:, :] = strip[rows + cot_at]


def inner_kernel(
    x_ref, c_ref, strip_ref, w1_ref, s1_ref, b1_ref, s2_ref, b2_ref, s3_ref, b3_ref, w2, w2t, w3_ref, w3t_ref,
    acts, gcat, d1, back, g1, gw3_ref, full_ref, gw1t_ref, xs, cs,
    *, rows, cols, chans, inner,
):
    wide = cols + STRIP
    step = 2
    col_ok = column_mask(wide, cols, inner)
    s1, b1, s2, b2, s3, b3 = (v[...] for v in (s1_ref, b1_ref, s2_ref, b2_ref, s3_ref, b3_ref))
    w1 = w1_ref[...]
    for r in range(rows):
        xs[r, 0:cols, :] = x_ref[r]
        xs[r, cols:wide, :] = strip_ref[r]
        cs[r, 0:cols, :] = c_ref[r]
        cs[r, cols:wide, :] = strip_ref[rows + r]
    for r0 in range(0, rows, step):
        act, sg = reduce_act(xs[r0 : r0 + step].reshape(step * wide, chans), w1, s1, b1)
        slope = (sg + act * (1.0 - sg)) * s1
        for k in range(step):
            r = r0 + k
            spread(acts, r, act[k * wide : (k + 1) * wide] * col_ok)
            d1[r * cols : (r + 1) * cols, :] = slope[k * wide : k * wide + cols]
    rest = (s2, b2, w3_ref[...], w3t_ref[...], s3, b3)
    gw3 = jnp.zeros((inner, chans), F32)
    for p0 in range(1, rows - 1, step):
        conv = conv3(lambda dh: acts[p0 - 1 + dh : p0 - 1 + dh + step].reshape(step * wide, 3 * inner), w2)
        skip = xs[p0 : p0 + step].reshape(step * wide, chans)
        ct = cs[p0 : p0 + step].reshape(step * wide, chans)
        a2, grad3, back3, grad2 = through(conv, skip, ct, *rest)
        for k in range(step):
            spread(gcat, p0 - 1 + k, grad2[k * wide : (k + 1) * wide] * col_ok)
            back[(p0 - 1 + k) * cols : (p0 + k) * cols, :] = back3[k * wide : k * wide + cols]
        own = [slice(k * wide, k * wide + cols) for k in range(step)]
        gw3 = gw3 + dot(
            jnp.concatenate([a2[at] for at in own], axis=0).T, jnp.concatenate([grad3[at] for at in own], axis=0)
        )
    gw3_ref[...] = gw3
    n = (rows - 2) * cols
    own_gt = gcat[:, 0:cols, inner : 2 * inner].reshape(n, inner).T
    for dh in range(3):
        full_ref[dh] = dot(own_gt, acts[dh : dh + rows - 2, 0:cols, :].reshape(n, 3 * inner))
    gw1t = jnp.zeros((inner, chans), F32)
    for p0 in range(2, rows - 2, step):
        conv = conv3(lambda dh: gcat[p0 - 2 + dh : p0 - 2 + dh + step, 0:cols, :].reshape(step * cols, 3 * inner), w2t)
        g = (conv * d1[p0 * cols : (p0 + step) * cols, :]).astype(BF)
        g1[(p0 - 2) * cols : (p0 - 2 + step) * cols, :] = g
        gw1t = gw1t + dot(g.T, x_ref[p0 : p0 + step].reshape(step * cols, chans))
    gw1t_ref[...] = gw1t


def rim_kernel(
    x_ref, c_ref, strip_ref, row_even, row_odd, w1_ref, s1_ref, b1_ref, s2_ref, b2_ref, s3_ref, b3_ref, w2, w2t, w3_ref, w3t_ref,
    acts, gcat, d1, gw3_ref, full_ref, gw1t_ref,
    share_ref, g1, back, hacts, hgrad,
    *, rows, cols, chans, inner, group_ch,
):
    wide = cols + STRIP
    col_ok = column_mask(wide, cols, inner)
    s1, b1, s2, b2, s3, b3 = (v[...] for v in (s1_ref, b1_ref, s2_ref, b2_ref, s3_ref, b3_ref))
    row_is_odd = lax.axis_index("row") % 2
    has_low, has_high = has_neighbours("row")

    def halo(i, low):
        a, b = row_even[i].astype(F32), row_odd[i].astype(F32)
        take_odd = (row_is_odd == 0) if low else (row_is_odd == 1)
        return jnp.where(take_odd, b, a).astype(BF)

    def wider(ref, r, base):
        return jnp.concatenate([ref[r], strip_ref[base + r]], axis=0)

    far = [halo(0, True), halo(1, True), halo(0, False), halo(1, False)]
    act, _ = reduce_act(jnp.concatenate(far, axis=0), w1_ref[...], s1, b1)
    for k in range(4):
        spread(hacts, k, act[k * wide : (k + 1) * wide] * (col_ok * (has_low if k < 2 else has_high)))
    def act_row(r):
        return hacts[r] if r < 2 else acts[r - 2] if r < rows + 2 else hacts[r - rows]

    mids = (0, 1, rows, rows + 1)
    conv = conv3(lambda dh: jnp.concatenate([act_row(q + dh) for q in mids], axis=0), w2)
    skip = jnp.concatenate([far[1], wider(x_ref, 0, 0), wider(x_ref, rows - 1, 0), far[2]], axis=0)
    ct = jnp.concatenate([halo(2, True), wider(c_ref, 0, rows), wider(c_ref, rows - 1, rows), halo(2, False)], axis=0)
    a2, grad3, back3, grad2 = through(conv, skip, ct, s2, b2, w3_ref[...], w3t_ref[...], s3, b3)
    for k in range(4):
        g = grad2[k * wide : (k + 1) * wide] * col_ok
        spread(hgrad, k, g * has_low if k == 0 else g * has_high if k == 3 else g)
    own = [slice(k * wide, k * wide + cols) for k in (1, 2)]
    for k in range(2):
        back[k * cols : (k + 1) * cols, :] = back3[own[k]]
    gw3 = gw3_ref[...] + dot(
        jnp.concatenate([a2[at] for at in own], axis=0).T, jnp.concatenate([grad3[at] for at in own], axis=0)
    )
    own_gt = jnp.concatenate([hgrad[k, 0:cols, inner : 2 * inner] for k in (1, 2)], axis=0).T
    sub = lax.broadcasted_iota(jnp.int32, (inner, 3 * inner), 0)
    lane = lax.broadcasted_iota(jnp.int32, (inner, 3 * inner), 1)
    same = jnp.where(sub // group_ch == (lane % inner) // group_ch, 1.0, 0.0).astype(F32)
    pick_sub = lax.broadcasted_iota(jnp.int32, (3 * inner, inner), 0)
    pick_lane = lax.broadcasted_iota(jnp.int32, (3 * inner, inner), 1)
    compact = jnp.zeros((inner, inner), F32)
    for dh in range(3):
        near = jnp.concatenate([act_row(q + dh)[0:cols] for q in (1, rows)], axis=0)
        full = ((full_ref[dh] + dot(own_gt, near)) * same).astype(BF)
        place = (dh * 3 + pick_sub // inner) * group_ch + pick_sub % group_ch
        compact = compact + dot(full, jnp.where(pick_lane == place, 1.0, 0.0).astype(BF))
    gw2 = compact.T

    def grad_row(q):
        return (hgrad[q] if q < 2 else gcat[q - 2] if q < rows else hgrad[q - rows + 2])[0:cols]

    outs = (0, 1, rows - 2, rows - 1)
    conv = conv3(lambda dh: jnp.concatenate([grad_row(p + dh) for p in outs], axis=0), w2t)
    slope = jnp.concatenate([d1[0 : 2 * cols, :], d1[(rows - 2) * cols :, :]], axis=0)
    g = (conv * slope).astype(BF)
    g1[...] = g
    gw1 = (gw1t_ref[...] + dot(g.T, jnp.concatenate([x_ref[p] for p in outs], axis=0))).T
    n_dp = share_ref.shape[1]
    one, three = chans // n_dp, inner // n_dp
    parity = parity_of_place()
    at = (parity, 1 - parity)
    for h in range(n_dp):
        slot = h ^ lax.axis_index("dp")
        share_ref[at[0], slot, 0:one, :] = gw1[h * one : (h + 1) * one]
        for k in range(chans // inner):
            share_ref[at[1], slot, k * three : (k + 1) * three, :] = gw3[
                h * three : (h + 1) * three, k * inner : (k + 1) * inner
            ]
        group = gw2 if h == 0 else pltpu.roll(gw2, inner - h * three, 1)
        share_ref[at[0], slot, one : one + GROUP_ROWS, :] = group[0:GROUP_ROWS]
        share_ref[at[1], slot, one : one + GROUP_ROWS, :] = group[GROUP_ROWS : 2 * GROUP_ROWS]


def out_kernel(g1_in, g1_rim, back_in, back_rim, w1_ref, out_ref, *, rows, cols, chans):
    w1t = w1_ref[...].T
    for p in range(rows):
        if 2 <= p < rows - 2:
            g = g1_in[(p - 2) * cols : (p - 1) * cols, :]
        else:
            k = p if p < 2 else p - rows + 4
            g = g1_rim[k * cols : (k + 1) * cols, :]
        if 1 <= p < rows - 1:
            b = back_in[(p - 1) * cols : p * cols, :]
        else:
            b = back_rim[0:cols, :] if p == 0 else back_rim[cols:, :]
        out_ref[p] = (dot(g, w1t) + b).astype(BF)


def last_kernel(
    a_ref, b_ref, r_out, g_out, e_out, r_ref, g_ref, e_ref, sems, *, scale, one, three, chans, inner, group_ch
):
    other_first = parity_of_place() == 1
    first = jnp.where(other_first, b_ref[...], a_ref[...]) * scale
    second = jnp.where(other_first, a_ref[...], b_ref[...]) * scale
    r_ref[...] = first[0:one]
    for k in range(chans // inner):
        e_ref[:, k * inner : (k + 1) * inner] = second[k * three : (k + 1) * three]
    for t in range(9):
        at = t * group_ch
        part = first[one + at : one + at + group_ch] if at < GROUP_ROWS else second[
            one + at - GROUP_ROWS : one + at - GROUP_ROWS + group_ch]
        g_ref[t // 3, t % 3] = part[:, 0:three]
    copies = [
        pltpu.make_async_copy(src, dst, sems.at[i])
        for i, (src, dst) in enumerate(((r_ref, r_out), (e_ref, e_out), (g_ref, g_out)))
    ]
    for copy in copies:
        copy.start()
    for copy in copies:
        copy.wait()


def crossed(value, axis, bit):
    n_row = lax.axis_size("row")
    if axis == "row":
        return lax.ppermute(value, "row", [(i, i ^ bit ^ 1) for i in range(n_row)])
    count = lax.axis_size(axis)
    pairs = [(i, j, i ^ bit, j ^ 1) for i in range(count) for j in range(n_row)]
    if axis == "dp":
        return lax.ppermute(value, ("dp", "row"), [(i * n_row + j, k * n_row + m) for i, j, k, m in pairs])
    return lax.ppermute(value, ("row", "col"), [(j * count + i, m * count + k) for i, j, k, m in pairs])


def body(
    features, reduce_weight, scale_one, shift_one, group_weight, scale_two, shift_two, expand_weight, scale_three,
    shift_three, cotangent,
):
    _, rows, cols, chans = features.shape
    inner = reduce_weight.shape[1]
    group_ch = group_weight.shape[2]
    x, c = features[0], cotangent[0]
    n_dp, n_row, n_col = (lax.axis_size(a) for a in ("dp", "row", "col"))
    col = lax.axis_index("col")

    wide = cols + STRIP
    one, three = chans // n_dp, inner // n_dp
    half_rows = one + GROUP_ROWS
    vmem = pl.BlockSpec(memory_space=pltpu.VMEM)
    params = pltpu.CompilerParams(vmem_limit_bytes=8 << 20)
    sizes = dict(rows=rows, cols=cols, chans=chans)
    shape = jax.ShapeDtypeStruct

    def col_edge(high):
        start = jnp.where(high, cols - EDGE, 0)
        return jnp.concatenate([lax.dynamic_slice_in_dim(v, start, EDGE, axis=1) for v in (x, c)], axis=0)

    to_even, to_odd = col_edge(col % 2 == 0), col_edge(col % 2 == 1)
    col_even, col_odd = swap_edges(to_even, to_odd, "col")
    sources = (
        expand_weight, reduce_weight, x, c, scale_one[None], shift_one[None], scale_two[None], shift_two[None],
        scale_three[None], shift_three[None],
    )
    w3, w1, x, c, *vecs, w2, w2t, w3t = pl.pallas_call(
        functools.partial(load_kernel, inner=inner, group_ch=group_ch),
        out_shape=tuple(shape(v.shape, v.dtype) for v in sources)
        + (shape((9 * inner, inner), BF), shape((9 * inner, inner), BF), shape((chans, inner), BF)),
        in_specs=[pl.BlockSpec(memory_space=pltpu.HBM)] * 11,
        out_specs=(vmem,) * 13,
        scratch_shapes=[pltpu.VMEM(group_weight.shape, BF), pltpu.SemaphoreType.DMA((11,))],
        compiler_params=params,
        name="load",
    )(*(pltpu.with_memory_space_constraint(v, pltpu.HBM) for v in (group_weight, *sources)))
    shared = (w1, *vecs, w2, w2t, w3, w3t)
    col_even, col_odd, shared, x, c = lax.optimization_barrier((col_even, col_odd, shared, x, c))
    strip, to_even, to_odd = pl.pallas_call(
        functools.partial(edges_kernel, rows=rows, cols=cols),
        out_shape=(shape((2 * rows, STRIP, chans), BF),) + (shape((3, wide, chans), BF),) * 2,
        in_specs=[vmem] * 4,
        out_specs=(vmem,) * 3,
        compiler_params=params,
        name="edges",
    )(x, c, col_even, col_odd)
    row_even, row_odd = swap_edges(to_even, to_odd, "row")
    acts, gcat, d1, back_in, g1_in, gw3, full, gw1t = pl.pallas_call(
        functools.partial(inner_kernel, inner=inner, **sizes),
        out_shape=(
            shape((rows, wide, 3 * inner), BF),
            shape((rows - 2, wide, 3 * inner), BF),
            shape((rows * cols, inner), F32),
            shape(((rows - 2) * cols, chans), F32),
            shape(((rows - 4) * cols, inner), BF),
            shape((inner, chans), F32),
            shape((3, inner, 3 * inner), F32),
            shape((inner, chans), F32),
        ),
        in_specs=[vmem] * 14,
        out_specs=(vmem,) * 8,
        scratch_shapes=[pltpu.VMEM((rows, wide, chans), BF), pltpu.VMEM((rows, wide, chans), BF)],
        compiler_params=params,
        name="inner",
    )(x, c, strip, *shared)
    shares, g1_rim, back_rim = pl.pallas_call(
        functools.partial(rim_kernel, inner=inner, group_ch=group_ch, **sizes),
        out_shape=(
            shape((2, n_dp, half_rows, inner), F32),
            shape((4 * cols, inner), BF),
            shape((2 * cols, chans), F32),
        ),
        in_specs=[vmem] * 22,
        out_specs=(vmem,) * 3,
        scratch_shapes=[pltpu.VMEM((4, wide, 3 * inner), BF), pltpu.VMEM((4, wide, 3 * inner), BF)],
        compiler_params=params,
        name="rim",
    )(x, c, strip, row_even, row_odd, *shared, acts, gcat, d1, gw3, full, gw1t)
    near = [(i, i ^ 1) for i in range(n_row)]
    shares = (shares[0] + lax.ppermute(shares[1], "row", near)).astype(BF)
    g1_rim, shares = lax.optimization_barrier((g1_rim, shares))
    input_grad = pl.pallas_call(
        functools.partial(out_kernel, **sizes),
        out_shape=shape((rows, cols, chans), BF),
        in_specs=[vmem] * 5,
        out_specs=vmem,
        compiler_params=params,
        name="out",
    )(g1_in, g1_rim, back_in, back_rim, w1)
    held = n_dp
    while held > 1:
        held //= 2
        other = crossed(shares[held:], "dp", held)
        shares = (shares[:held].astype(F32) + other.astype(F32)).astype(BF)
    total = shares[0]
    steps = [("row", 1 << k) for k in range(1, n_row.bit_length() - 1)]
    steps += [("col", 1 << k) for k in range(n_col.bit_length() - 1)]
    for axis, bit in steps:
        other = crossed(total, axis, bit)
        if (axis, bit) == steps[0]:
            input_grad, other = lax.optimization_barrier((input_grad, other))
        summed = total.astype(F32) + other.astype(F32)
        total = summed.astype(BF)
    pixels = rows * cols * n_dp * n_row * n_col
    reduce_grad, group_grad, expand_grad = pl.pallas_call(
        functools.partial(
            last_kernel, scale=pixels**-0.5, one=one, three=three, chans=chans, inner=inner, group_ch=group_ch
        ),
        out_shape=(
            jax.ShapeDtypeStruct((one, inner), F32),
            jax.ShapeDtypeStruct((3, 3, group_ch, three), F32),
            jax.ShapeDtypeStruct((three, chans), F32),
        ),
        in_specs=[vmem, vmem],
        out_specs=(pl.BlockSpec(memory_space=pl.ANY),) * 3,
        scratch_shapes=[
            pltpu.VMEM((one, inner), F32),
            pltpu.VMEM((3, 3, group_ch, three), F32),
            pltpu.VMEM((three, chans), F32),
            pltpu.SemaphoreType.DMA((3,)),
        ],
        compiler_params=pltpu.CompilerParams(vmem_limit_bytes=2 << 20),
        name="last",
    )(summed, lax.ppermute(summed, "row", near))
    return input_grad[None], reduce_grad, jnp.transpose(group_grad, (3, 0, 1, 2)), expand_grad


def solution(mesh):
    image = P("dp", "row", "col", None)
    return jax.shard_map(
        body,
        mesh=mesh,
        in_specs=(image,) + (P(),) * 9 + (image,),
        out_specs=(image, P("dp", None), P("dp", None, None, None), P("dp", None)),
        check_vma=False,
    )
```

```python
import functools
import itertools

import jax
import jax.numpy as jnp
from jax import lax
from jax.experimental import pallas as pl
from jax.experimental.pallas import tpu as pltpu
from jax.sharding import PartitionSpec as P

BF = jnp.bfloat16
F32 = jnp.float32
EDGE = 2
STRIP = 16
GROUP_ROWS = 24


def swap_edges(to_even, to_odd, axis):
    count, bands = lax.axis_size(axis), lax.axis_size("dp")
    got_even = lax.ppermute(to_even, axis, [(i, i ^ 1) for i in range(count)])
    names = ("dp", "row", "col")
    sizes = [lax.axis_size(a) for a in names]
    which = names.index(axis)
    perm = []
    for at in itertools.product(*(range(n) for n in sizes)):
        to = list(at)
        if 0 < at[which] < count - 1:
            to[which] = ((at[which] - 1) ^ 1) + 1
        elif axis == "col":
            to[1] ^= 1
        elif bands > 1:
            to[0] ^= 1
        perm.append(tuple(functools.reduce(lambda v, k: v * sizes[k] + p[k], range(3), 0) for p in (at, to)))
    got_odd = lax.ppermute(to_odd, names, perm)
    return got_even, got_odd


def dot(a, b):
    return jnp.dot(a, b, preferred_element_type=F32)


def gate(v):
    return 0.5 + 0.5 * jnp.tanh(0.5 * v)


def parity_of_place():
    bits = 0
    for axis in ("dp", "row", "col"):
        at = lax.axis_index(axis)
        for k in range((lax.axis_size(axis) - 1).bit_length()):
            bits = bits + (at >> k)
    return bits % 2


def has_neighbours(axis):
    at = lax.axis_index(axis)
    return jnp.where(at > 0, 1.0, 0.0).astype(F32), jnp.where(at < lax.axis_size(axis) - 1, 1.0, 0.0).astype(F32)


def column_mask(wide, cols, inner):
    spot = lax.broadcasted_iota(jnp.int32, (wide, inner), 0)
    has_low, has_high = has_neighbours("col")
    return jnp.where(spot < cols, 1.0, jnp.where(spot < cols + STRIP // 2, has_high, has_low))


def spread(ref, r, v):
    wide, inner = v.shape
    ref[r, :, 0:inner] = pltpu.roll(v, 1, 0).astype(BF)
    ref[r, :, inner : 2 * inner] = v.astype(BF)
    ref[r, :, 2 * inner :] = pltpu.roll(v, wide - 1, 0).astype(BF)


def conv_pairs(row, starts, w_ref):
    left = [jnp.concatenate([row(i + j) for j in range(4)], axis=1) for i in starts]
    out = dot(jnp.concatenate(left, axis=0), w_ref[...])
    n, inner = left[0].shape[0], w_ref.shape[1] // 2
    return [out[i * n : (i + 1) * n, k * inner : (k + 1) * inner] for i in range(len(starts)) for k in range(2)]


def reduce_act(x, w1, s1, b1):
    pre = dot(x, w1) * s1 + b1
    sg = gate(pre)
    return pre * sg, sg


def through(conv, skip, ct, s2, b2, w3, w3t, s3, b3):
    pre2 = conv * s2 + b2
    sg2 = gate(pre2)
    silu2 = pre2 * sg2
    a2 = silu2.astype(BF)
    pre3 = dot(a2, w3) * s3 + b3 + skip.astype(F32)
    sg3 = gate(pre3)
    back3 = ct.astype(F32) * (sg3 + pre3 * sg3 * (1.0 - sg3))
    grad3 = (back3 * s3).astype(BF)
    grad2 = dot(grad3, w3t) * ((sg2 + silu2 * (1.0 - sg2)) * s2)
    return a2, grad3, back3, grad2


def cut_kernel(x_hbm, c_hbm, odd_ref, even_ref, low_ref, high_ref, sems, *, rows, cols):
    copies = []
    for i, src in enumerate((x_hbm, c_hbm)):
        at = slice(i * rows, (i + 1) * rows)
        copies.append(pltpu.make_async_copy(src.at[:, 0:8, :], low_ref.at[at], sems.at[2 * i]))
        copies.append(pltpu.make_async_copy(src.at[:, cols - 8 : cols, :], high_ref.at[at], sems.at[2 * i + 1]))
    for copy in copies:
        copy.start()
    is_odd = lax.axis_index("col") % 2 == 1
    for copy in copies:
        copy.wait()
    for r in range(2 * rows):
        low = low_ref[r].astype(F32)[0:EDGE]
        high = high_ref[r].astype(F32)[8 - EDGE : 8]
        even_ref[r] = jnp.where(is_odd, low, high).astype(BF)
        odd_ref[r] = jnp.where(is_odd, high, low).astype(BF)


def load_kernel(*refs, inner, group_ch):
    sources, targets, (w2, w2t, w3t, same, pick, gw_ref, sems) = refs[:11], refs[11:21], refs[21:]
    gw_hbm, sources = sources[0], sources[1:]
    copies = [pltpu.make_async_copy(gw_hbm, gw_ref, sems.at[10])]
    copies += [pltpu.make_async_copy(src, dst, sems.at[i]) for i, (src, dst) in enumerate(zip(sources, targets))]
    for copy in copies:
        copy.start()
    copies[0].wait()
    sub = lax.broadcasted_iota(jnp.int32, (inner, inner), 0)
    lane = lax.broadcasted_iota(jnp.int32, (inner, inner), 1)
    diag = jnp.where(sub // group_ch == lane // group_ch, 1.0, 0.0).astype(F32)
    for t in range(9):
        four = gw_ref[t // 3, t % 3].astype(F32)
        eight = jnp.concatenate([four, four], axis=0)
        tiled = jnp.broadcast_to(eight[None], (inner // 8, 8, inner)).reshape(inner, inner)
        dense = tiled * diag
        for ref, tap, block in ((w2, t, dense.astype(BF)), (w2t, 8 - t, dense.T.astype(BF))):
            ref[tap * inner : (tap + 1) * inner, 0:inner] = block
            ref[(tap + 3) * inner : (tap + 4) * inner, inner:] = block
    for ref in (w2, w2t):
        ref[9 * inner :, 0:inner] = jnp.zeros((3 * inner, inner), BF)
        ref[0 : 3 * inner, inner:] = jnp.zeros((3 * inner, inner), BF)
    for k in range(3):
        same[:, k * inner : (k + 1) * inner] = diag
    for t in range(9):
        place = t * group_ch + sub % group_ch
        pick[t * inner : (t + 1) * inner, :] = jnp.where(lane == place, 1.0, 0.0).astype(BF)
    copies[1].wait()
    w3t[...] = targets[0][...].T
    for copy in copies[2:]:
        copy.wait()


def edges_kernel(x_ref, c_ref, col_odd, col_even, strip, even_ref, odd_ref, *, rows, cols):
    col_is_odd = lax.axis_index("col") % 2 == 1
    row_is_odd = lax.axis_index("row") % 2
    chans = x_ref.shape[2]
    gap = jnp.zeros((STRIP - 2 * EDGE, chans), F32)
    for r in range(2 * rows):
        a, b = col_even[r].astype(F32), col_odd[r].astype(F32)
        high, low = jnp.where(col_is_odd, b, a), jnp.where(col_is_odd, a, b)
        strip[r] = jnp.concatenate([high, gap, low], axis=0).astype(BF)
    for ref, sends_high in ((even_ref, row_is_odd == 0), (odd_ref, row_is_odd == 1)):
        at = jnp.where(sends_high, rows - 2, 0)
        cot_at = jnp.where(sends_high, rows - 1, 0)
        for i in range(2):
            ref[i, 0:cols, :] = x_ref[at + i]
            ref[i, cols:, :] = strip[at + i]
        ref[2, 0:cols, :] = c_ref[cot_at]
        ref[2, cols:, :] = strip[rows + cot_at]


def inner_kernel(
    x_ref, c_ref, strip_ref, w1_ref, s1_ref, b1_ref, s2_ref, b2_ref, s3_ref, b3_ref, w2, w2t, w3_ref, w3t_ref,
    acts, gcat, d1, back, g1, gw3_ref, full_ref, gw1_ref, xt, xs, cs,
    *, rows, cols, chans, inner,
):
    wide = cols + STRIP
    step = 2
    col_ok = column_mask(wide, cols, inner)
    s1, b1, s2, b2, s3, b3 = (v[...] for v in (s1_ref, b1_ref, s2_ref, b2_ref, s3_ref, b3_ref))
    w1 = w1_ref[...]
    for r in range(rows):
        xs[r, 0:cols, :] = x_ref[r]
        xs[r, cols:wide, :] = strip_ref[r]
        cs[r, 0:cols, :] = c_ref[r]
        cs[r, cols:wide, :] = strip_ref[rows + r]
    for r0 in range(0, rows, step):
        act, sg = reduce_act(xs[r0 : r0 + step].reshape(step * wide, chans), w1, s1, b1)
        slope = (sg + act * (1.0 - sg)) * s1
        for k in range(step):
            r = r0 + k
            spread(acts, r, act[k * wide : (k + 1) * wide] * col_ok)
            d1[r * cols : (r + 1) * cols, :] = slope[k * wide : k * wide + cols]
    rest = (s2, b2, w3_ref[...], w3t_ref[...], s3, b3)
    gw3 = jnp.zeros((inner, chans), F32)
    convs = conv_pairs(lambda r: acts[r], range(0, rows - 2, step), w2)
    for p0 in range(1, rows - 1, step):
        conv = jnp.concatenate(convs[p0 - 1 : p0 - 1 + step], axis=0)
        skip = xs[p0 : p0 + step].reshape(step * wide, chans)
        ct = cs[p0 : p0 + step].reshape(step * wide, chans)
        a2, grad3, back3, grad2 = through(conv, skip, ct, *rest)
        for k in range(step):
            spread(gcat, p0 - 1 + k, grad2[k * wide : (k + 1) * wide] * col_ok)
            back[(p0 - 1 + k) * cols : (p0 + k) * cols, :] = back3[k * wide : k * wide + cols]
        own = [slice(k * wide, k * wide + cols) for k in range(step)]
        gw3 = gw3 + dot(
            jnp.concatenate([a2[at] for at in own], axis=0).T, jnp.concatenate([grad3[at] for at in own], axis=0)
        )
    gw3_ref[...] = gw3
    n = (rows - 2) * cols
    own_gt = gcat[:, 0:cols, inner : 2 * inner].reshape(n, inner).T
    for dh in range(3):
        full_ref[dh] = dot(own_gt, acts[dh : dh + rows - 2, 0:cols, :].reshape(n, 3 * inner))
    gw1t = jnp.zeros((inner, chans), F32)
    convs = conv_pairs(lambda r: gcat[r, 0:cols, :], range(0, rows - 4, step), w2t)
    for p0 in range(2, rows - 2, step):
        conv = jnp.concatenate(convs[p0 - 2 : p0 - 2 + step], axis=0)
        g = (conv * d1[p0 * cols : (p0 + step) * cols, :]).astype(BF)
        g1[(p0 - 2) * cols : (p0 - 2 + step) * cols, :] = g
        gw1t = gw1t + dot(g.T, x_ref[p0 : p0 + step].reshape(step * cols, chans))
    gw1_ref[...] = gw1t.T
    for k, p in enumerate((0, 1, rows - 2, rows - 1)):
        xt[:, k * cols : (k + 1) * cols] = x_ref[p].T


def rim_kernel(
    x_ref, c_ref, strip_ref, row_even, row_odd, w1_ref, s1_ref, b1_ref, s2_ref, b2_ref, s3_ref, b3_ref, w2, w2t, w3_ref, w3t_ref,
    acts, gcat, d1, gw3_ref, full_ref, gw1_ref, xt, same, pick,
    share_ref, g1, back, hacts, hgrad, far_ref,
    *, rows, cols, chans, inner, group_ch,
):
    wide = cols + STRIP
    col_ok = column_mask(wide, cols, inner)
    s1, b1, s2, b2, s3, b3 = (v[...] for v in (s1_ref, b1_ref, s2_ref, b2_ref, s3_ref, b3_ref))
    row_is_odd = lax.axis_index("row") % 2
    has_low, has_high = has_neighbours("row")

    @pl.when(row_is_odd == 0)
    def _():
        far_ref[0:3] = row_odd[...]
        far_ref[3:6] = row_even[...]

    @pl.when(row_is_odd == 1)
    def _():
        far_ref[0:3] = row_even[...]
        far_ref[3:6] = row_odd[...]

    def wider(ref, r, base):
        return jnp.concatenate([ref[r], strip_ref[base + r]], axis=0)

    far = [far_ref[i] for i in (0, 1, 3, 4)]
    act, _ = reduce_act(jnp.concatenate(far, axis=0), w1_ref[...], s1, b1)
    for k in range(4):
        spread(hacts, k, act[k * wide : (k + 1) * wide] * (col_ok * (has_low if k < 2 else has_high)))
    def act_row(r):
        return hacts[r] if r < 2 else acts[r - 2] if r < rows + 2 else hacts[r - rows]

    conv = jnp.concatenate(conv_pairs(act_row, (0, rows), w2), axis=0)
    skip = jnp.concatenate([far[1], wider(x_ref, 0, 0), wider(x_ref, rows - 1, 0), far[2]], axis=0)
    ct = jnp.concatenate([far_ref[2], wider(c_ref, 0, rows), wider(c_ref, rows - 1, rows), far_ref[5]], axis=0)
    a2, grad3, back3, grad2 = through(conv, skip, ct, s2, b2, w3_ref[...], w3t_ref[...], s3, b3)
    for k in range(4):
        g = grad2[k * wide : (k + 1) * wide] * col_ok
        spread(hgrad, k, g * has_low if k == 0 else g * has_high if k == 3 else g)
    own = [slice(k * wide, k * wide + cols) for k in (1, 2)]
    for k in range(2):
        back[k * cols : (k + 1) * cols, :] = back3[own[k]]
    gw3 = gw3_ref[...] + dot(
        jnp.concatenate([a2[at] for at in own], axis=0).T, jnp.concatenate([grad3[at] for at in own], axis=0)
    )
    def grad_row(q):
        return (hgrad[q] if q < 2 else gcat[q - 2] if q < rows else hgrad[q - rows + 2])[0:cols]

    outs = (0, 1, rows - 2, rows - 1)
    conv = jnp.concatenate(conv_pairs(grad_row, (0, rows - 2), w2t), axis=0)
    slope = jnp.concatenate([d1[0 : 2 * cols, :], d1[(rows - 2) * cols :, :]], axis=0)
    g = (conv * slope).astype(BF)
    g1[...] = g
    own_gt = jnp.concatenate([hgrad[k, 0:cols, inner : 2 * inner] for k in (1, 2)], axis=0).T
    compact = jnp.zeros((inner, inner), F32)
    for dh in range(3):
        near = jnp.concatenate([act_row(q + dh)[0:cols] for q in (1, rows)], axis=0)
        full = ((full_ref[dh] + dot(own_gt, near)) * same[...]).astype(BF)
        compact = compact + dot(full, pick[dh * 3 * inner : (dh + 1) * 3 * inner, :])
    gw2 = compact.T

    gw1 = gw1_ref[...] + dot(xt[...], g)
    n_dp = share_ref.shape[1]
    one, three = chans // n_dp, inner // n_dp
    parity = parity_of_place()
    at = (parity, 1 - parity)
    for h in range(n_dp):
        slot = h ^ lax.axis_index("dp")
        share_ref[at[0], slot, 0:one, :] = gw1[h * one : (h + 1) * one]
        for k in range(chans // inner):
            share_ref[at[1], slot, k * three : (k + 1) * three, :] = gw3[
                h * three : (h + 1) * three, k * inner : (k + 1) * inner
            ]
        group = gw2 if h == 0 else pltpu.roll(gw2, inner - h * three, 1)
        share_ref[at[0], slot, one : one + GROUP_ROWS, :] = group[0:GROUP_ROWS]
        share_ref[at[1], slot, one : one + GROUP_ROWS, :] = group[GROUP_ROWS : 2 * GROUP_ROWS]


def out_kernel(g1_in, g1_rim, back_in, back_rim, w1_ref, out_ref, *, rows, cols, chans):
    w1t = w1_ref[...].T
    for p in range(rows):
        if 2 <= p < rows - 2:
            g = g1_in[(p - 2) * cols : (p - 1) * cols, :]
        else:
            k = p if p < 2 else p - rows + 4
            g = g1_rim[k * cols : (k + 1) * cols, :]
        if 1 <= p < rows - 1:
            b = back_in[(p - 1) * cols : p * cols, :]
        else:
            b = back_rim[0:cols, :] if p == 0 else back_rim[cols:, :]
        out_ref[p] = (dot(g, w1t) + b).astype(BF)


def last_kernel(
    a_ref, b_ref, r_out, g_out, e_out, r_ref, g_ref, e_ref, sems, *, scale, one, three, chans, inner, group_ch
):
    other_first = parity_of_place() == 1
    first = jnp.where(other_first, b_ref[...], a_ref[...]) * scale
    second = jnp.where(other_first, a_ref[...], b_ref[...]) * scale
    r_ref[...] = first[0:one]
    for k in range(chans // inner):
        e_ref[:, k * inner : (k + 1) * inner] = second[k * three : (k + 1) * three]
    for t in range(9):
        at = t * group_ch
        part = first[one + at : one + at + group_ch] if at < GROUP_ROWS else second[
            one + at - GROUP_ROWS : one + at - GROUP_ROWS + group_ch]
        g_ref[t // 3, t % 3] = part[:, 0:three]
    copies = [
        pltpu.make_async_copy(src, dst, sems.at[i])
        for i, (src, dst) in enumerate(((r_ref, r_out), (e_ref, e_out), (g_ref, g_out)))
    ]
    for copy in copies:
        copy.start()
    for copy in copies:
        copy.wait()


def crossed(value, axis, bit):
    n_row = lax.axis_size("row")
    if axis == "row":
        return lax.ppermute(value, "row", [(i, i ^ bit ^ 1) for i in range(n_row)])
    count = lax.axis_size(axis)
    pairs = [(i, j, i ^ bit, j ^ 1) for i in range(count) for j in range(n_row)]
    if axis == "dp":
        return lax.ppermute(value, ("dp", "row"), [(i * n_row + j, k * n_row + m) for i, j, k, m in pairs])
    return lax.ppermute(value, ("row", "col"), [(j * count + i, m * count + k) for i, j, k, m in pairs])


def body(
    features, reduce_weight, scale_one, shift_one, group_weight, scale_two, shift_two, expand_weight, scale_three,
    shift_three, cotangent,
):
    _, rows, cols, chans = features.shape
    inner = reduce_weight.shape[1]
    group_ch = group_weight.shape[2]
    x, c = features[0], cotangent[0]
    n_dp, n_row, n_col = (lax.axis_size(a) for a in ("dp", "row", "col"))

    wide = cols + STRIP
    one, three = chans // n_dp, inner // n_dp
    half_rows = one + GROUP_ROWS
    vmem = pl.BlockSpec(memory_space=pltpu.VMEM)
    params = pltpu.CompilerParams(vmem_limit_bytes=8 << 20)
    sizes = dict(rows=rows, cols=cols, chans=chans)
    shape = jax.ShapeDtypeStruct

    x, c = (pltpu.with_memory_space_constraint(v, pltpu.HBM) for v in (x, c))
    to_odd, to_even = pl.pallas_call(
        functools.partial(cut_kernel, rows=rows, cols=cols),
        out_shape=(shape((2 * rows, EDGE, chans), BF),) * 2,
        in_specs=[pl.BlockSpec(memory_space=pltpu.HBM)] * 2,
        out_specs=(vmem,) * 2,
        scratch_shapes=[pltpu.VMEM((2 * rows, 8, chans), BF)] * 2 + [pltpu.SemaphoreType.DMA((4,))],
        compiler_params=params,
        name="cut",
    )(x, c)
    col_even, col_odd = swap_edges(to_even, to_odd, "col")
    sources = (
        expand_weight, reduce_weight, x, c, scale_one[None], shift_one[None], scale_two[None], shift_two[None],
        scale_three[None], shift_three[None],
    )
    w3, w1, x, c, *vecs, w2, w2t, w3t, same, pick = pl.pallas_call(
        functools.partial(load_kernel, inner=inner, group_ch=group_ch),
        out_shape=tuple(shape(v.shape, v.dtype) for v in sources)
        + (shape((12 * inner, 2 * inner), BF), shape((12 * inner, 2 * inner), BF), shape((chans, inner), BF))
        + (shape((inner, 3 * inner), F32), shape((9 * inner, inner), BF)),
        in_specs=[pl.BlockSpec(memory_space=pltpu.HBM)] * 11,
        out_specs=(vmem,) * 15,
        scratch_shapes=[pltpu.VMEM(group_weight.shape, BF), pltpu.SemaphoreType.DMA((11,))],
        compiler_params=params,
        name="load",
    )(*(pltpu.with_memory_space_constraint(v, pltpu.HBM) for v in (group_weight, *sources)))
    shared = (w1, *vecs, w2, w2t, w3, w3t)
    col_odd, col_even, shared, x, c = lax.optimization_barrier((col_odd, col_even, shared, x, c))
    strip, to_even, to_odd = pl.pallas_call(
        functools.partial(edges_kernel, rows=rows, cols=cols),
        out_shape=(shape((2 * rows, STRIP, chans), BF),) + (shape((3, wide, chans), BF),) * 2,
        in_specs=[vmem] * 4,
        out_specs=(vmem,) * 3,
        compiler_params=params,
        name="edges",
    )(x, c, col_odd, col_even)
    row_even, row_odd = swap_edges(to_even, to_odd, "row")
    acts, gcat, d1, back_in, g1_in, gw3, full, gw1, xt = pl.pallas_call(
        functools.partial(inner_kernel, inner=inner, **sizes),
        out_shape=(
            shape((rows, wide, 3 * inner), BF),
            shape((rows - 2, wide, 3 * inner), BF),
            shape((rows * cols, inner), F32),
            shape(((rows - 2) * cols, chans), F32),
            shape(((rows - 4) * cols, inner), BF),
            shape((inner, chans), F32),
            shape((3, inner, 3 * inner), F32),
            shape((chans, inner), F32),
            shape((chans, 4 * cols), BF),
        ),
        in_specs=[vmem] * 14,
        out_specs=(vmem,) * 9,
        scratch_shapes=[pltpu.VMEM((rows, wide, chans), BF), pltpu.VMEM((rows, wide, chans), BF)],
        compiler_params=params,
        name="inner",
    )(x, c, strip, *shared)
    shares, g1_rim, back_rim = pl.pallas_call(
        functools.partial(rim_kernel, inner=inner, group_ch=group_ch, **sizes),
        out_shape=(
            shape((2, n_dp, half_rows, inner), F32),
            shape((4 * cols, inner), BF),
            shape((2 * cols, chans), F32),
        ),
        in_specs=[vmem] * 25,
        out_specs=(vmem,) * 3,
        scratch_shapes=[pltpu.VMEM((4, wide, 3 * inner), BF)] * 2 + [pltpu.VMEM((6, wide, chans), BF)],
        compiler_params=params,
        name="rim",
    )(x, c, strip, row_even, row_odd, *shared, acts, gcat, d1, gw3, full, gw1, xt, same, pick)
    near = [(i, i ^ 1) for i in range(n_row)]
    shares = (shares[0] + lax.ppermute(shares[1], "row", near)).astype(BF)
    g1_rim, shares = lax.optimization_barrier((g1_rim, shares))
    input_grad = pl.pallas_call(
        functools.partial(out_kernel, **sizes),
        out_shape=shape((rows, cols, chans), BF),
        in_specs=[vmem] * 5,
        out_specs=vmem,
        compiler_params=params,
        name="out",
    )(g1_in, g1_rim, back_in, back_rim, w1)
    held = n_dp
    while held > 1:
        held //= 2
        other = crossed(shares[held:], "dp", held)
        shares = (shares[:held].astype(F32) + other.astype(F32)).astype(BF)
    total = shares[0]
    steps = [("row", 1 << k) for k in range(1, n_row.bit_length() - 1)]
    steps += [("col", 1 << k) for k in range(n_col.bit_length() - 1)]
    for axis, bit in steps:
        other = crossed(total, axis, bit)
        if (axis, bit) == steps[0]:
            input_grad, other = lax.optimization_barrier((input_grad, other))
        summed = total.astype(F32) + other.astype(F32)
        total = summed.astype(BF)
    pixels = rows * cols * n_dp * n_row * n_col
    reduce_grad, group_grad, expand_grad = pl.pallas_call(
        functools.partial(
            last_kernel, scale=pixels**-0.5, one=one, three=three, chans=chans, inner=inner, group_ch=group_ch
        ),
        out_shape=(
            jax.ShapeDtypeStruct((one, inner), F32),
            jax.ShapeDtypeStruct((3, 3, group_ch, three), F32),
            jax.ShapeDtypeStruct((three, chans), F32),
        ),
        in_specs=[vmem, vmem],
        out_specs=(pl.BlockSpec(memory_space=pl.ANY),) * 3,
        scratch_shapes=[
            pltpu.VMEM((one, inner), F32),
            pltpu.VMEM((3, 3, group_ch, three), F32),
            pltpu.VMEM((three, chans), F32),
            pltpu.SemaphoreType.DMA((3,)),
        ],
        compiler_params=pltpu.CompilerParams(vmem_limit_bytes=2 << 20),
        name="last",
    )(summed, lax.ppermute(summed, "row", near))
    return input_grad[None], reduce_grad, jnp.transpose(group_grad, (3, 0, 1, 2)), expand_grad


def solution(mesh):
    image = P("dp", "row", "col", None)
    return jax.shard_map(
        body,
        mesh=mesh,
        in_specs=(image,) + (P(),) * 9 + (image,),
        out_specs=(image, P("dp", None), P("dp", None, None, None), P("dp", None)),
        check_vma=False,
    )
```

```python
import functools
import itertools

import jax
import jax.numpy as jnp
from jax import lax
from jax.experimental import pallas as pl
from jax.experimental.pallas import tpu as pltpu
from jax.sharding import PartitionSpec as P

BF = jnp.bfloat16
F32 = jnp.float32
EDGE = 2
STRIP = 16
GROUP_ROWS = 24


def swap_edges(to_even, to_odd, axis):
    count, bands = lax.axis_size(axis), lax.axis_size("dp")
    got_even = lax.ppermute(to_even, axis, [(i, i ^ 1) for i in range(count)])
    names = ("dp", "row", "col")
    sizes = [lax.axis_size(a) for a in names]
    which = names.index(axis)
    perm = []
    for at in itertools.product(*(range(n) for n in sizes)):
        to = list(at)
        if 0 < at[which] < count - 1:
            to[which] = ((at[which] - 1) ^ 1) + 1
        elif axis == "col":
            to[1] ^= 1
        elif bands > 1:
            to[0] ^= 1
        perm.append(tuple(functools.reduce(lambda v, k: v * sizes[k] + p[k], range(3), 0) for p in (at, to)))
    got_odd = lax.ppermute(to_odd, names, perm)
    return got_even, got_odd


def dot(a, b):
    return jnp.dot(a, b, preferred_element_type=F32)


def gate(v):
    return 0.5 + 0.5 * jnp.tanh(0.5 * v)


def parity_of_place():
    bits = 0
    for axis in ("dp", "row", "col"):
        at = lax.axis_index(axis)
        for k in range((lax.axis_size(axis) - 1).bit_length()):
            bits = bits + (at >> k)
    return bits % 2


def has_neighbours(axis):
    at = lax.axis_index(axis)
    return jnp.where(at > 0, 1.0, 0.0).astype(F32), jnp.where(at < lax.axis_size(axis) - 1, 1.0, 0.0).astype(F32)


def column_mask(wide, cols, inner):
    spot = lax.broadcasted_iota(jnp.int32, (wide, inner), 0)
    has_low, has_high = has_neighbours("col")
    return jnp.where(spot < cols, 1.0, jnp.where(spot < cols + STRIP // 2, has_high, has_low))


def spread(ref, r, v):
    wide, inner = v.shape
    ref[r, :, 0:inner] = pltpu.roll(v, 1, 0).astype(BF)
    ref[r, :, inner : 2 * inner] = v.astype(BF)
    ref[r, :, 2 * inner :] = pltpu.roll(v, wide - 1, 0).astype(BF)


def conv_pairs(row, starts, w_ref):
    left = [jnp.concatenate([row(i + j) for j in range(4)], axis=1) for i in starts]
    out = dot(jnp.concatenate(left, axis=0), w_ref[...])
    n, inner = left[0].shape[0], w_ref.shape[1] // 2
    return [out[i * n : (i + 1) * n, k * inner : (k + 1) * inner] for i in range(len(starts)) for k in range(2)]


def reduce_act(x, w1, s1, b1):
    pre = dot(x, w1) * s1 + b1
    sg = gate(pre)
    return pre * sg, sg


def through(conv, skip, ct, s2, b2, w3, w3t, s3, b3):
    pre2 = conv * s2 + b2
    sg2 = gate(pre2)
    silu2 = pre2 * sg2
    a2 = silu2.astype(BF)
    pre3 = dot(a2, w3) * s3 + b3 + skip.astype(F32)
    sg3 = gate(pre3)
    back3 = ct.astype(F32) * (sg3 + pre3 * sg3 * (1.0 - sg3))
    grad3 = (back3 * s3).astype(BF)
    grad2 = dot(grad3, w3t) * ((sg2 + silu2 * (1.0 - sg2)) * s2)
    return a2, grad3, back3, grad2


def cut_kernel(x_hbm, c_hbm, odd_ref, even_ref, low_ref, high_ref, sems, *, rows, cols):
    copies = []
    for i, src in enumerate((x_hbm, c_hbm)):
        at = slice(i * rows, (i + 1) * rows)
        copies.append(pltpu.make_async_copy(src.at[:, 0:8, :], low_ref.at[at], sems.at[2 * i]))
        copies.append(pltpu.make_async_copy(src.at[:, cols - 8 : cols, :], high_ref.at[at], sems.at[2 * i + 1]))
    for copy in copies:
        copy.start()
    is_odd = lax.axis_index("col") % 2 == 1
    for copy in copies:
        copy.wait()
    for r in range(2 * rows):
        low = low_ref[r].astype(F32)[0:EDGE]
        high = high_ref[r].astype(F32)[8 - EDGE : 8]
        even_ref[r] = jnp.where(is_odd, low, high).astype(BF)
        odd_ref[r] = jnp.where(is_odd, high, low).astype(BF)


def load_kernel(*refs, inner, group_ch):
    sources, targets, (w2, w2t, w3t, same, pick, gw_ref, sems) = refs[:11], refs[11:21], refs[21:]
    gw_hbm, sources = sources[0], sources[1:]
    copies = [pltpu.make_async_copy(gw_hbm, gw_ref, sems.at[10])]
    copies += [pltpu.make_async_copy(src, dst, sems.at[i]) for i, (src, dst) in enumerate(zip(sources, targets))]
    for copy in copies:
        copy.start()
    copies[0].wait()
    sub = lax.broadcasted_iota(jnp.int32, (inner, inner), 0)
    lane = lax.broadcasted_iota(jnp.int32, (inner, inner), 1)
    diag = jnp.where(sub // group_ch == lane // group_ch, 1.0, 0.0).astype(F32)
    for t in range(9):
        four = gw_ref[t // 3, t % 3].astype(F32)
        eight = jnp.concatenate([four, four], axis=0)
        tiled = jnp.broadcast_to(eight[None], (inner // 8, 8, inner)).reshape(inner, inner)
        dense = tiled * diag
        for ref, tap, block in ((w2, t, dense.astype(BF)), (w2t, 8 - t, dense.T.astype(BF))):
            ref[tap * inner : (tap + 1) * inner, 0:inner] = block
            ref[(tap + 3) * inner : (tap + 4) * inner, inner:] = block
    for ref in (w2, w2t):
        ref[9 * inner :, 0:inner] = jnp.zeros((3 * inner, inner), BF)
        ref[0 : 3 * inner, inner:] = jnp.zeros((3 * inner, inner), BF)
    for k in range(3):
        same[:, k * inner : (k + 1) * inner] = diag
    for t in range(9):
        place = t * group_ch + sub % group_ch
        pick[t * inner : (t + 1) * inner, :] = jnp.where(lane == place, 1.0, 0.0).astype(BF)
    copies[1].wait()
    w3t[...] = targets[0][...].T
    for copy in copies[2:]:
        copy.wait()


def edges_kernel(
    x_ref, c_ref, col_odd, col_even, w1_ref, s1_ref, b1_ref, strip, odd_ref, even_ref, *, rows, cols
):
    col_is_odd = lax.axis_index("col") % 2 == 1
    row_is_odd = lax.axis_index("row") % 2
    chans, inner = w1_ref.shape
    wide = cols + STRIP
    gap = jnp.zeros((STRIP - 2 * EDGE, chans), F32)
    for r in range(2 * rows):
        a, b = col_even[r].astype(F32), col_odd[r].astype(F32)
        high, low = jnp.where(col_is_odd, b, a), jnp.where(col_is_odd, a, b)
        strip[r] = jnp.concatenate([high, gap, low], axis=0).astype(BF)
    behind = [v for r in (1, rows - 2) for v in (x_ref[r], strip[r])]
    act, _ = reduce_act(jnp.concatenate(behind, axis=0), w1_ref[...], s1_ref[...], b1_ref[...])
    col_ok = column_mask(wide, cols, inner)
    act_low, act_high = act[0:wide] * col_ok, act[wide:] * col_ok
    for ref, sends_high in ((even_ref, row_is_odd == 0), (odd_ref, row_is_odd == 1)):
        at = jnp.where(sends_high, rows - 1, 0)
        ref[0:cols, :] = x_ref[at]
        ref[cols:wide, :] = strip[at]
        ref[wide : wide + cols, :] = c_ref[at]
        ref[wide + cols : 2 * wide, :] = strip[rows + at]
        sent = jnp.where(sends_high, act_high, act_low)
        ref[2 * wide :, 0:inner] = sent[0 : wide // 2].astype(BF)
        ref[2 * wide :, inner:] = sent[wide // 2 :].astype(BF)


def inner_kernel(
    x_ref, c_ref, strip_ref, w1_ref, s1_ref, b1_ref, s2_ref, b2_ref, s3_ref, b3_ref, w2, w2t, w3_ref, w3t_ref,
    acts, gcat, d1, back, g1, gw3_ref, full_ref, gw1_ref, xt, xs, cs,
    *, rows, cols, chans, inner,
):
    wide = cols + STRIP
    step = 2
    col_ok = column_mask(wide, cols, inner)
    s1, b1, s2, b2, s3, b3 = (v[...] for v in (s1_ref, b1_ref, s2_ref, b2_ref, s3_ref, b3_ref))
    w1 = w1_ref[...]
    for r in range(rows):
        xs[r, 0:cols, :] = x_ref[r]
        xs[r, cols:wide, :] = strip_ref[r]
        cs[r, 0:cols, :] = c_ref[r]
        cs[r, cols:wide, :] = strip_ref[rows + r]
    for r0 in range(0, rows, step):
        act, sg = reduce_act(xs[r0 : r0 + step].reshape(step * wide, chans), w1, s1, b1)
        slope = (sg + act * (1.0 - sg)) * s1
        for k in range(step):
            r = r0 + k
            spread(acts, r, act[k * wide : (k + 1) * wide] * col_ok)
            d1[r * cols : (r + 1) * cols, :] = slope[k * wide : k * wide + cols]
    rest = (s2, b2, w3_ref[...], w3t_ref[...], s3, b3)
    gw3 = jnp.zeros((inner, chans), F32)
    convs = conv_pairs(lambda r: acts[r], range(0, rows - 2, step), w2)
    for p0 in range(1, rows - 1, step):
        conv = jnp.concatenate(convs[p0 - 1 : p0 - 1 + step], axis=0)
        skip = xs[p0 : p0 + step].reshape(step * wide, chans)
        ct = cs[p0 : p0 + step].reshape(step * wide, chans)
        a2, grad3, back3, grad2 = through(conv, skip, ct, *rest)
        for k in range(step):
            spread(gcat, p0 - 1 + k, grad2[k * wide : (k + 1) * wide] * col_ok)
            back[(p0 - 1 + k) * cols : (p0 + k) * cols, :] = back3[k * wide : k * wide + cols]
        own = [slice(k * wide, k * wide + cols) for k in range(step)]
        gw3 = gw3 + dot(
            jnp.concatenate([a2[at] for at in own], axis=0).T, jnp.concatenate([grad3[at] for at in own], axis=0)
        )
    gw3_ref[...] = gw3
    n = (rows - 2) * cols
    own_gt = gcat[:, 0:cols, inner : 2 * inner].reshape(n, inner).T
    for dh in range(3):
        full_ref[dh] = dot(own_gt, acts[dh : dh + rows - 2, 0:cols, :].reshape(n, 3 * inner))
    gw1t = jnp.zeros((inner, chans), F32)
    convs = conv_pairs(lambda r: gcat[r, 0:cols, :], range(0, rows - 4, step), w2t)
    for p0 in range(2, rows - 2, step):
        conv = jnp.concatenate(convs[p0 - 2 : p0 - 2 + step], axis=0)
        g = (conv * d1[p0 * cols : (p0 + step) * cols, :]).astype(BF)
        g1[(p0 - 2) * cols : (p0 - 2 + step) * cols, :] = g
        gw1t = gw1t + dot(g.T, x_ref[p0 : p0 + step].reshape(step * cols, chans))
    gw1_ref[...] = gw1t.T
    for k, p in enumerate((0, 1, rows - 2, rows - 1)):
        xt[:, k * cols : (k + 1) * cols] = x_ref[p].T


def rim_kernel(
    x_ref, c_ref, strip_ref, row_even, row_odd, w1_ref, s1_ref, b1_ref, s2_ref, b2_ref, s3_ref, b3_ref, w2, w2t, w3_ref, w3t_ref,
    acts, gcat, d1, gw3_ref, full_ref, gw1_ref, xt, same, pick,
    share_ref, g1, back, hacts, hgrad, far_ref,
    *, rows, cols, chans, inner, group_ch,
):
    wide = cols + STRIP
    col_ok = column_mask(wide, cols, inner)
    s1, b1, s2, b2, s3, b3 = (v[...] for v in (s1_ref, b1_ref, s2_ref, b2_ref, s3_ref, b3_ref))
    row_is_odd = lax.axis_index("row") % 2
    has_low, has_high = has_neighbours("row")

    @pl.when(row_is_odd == 0)
    def _():
        far_ref[0] = row_odd[...]
        far_ref[1] = row_even[...]

    @pl.when(row_is_odd == 1)
    def _():
        far_ref[0] = row_even[...]
        far_ref[1] = row_odd[...]

    def wider(ref, r, base):
        return jnp.concatenate([ref[r], strip_ref[base + r]], axis=0)

    near = [far_ref[i, 0:wide, :] for i in range(2)]
    near_cot = [far_ref[i, wide : 2 * wide, :] for i in range(2)]
    act, _ = reduce_act(jnp.concatenate(near, axis=0), w1_ref[...], s1, b1)
    for k, has in ((0, has_low), (1, has_high)):
        sent = far_ref[k, 2 * wide :, :].astype(F32)
        spread(hacts, 3 * k, jnp.concatenate([sent[:, 0:inner], sent[:, inner:]], axis=0) * has)
        spread(hacts, 1 + k, act[k * wide : (k + 1) * wide] * (col_ok * has))
    def act_row(r):
        return hacts[r] if r < 2 else acts[r - 2] if r < rows + 2 else hacts[r - rows]

    conv = jnp.concatenate(conv_pairs(act_row, (0, rows), w2), axis=0)
    skip = jnp.concatenate([near[0], wider(x_ref, 0, 0), wider(x_ref, rows - 1, 0), near[1]], axis=0)
    ct = jnp.concatenate([near_cot[0], wider(c_ref, 0, rows), wider(c_ref, rows - 1, rows), near_cot[1]], axis=0)
    a2, grad3, back3, grad2 = through(conv, skip, ct, s2, b2, w3_ref[...], w3t_ref[...], s3, b3)
    for k in range(4):
        g = grad2[k * wide : (k + 1) * wide] * col_ok
        spread(hgrad, k, g * has_low if k == 0 else g * has_high if k == 3 else g)
    own = [slice(k * wide, k * wide + cols) for k in (1, 2)]
    for k in range(2):
        back[k * cols : (k + 1) * cols, :] = back3[own[k]]
    gw3 = gw3_ref[...] + dot(
        jnp.concatenate([a2[at] for at in own], axis=0).T, jnp.concatenate([grad3[at] for at in own], axis=0)
    )
    def grad_row(q):
        return (hgrad[q] if q < 2 else gcat[q - 2] if q < rows else hgrad[q - rows + 2])[0:cols]

    outs = (0, 1, rows - 2, rows - 1)
    conv = jnp.concatenate(conv_pairs(grad_row, (0, rows - 2), w2t), axis=0)
    slope = jnp.concatenate([d1[0 : 2 * cols, :], d1[(rows - 2) * cols :, :]], axis=0)
    g = (conv * slope).astype(BF)
    g1[...] = g
    own_gt = jnp.concatenate([hgrad[k, 0:cols, inner : 2 * inner] for k in (1, 2)], axis=0).T
    compact = jnp.zeros((inner, inner), F32)
    for dh in range(3):
        around = jnp.concatenate([act_row(q + dh)[0:cols] for q in (1, rows)], axis=0)
        full = ((full_ref[dh] + dot(own_gt, around)) * same[...]).astype(BF)
        compact = compact + dot(full, pick[dh * 3 * inner : (dh + 1) * 3 * inner, :])
    gw2 = compact.T

    gw1 = gw1_ref[...] + dot(xt[...], g)
    n_dp = share_ref.shape[1]
    one, three = chans // n_dp, inner // n_dp
    parity = parity_of_place()
    at = (parity, 1 - parity)
    for h in range(n_dp):
        slot = h ^ lax.axis_index("dp")
        share_ref[at[0], slot, 0:one, :] = gw1[h * one : (h + 1) * one]
        for k in range(chans // inner):
            share_ref[at[1], slot, k * three : (k + 1) * three, :] = gw3[
                h * three : (h + 1) * three, k * inner : (k + 1) * inner
            ]
        group = gw2 if h == 0 else pltpu.roll(gw2, inner - h * three, 1)
        share_ref[at[0], slot, one : one + GROUP_ROWS, :] = group[0:GROUP_ROWS]
        share_ref[at[1], slot, one : one + GROUP_ROWS, :] = group[GROUP_ROWS : 2 * GROUP_ROWS]


def out_kernel(g1_in, g1_rim, back_in, back_rim, w1_ref, out_ref, *, rows, cols, chans):
    w1t = w1_ref[...].T
    for p in range(rows):
        if 2 <= p < rows - 2:
            g = g1_in[(p - 2) * cols : (p - 1) * cols, :]
        else:
            k = p if p < 2 else p - rows + 4
            g = g1_rim[k * cols : (k + 1) * cols, :]
        if 1 <= p < rows - 1:
            b = back_in[(p - 1) * cols : p * cols, :]
        else:
            b = back_rim[0:cols, :] if p == 0 else back_rim[cols:, :]
        out_ref[p] = (dot(g, w1t) + b).astype(BF)


def last_kernel(
    a_ref, b_ref, r_out, g_out, e_out, r_ref, g_ref, e_ref, sems, *, scale, one, three, chans, inner, group_ch
):
    other_first = parity_of_place() == 1
    first = jnp.where(other_first, b_ref[...], a_ref[...]) * scale
    second = jnp.where(other_first, a_ref[...], b_ref[...]) * scale
    r_ref[...] = first[0:one]
    for k in range(chans // inner):
        e_ref[:, k * inner : (k + 1) * inner] = second[k * three : (k + 1) * three]
    for t in range(9):
        at = t * group_ch
        part = first[one + at : one + at + group_ch] if at < GROUP_ROWS else second[
            one + at - GROUP_ROWS : one + at - GROUP_ROWS + group_ch]
        g_ref[t // 3, t % 3] = part[:, 0:three]
    copies = [
        pltpu.make_async_copy(src, dst, sems.at[i])
        for i, (src, dst) in enumerate(((r_ref, r_out), (e_ref, e_out), (g_ref, g_out)))
    ]
    for copy in copies:
        copy.start()
    for copy in copies:
        copy.wait()


def crossed(value, move, other_move):
    names = ("dp", "row", "col")
    sizes = [lax.axis_size(a) for a in names]
    perm = []
    for at in itertools.product(*(range(n) for n in sizes)):
        axis, bit = other_move if sum(i.bit_count() for i in at) % 2 else move
        to = list(at)
        to[names.index(axis)] ^= bit
        to[1] ^= 1
        perm.append(tuple(functools.reduce(lambda v, k: v * sizes[k] + p[k], range(3), 0) for p in (at, to)))
    return lax.ppermute(value, names, perm)


def body(
    features, reduce_weight, scale_one, shift_one, group_weight, scale_two, shift_two, expand_weight, scale_three,
    shift_three, cotangent,
):
    _, rows, cols, chans = features.shape
    inner = reduce_weight.shape[1]
    group_ch = group_weight.shape[2]
    x, c = features[0], cotangent[0]
    n_dp, n_row, n_col = (lax.axis_size(a) for a in ("dp", "row", "col"))

    wide = cols + STRIP
    one, three = chans // n_dp, inner // n_dp
    half_rows = one + GROUP_ROWS
    vmem = pl.BlockSpec(memory_space=pltpu.VMEM)
    params = pltpu.CompilerParams(vmem_limit_bytes=8 << 20)
    sizes = dict(rows=rows, cols=cols, chans=chans)
    shape = jax.ShapeDtypeStruct

    x, c = (pltpu.with_memory_space_constraint(v, pltpu.HBM) for v in (x, c))
    to_odd, to_even = pl.pallas_call(
        functools.partial(cut_kernel, rows=rows, cols=cols),
        out_shape=(shape((2 * rows, EDGE, chans), BF),) * 2,
        in_specs=[pl.BlockSpec(memory_space=pltpu.HBM)] * 2,
        out_specs=(vmem,) * 2,
        scratch_shapes=[pltpu.VMEM((2 * rows, 8, chans), BF)] * 2 + [pltpu.SemaphoreType.DMA((4,))],
        compiler_params=params,
        name="cut",
    )(x, c)
    col_even, col_odd = swap_edges(to_even, to_odd, "col")
    sources = (
        expand_weight, reduce_weight, x, c, scale_one[None], shift_one[None], scale_two[None], shift_two[None],
        scale_three[None], shift_three[None],
    )
    w3, w1, x, c, *vecs, w2, w2t, w3t, same, pick = pl.pallas_call(
        functools.partial(load_kernel, inner=inner, group_ch=group_ch),
        out_shape=tuple(shape(v.shape, v.dtype) for v in sources)
        + (shape((12 * inner, 2 * inner), BF), shape((12 * inner, 2 * inner), BF), shape((chans, inner), BF))
        + (shape((inner, 3 * inner), F32), shape((9 * inner, inner), BF)),
        in_specs=[pl.BlockSpec(memory_space=pltpu.HBM)] * 11,
        out_specs=(vmem,) * 15,
        scratch_shapes=[pltpu.VMEM(group_weight.shape, BF), pltpu.SemaphoreType.DMA((11,))],
        compiler_params=params,
        name="load",
    )(*(pltpu.with_memory_space_constraint(v, pltpu.HBM) for v in (group_weight, *sources)))
    shared = (w1, *vecs, w2, w2t, w3, w3t)
    col_odd, col_even, shared, x, c = lax.optimization_barrier((col_odd, col_even, shared, x, c))
    w1, *vecs = shared[:7]
    message = 2 * wide + wide * inner // chans
    strip, to_odd, to_even = pl.pallas_call(
        functools.partial(edges_kernel, rows=rows, cols=cols),
        out_shape=(shape((2 * rows, STRIP, chans), BF),) + (shape((message, chans), BF),) * 2,
        in_specs=[vmem] * 7,
        out_specs=(vmem,) * 3,
        compiler_params=params,
        name="edges",
    )(x, c, col_odd, col_even, w1, *vecs[:2])
    row_even, row_odd = swap_edges(to_even, to_odd, "row")
    acts, gcat, d1, back_in, g1_in, gw3, full, gw1, xt = pl.pallas_call(
        functools.partial(inner_kernel, inner=inner, **sizes),
        out_shape=(
            shape((rows, wide, 3 * inner), BF),
            shape((rows - 2, wide, 3 * inner), BF),
            shape((rows * cols, inner), F32),
            shape(((rows - 2) * cols, chans), F32),
            shape(((rows - 4) * cols, inner), BF),
            shape((inner, chans), F32),
            shape((3, inner, 3 * inner), F32),
            shape((chans, inner), F32),
            shape((chans, 4 * cols), BF),
        ),
        in_specs=[vmem] * 14,
        out_specs=(vmem,) * 9,
        scratch_shapes=[pltpu.VMEM((rows, wide, chans), BF), pltpu.VMEM((rows, wide, chans), BF)],
        compiler_params=params,
        name="inner",
    )(x, c, strip, *shared)
    shares, g1_rim, back_rim = pl.pallas_call(
        functools.partial(rim_kernel, inner=inner, group_ch=group_ch, **sizes),
        out_shape=(
            shape((2, n_dp, half_rows, inner), F32),
            shape((4 * cols, inner), BF),
            shape((2 * cols, chans), F32),
        ),
        in_specs=[vmem] * 25,
        out_specs=(vmem,) * 3,
        scratch_shapes=[pltpu.VMEM((4, wide, 3 * inner), BF)] * 2 + [pltpu.VMEM((2, message, chans), BF)],
        compiler_params=params,
        name="rim",
    )(x, c, strip, row_even, row_odd, *shared, acts, gcat, d1, gw3, full, gw1, xt, same, pick)
    near = [(i, i ^ 1) for i in range(n_row)]
    shares = (shares[0] + lax.ppermute(shares[1], "row", near)).astype(BF)
    g1_rim, shares = lax.optimization_barrier((g1_rim, shares))
    input_grad = pl.pallas_call(
        functools.partial(out_kernel, **sizes),
        out_shape=shape((rows, cols, chans), BF),
        in_specs=[vmem] * 5,
        out_specs=vmem,
        compiler_params=params,
        name="out",
    )(g1_in, g1_rim, back_in, back_rim, w1)
    held = n_dp
    while held > 1:
        held //= 2
        other = crossed(shares[held:], ("dp", held), ("dp", held))
        shares = (shares[:held].astype(F32) + other.astype(F32)).astype(BF)
    total = shares[0]
    steps = [("row", 1 << k) for k in range(1, n_row.bit_length() - 1)]
    steps += [("col", 1 << k) for k in reversed(range(n_col.bit_length() - 1))]
    for i, step in enumerate(steps):
        other = crossed(total, step, steps[(i + 1) % len(steps)])
        if i == 0:
            input_grad, other = lax.optimization_barrier((input_grad, other))
        summed = total.astype(F32) + other.astype(F32)
        total = summed.astype(BF)
    pixels = rows * cols * n_dp * n_row * n_col
    reduce_grad, group_grad, expand_grad = pl.pallas_call(
        functools.partial(
            last_kernel, scale=pixels**-0.5, one=one, three=three, chans=chans, inner=inner, group_ch=group_ch
        ),
        out_shape=(
            jax.ShapeDtypeStruct((one, inner), F32),
            jax.ShapeDtypeStruct((3, 3, group_ch, three), F32),
            jax.ShapeDtypeStruct((three, chans), F32),
        ),
        in_specs=[vmem, vmem],
        out_specs=(pl.BlockSpec(memory_space=pl.ANY),) * 3,
        scratch_shapes=[
            pltpu.VMEM((one, inner), F32),
            pltpu.VMEM((3, 3, group_ch, three), F32),
            pltpu.VMEM((three, chans), F32),
            pltpu.SemaphoreType.DMA((3,)),
        ],
        compiler_params=pltpu.CompilerParams(vmem_limit_bytes=2 << 20),
        name="last",
    )(summed, lax.ppermute(summed, "row", near))
    return input_grad[None], reduce_grad, jnp.transpose(group_grad, (3, 0, 1, 2)), expand_grad


def solution(mesh):
    image = P("dp", "row", "col", None)
    return jax.shard_map(
        body,
        mesh=mesh,
        in_specs=(image,) + (P(),) * 9 + (image,),
        out_specs=(image, P("dp", None), P("dp", None, None, None), P("dp", None)),
        check_vma=False,
    )
```

```python
import functools
import itertools

import jax
import jax.numpy as jnp
from jax import lax
from jax.experimental import pallas as pl
from jax.experimental.pallas import tpu as pltpu
from jax.sharding import PartitionSpec as P

BF = jnp.bfloat16
F32 = jnp.float32
EDGE = 2
STRIP = 16
GROUP_ROWS = 24


def swap_edges(to_even, to_odd, axis):
    count, bands = lax.axis_size(axis), lax.axis_size("dp")
    got_even = lax.ppermute(to_even, axis, [(i, i ^ 1) for i in range(count)])
    names = ("dp", "row", "col")
    sizes = [lax.axis_size(a) for a in names]
    which = names.index(axis)
    perm = []
    for at in itertools.product(*(range(n) for n in sizes)):
        to = list(at)
        if 0 < at[which] < count - 1:
            to[which] = ((at[which] - 1) ^ 1) + 1
        elif axis == "col":
            to[1] ^= 1
        elif bands > 1:
            to[0] ^= 1
        perm.append(tuple(functools.reduce(lambda v, k: v * sizes[k] + p[k], range(3), 0) for p in (at, to)))
    got_odd = lax.ppermute(to_odd, names, perm)
    return got_even, got_odd


def dot(a, b):
    return jnp.dot(a, b, preferred_element_type=F32)


def gate(v):
    return 0.5 + 0.5 * jnp.tanh(0.5 * v)


def parity_of_place():
    bits = 0
    for axis in ("dp", "row", "col"):
        at = lax.axis_index(axis)
        for k in range((lax.axis_size(axis) - 1).bit_length()):
            bits = bits + (at >> k)
    return bits % 2


def has_neighbours(axis):
    at = lax.axis_index(axis)
    return jnp.where(at > 0, 1.0, 0.0).astype(F32), jnp.where(at < lax.axis_size(axis) - 1, 1.0, 0.0).astype(F32)


def column_mask(wide, cols, inner):
    spot = lax.broadcasted_iota(jnp.int32, (wide, inner), 0)
    has_low, has_high = has_neighbours("col")
    return jnp.where(spot < cols, 1.0, jnp.where(spot < cols + STRIP // 2, has_high, has_low))


def spread(ref, r, v):
    wide, inner = v.shape
    ref[r, :, 0:inner] = pltpu.roll(v, 1, 0).astype(BF)
    ref[r, :, inner : 2 * inner] = v.astype(BF)
    ref[r, :, 2 * inner :] = pltpu.roll(v, wide - 1, 0).astype(BF)


def conv_pairs(row, starts, w_ref):
    left = [jnp.concatenate([row(i + j) for j in range(4)], axis=1) for i in starts]
    out = dot(jnp.concatenate(left, axis=0), w_ref[...])
    n, inner = left[0].shape[0], w_ref.shape[1] // 2
    return [out[i * n : (i + 1) * n, k * inner : (k + 1) * inner] for i in range(len(starts)) for k in range(2)]


def reduce_act(x, w1, s1, b1):
    pre = dot(x, w1) * s1 + b1
    sg = gate(pre)
    return pre * sg, sg


def through(conv, skip, ct, s2, b2, w3, w3t, s3, b3):
    pre2 = conv * s2 + b2
    sg2 = gate(pre2)
    silu2 = pre2 * sg2
    a2 = silu2.astype(BF)
    pre3 = dot(a2, w3) * s3 + b3 + skip.astype(F32)
    sg3 = gate(pre3)
    back3 = ct.astype(F32) * (sg3 + pre3 * sg3 * (1.0 - sg3))
    grad3 = (back3 * s3).astype(BF)
    grad2 = dot(grad3, w3t) * ((sg2 + silu2 * (1.0 - sg2)) * s2)
    return a2, grad3, back3, grad2


def cut_kernel(x_hbm, c_hbm, odd_ref, even_ref, low_ref, high_ref, sems, *, rows, cols):
    copies = []
    for i, src in enumerate((x_hbm, c_hbm)):
        at = slice(i * rows, (i + 1) * rows)
        copies.append(pltpu.make_async_copy(src.at[:, 0:8, :], low_ref.at[at], sems.at[2 * i]))
        copies.append(pltpu.make_async_copy(src.at[:, cols - 8 : cols, :], high_ref.at[at], sems.at[2 * i + 1]))
    for copy in copies:
        copy.start()
    is_odd = lax.axis_index("col") % 2 == 1
    for copy in copies:
        copy.wait()
    for r in range(2 * rows):
        low = low_ref[r].astype(F32)[0:EDGE]
        high = high_ref[r].astype(F32)[8 - EDGE : 8]
        even_ref[r] = jnp.where(is_odd, low, high).astype(BF)
        odd_ref[r] = jnp.where(is_odd, high, low).astype(BF)


def load_kernel(*refs, inner, group_ch):
    sources, targets, (w2, w2t, w3t, same, pick, gw_ref, sems) = refs[:11], refs[11:21], refs[21:]
    gw_hbm, sources = sources[0], sources[1:]
    copies = [pltpu.make_async_copy(gw_hbm, gw_ref, sems.at[10])]
    copies += [pltpu.make_async_copy(src, dst, sems.at[i]) for i, (src, dst) in enumerate(zip(sources, targets))]
    for copy in copies:
        copy.start()
    copies[0].wait()
    sub = lax.broadcasted_iota(jnp.int32, (inner, inner), 0)
    lane = lax.broadcasted_iota(jnp.int32, (inner, inner), 1)
    diag = jnp.where(sub // group_ch == lane // group_ch, 1.0, 0.0).astype(F32)
    for t in range(9):
        four = gw_ref[t // 3, t % 3].astype(F32)
        eight = jnp.concatenate([four, four], axis=0)
        tiled = jnp.broadcast_to(eight[None], (inner // 8, 8, inner)).reshape(inner, inner)
        dense = tiled * diag
        for ref, tap, block in ((w2, t, dense.astype(BF)), (w2t, 8 - t, dense.T.astype(BF))):
            ref[tap * inner : (tap + 1) * inner, 0:inner] = block
            ref[(tap + 3) * inner : (tap + 4) * inner, inner:] = block
    for ref in (w2, w2t):
        ref[9 * inner :, 0:inner] = jnp.zeros((3 * inner, inner), BF)
        ref[0 : 3 * inner, inner:] = jnp.zeros((3 * inner, inner), BF)
    for k in range(3):
        same[:, k * inner : (k + 1) * inner] = diag
    for t in range(9):
        place = t * group_ch + sub % group_ch
        pick[t * inner : (t + 1) * inner, :] = jnp.where(lane == place, 1.0, 0.0).astype(BF)
    copies[1].wait()
    w3t[...] = targets[0][...].T
    for copy in copies[2:]:
        copy.wait()


def edges_kernel(
    x_ref, c_ref, col_odd, col_even, w1_ref, s1_ref, b1_ref, strip, odd_ref, even_ref, *, rows, cols
):
    col_is_odd = lax.axis_index("col") % 2 == 1
    row_is_odd = lax.axis_index("row") % 2
    chans, inner = w1_ref.shape
    wide = cols + STRIP
    gap = jnp.zeros((STRIP - 2 * EDGE, chans), F32)
    for r in range(2 * rows):
        a, b = col_even[r].astype(F32), col_odd[r].astype(F32)
        high, low = jnp.where(col_is_odd, b, a), jnp.where(col_is_odd, a, b)
        strip[r] = jnp.concatenate([high, gap, low], axis=0).astype(BF)
    behind = [v for r in (1, rows - 2) for v in (x_ref[r], strip[r])]
    act, _ = reduce_act(jnp.concatenate(behind, axis=0), w1_ref[...], s1_ref[...], b1_ref[...])
    col_ok = column_mask(wide, cols, inner)
    act_low, act_high = act[0:wide] * col_ok, act[wide:] * col_ok
    for ref, sends_high in ((even_ref, row_is_odd == 0), (odd_ref, row_is_odd == 1)):
        at = jnp.where(sends_high, rows - 1, 0)
        ref[0:cols, :] = x_ref[at]
        ref[cols:wide, :] = strip[at]
        ref[wide : wide + cols, :] = c_ref[at]
        ref[wide + cols : 2 * wide, :] = strip[rows + at]
        sent = jnp.where(sends_high, act_high, act_low)
        ref[2 * wide :, 0:inner] = sent[0 : wide // 2].astype(BF)
        ref[2 * wide :, inner:] = sent[wide // 2 :].astype(BF)


def inner_kernel(
    x_ref, c_ref, strip_ref, w1_ref, s1_ref, b1_ref, s2_ref, b2_ref, s3_ref, b3_ref, w2, w2t, w3_ref, w3t_ref,
    acts, gcat, d1, back, g1, gw3_ref, full_ref, gw1_ref, xt, xs, cs,
    *, rows, cols, chans, inner,
):
    wide = cols + STRIP
    step = 2
    col_ok = column_mask(wide, cols, inner)
    s1, b1, s2, b2, s3, b3 = (v[...] for v in (s1_ref, b1_ref, s2_ref, b2_ref, s3_ref, b3_ref))
    w1 = w1_ref[...]
    for r in range(rows):
        xs[r, 0:cols, :] = x_ref[r]
        xs[r, cols:wide, :] = strip_ref[r]
        cs[r, 0:cols, :] = c_ref[r]
        cs[r, cols:wide, :] = strip_ref[rows + r]
    for r0 in range(0, rows, step):
        act, sg = reduce_act(xs[r0 : r0 + step].reshape(step * wide, chans), w1, s1, b1)
        slope = (sg + act * (1.0 - sg)) * s1
        for k in range(step):
            r = r0 + k
            spread(acts, r, act[k * wide : (k + 1) * wide] * col_ok)
            d1[r * cols : (r + 1) * cols, :] = slope[k * wide : k * wide + cols]
    rest = (s2, b2, w3_ref[...], w3t_ref[...], s3, b3)
    gw3 = jnp.zeros((inner, chans), F32)
    convs = conv_pairs(lambda r: acts[r], range(0, rows - 2, step), w2)
    for p0 in range(1, rows - 1, step):
        conv = jnp.concatenate(convs[p0 - 1 : p0 - 1 + step], axis=0)
        skip = xs[p0 : p0 + step].reshape(step * wide, chans)
        ct = cs[p0 : p0 + step].reshape(step * wide, chans)
        a2, grad3, back3, grad2 = through(conv, skip, ct, *rest)
        for k in range(step):
            spread(gcat, p0 - 1 + k, grad2[k * wide : (k + 1) * wide] * col_ok)
            back[(p0 - 1 + k) * cols : (p0 + k) * cols, :] = back3[k * wide : k * wide + cols]
        own = [slice(k * wide, k * wide + cols) for k in range(step)]
        gw3 = gw3 + dot(
            jnp.concatenate([a2[at] for at in own], axis=0).T, jnp.concatenate([grad3[at] for at in own], axis=0)
        )
    gw3_ref[...] = gw3
    n = (rows - 2) * cols
    own_gt = gcat[:, 0:cols, inner : 2 * inner].reshape(n, inner).T
    for dh in range(3):
        full_ref[dh] = dot(own_gt, acts[dh : dh + rows - 2, 0:cols, :].reshape(n, 3 * inner))
    gw1t = jnp.zeros((inner, chans), F32)
    convs = conv_pairs(lambda r: gcat[r, 0:cols, :], range(0, rows - 4, step), w2t)
    for p0 in range(2, rows - 2, step):
        conv = jnp.concatenate(convs[p0 - 2 : p0 - 2 + step], axis=0)
        g = (conv * d1[p0 * cols : (p0 + step) * cols, :]).astype(BF)
        g1[(p0 - 2) * cols : (p0 - 2 + step) * cols, :] = g
        gw1t = gw1t + dot(g.T, x_ref[p0 : p0 + step].reshape(step * cols, chans))
    gw1_ref[...] = gw1t.T
    for k, p in enumerate((0, 1, rows - 2, rows - 1)):
        xt[:, k * cols : (k + 1) * cols] = x_ref[p].T


def rim_kernel(
    x_ref, c_ref, strip_ref, row_even, row_odd, w1_ref, s1_ref, b1_ref, s2_ref, b2_ref, s3_ref, b3_ref, w2, w2t, w3_ref, w3t_ref,
    acts, gcat, d1, gw3_ref, full_ref, gw1_ref, xt, same, pick,
    share_ref, g1, back, hacts, hgrad, far_ref,
    *, rows, cols, chans, inner, group_ch,
):
    wide = cols + STRIP
    col_ok = column_mask(wide, cols, inner)
    s1, b1, s2, b2, s3, b3 = (v[...] for v in (s1_ref, b1_ref, s2_ref, b2_ref, s3_ref, b3_ref))
    row_is_odd = lax.axis_index("row") % 2
    has_low, has_high = has_neighbours("row")

    @pl.when(row_is_odd == 0)
    def _():
        far_ref[0] = row_odd[...]
        far_ref[1] = row_even[...]

    @pl.when(row_is_odd == 1)
    def _():
        far_ref[0] = row_even[...]
        far_ref[1] = row_odd[...]

    def wider(ref, r, base):
        return jnp.concatenate([ref[r], strip_ref[base + r]], axis=0)

    near = [far_ref[i, 0:wide, :] for i in range(2)]
    near_cot = [far_ref[i, wide : 2 * wide, :] for i in range(2)]
    act, _ = reduce_act(jnp.concatenate(near, axis=0), w1_ref[...], s1, b1)
    for k, has in ((0, has_low), (1, has_high)):
        sent = far_ref[k, 2 * wide :, :].astype(F32)
        spread(hacts, 3 * k, jnp.concatenate([sent[:, 0:inner], sent[:, inner:]], axis=0) * has)
        spread(hacts, 1 + k, act[k * wide : (k + 1) * wide] * (col_ok * has))
    def act_row(r):
        return hacts[r] if r < 2 else acts[r - 2] if r < rows + 2 else hacts[r - rows]

    conv = jnp.concatenate(conv_pairs(act_row, (0, rows), w2), axis=0)
    skip = jnp.concatenate([near[0], wider(x_ref, 0, 0), wider(x_ref, rows - 1, 0), near[1]], axis=0)
    ct = jnp.concatenate([near_cot[0], wider(c_ref, 0, rows), wider(c_ref, rows - 1, rows), near_cot[1]], axis=0)
    a2, grad3, back3, grad2 = through(conv, skip, ct, s2, b2, w3_ref[...], w3t_ref[...], s3, b3)
    for k in range(4):
        g = grad2[k * wide : (k + 1) * wide] * col_ok
        spread(hgrad, k, g * has_low if k == 0 else g * has_high if k == 3 else g)
    own = [slice(k * wide, k * wide + cols) for k in (1, 2)]
    for k in range(2):
        back[k * cols : (k + 1) * cols, :] = back3[own[k]]
    def grad_row(q):
        return (hgrad[q] if q < 2 else gcat[q - 2] if q < rows else hgrad[q - rows + 2])[0:cols]

    outs = (0, 1, rows - 2, rows - 1)
    conv = jnp.concatenate(conv_pairs(grad_row, (0, rows - 2), w2t), axis=0)
    slope = jnp.concatenate([d1[0 : 2 * cols, :], d1[(rows - 2) * cols :, :]], axis=0)
    g = (conv * slope).astype(BF)
    g1[...] = g
    own_gt = jnp.concatenate([hgrad[k, 0:cols, inner : 2 * inner] for k in (1, 2)], axis=0).T
    around = jnp.concatenate(
        [jnp.concatenate([act_row(q + dh)[0:cols] for q in (1, rows)], axis=0) for dh in range(3)], axis=1
    )
    full = dot(own_gt, around)
    full = jnp.concatenate(
        [(full_ref[dh] + full[:, dh * 3 * inner : (dh + 1) * 3 * inner]) * same[...] for dh in range(3)], axis=1
    )
    compact = dot(full.astype(BF), pick[...])
    gw2 = compact.T

    gw1 = gw1_ref[...] + dot(xt[...], g)
    gw3 = gw3_ref[...] + dot(
        jnp.concatenate([a2[at] for at in own], axis=0).T, jnp.concatenate([grad3[at] for at in own], axis=0)
    )
    n_dp = share_ref.shape[1]
    one, three = chans // n_dp, inner // n_dp
    parity = parity_of_place()
    at = (parity, 1 - parity)
    for h in range(n_dp):
        slot = h ^ lax.axis_index("dp")
        share_ref[at[0], slot, 0:one, :] = gw1[h * one : (h + 1) * one]
        for k in range(chans // inner):
            share_ref[at[1], slot, k * three : (k + 1) * three, :] = gw3[
                h * three : (h + 1) * three, k * inner : (k + 1) * inner
            ]
        group = gw2 if h == 0 else pltpu.roll(gw2, inner - h * three, 1)
        share_ref[at[0], slot, one : one + GROUP_ROWS, :] = group[0:GROUP_ROWS]
        share_ref[at[1], slot, one : one + GROUP_ROWS, :] = group[GROUP_ROWS : 2 * GROUP_ROWS]


def out_kernel(g1_in, g1_rim, back_in, back_rim, w1_ref, out_ref, *, rows, cols, chans):
    w1t = w1_ref[...].T
    for p in range(rows):
        if 2 <= p < rows - 2:
            g = g1_in[(p - 2) * cols : (p - 1) * cols, :]
        else:
            k = p if p < 2 else p - rows + 4
            g = g1_rim[k * cols : (k + 1) * cols, :]
        if 1 <= p < rows - 1:
            b = back_in[(p - 1) * cols : p * cols, :]
        else:
            b = back_rim[0:cols, :] if p == 0 else back_rim[cols:, :]
        out_ref[p] = (dot(g, w1t) + b).astype(BF)


def last_kernel(
    a_ref, b_ref, r_out, g_out, e_out, r_ref, g_ref, e_ref, sems, *, scale, one, three, chans, inner, group_ch
):
    other_first = parity_of_place() == 1
    first = jnp.where(other_first, b_ref[...], a_ref[...]) * scale
    second = jnp.where(other_first, a_ref[...], b_ref[...]) * scale
    r_ref[...] = first[0:one]
    for k in range(chans // inner):
        e_ref[:, k * inner : (k + 1) * inner] = second[k * three : (k + 1) * three]
    for t in range(9):
        at = t * group_ch
        part = first[one + at : one + at + group_ch] if at < GROUP_ROWS else second[
            one + at - GROUP_ROWS : one + at - GROUP_ROWS + group_ch]
        g_ref[t // 3, t % 3] = part[:, 0:three]
    copies = [
        pltpu.make_async_copy(src, dst, sems.at[i])
        for i, (src, dst) in enumerate(((r_ref, r_out), (e_ref, e_out), (g_ref, g_out)))
    ]
    for copy in copies:
        copy.start()
    for copy in copies:
        copy.wait()


def crossed(value, move, other_move):
    names = ("dp", "row", "col")
    sizes = [lax.axis_size(a) for a in names]
    perm = []
    for at in itertools.product(*(range(n) for n in sizes)):
        axis, bit = other_move if sum(i.bit_count() for i in at) % 2 else move
        to = list(at)
        to[names.index(axis)] ^= bit
        to[1] ^= 1
        perm.append(tuple(functools.reduce(lambda v, k: v * sizes[k] + p[k], range(3), 0) for p in (at, to)))
    return lax.ppermute(value, names, perm)


def body(
    features, reduce_weight, scale_one, shift_one, group_weight, scale_two, shift_two, expand_weight, scale_three,
    shift_three, cotangent,
):
    _, rows, cols, chans = features.shape
    inner = reduce_weight.shape[1]
    group_ch = group_weight.shape[2]
    x, c = features[0], cotangent[0]
    n_dp, n_row, n_col = (lax.axis_size(a) for a in ("dp", "row", "col"))

    wide = cols + STRIP
    one, three = chans // n_dp, inner // n_dp
    half_rows = one + GROUP_ROWS
    vmem = pl.BlockSpec(memory_space=pltpu.VMEM)
    params = pltpu.CompilerParams(vmem_limit_bytes=8 << 20)
    sizes = dict(rows=rows, cols=cols, chans=chans)
    shape = jax.ShapeDtypeStruct

    x, c = (pltpu.with_memory_space_constraint(v, pltpu.HBM) for v in (x, c))
    to_odd, to_even = pl.pallas_call(
        functools.partial(cut_kernel, rows=rows, cols=cols),
        out_shape=(shape((2 * rows, EDGE, chans), BF),) * 2,
        in_specs=[pl.BlockSpec(memory_space=pltpu.HBM)] * 2,
        out_specs=(vmem,) * 2,
        scratch_shapes=[pltpu.VMEM((2 * rows, 8, chans), BF)] * 2 + [pltpu.SemaphoreType.DMA((4,))],
        compiler_params=params,
        name="cut",
    )(x, c)
    col_even, col_odd = swap_edges(to_even, to_odd, "col")
    sources = (
        expand_weight, reduce_weight, x, c, scale_one[None], shift_one[None], scale_two[None], shift_two[None],
        scale_three[None], shift_three[None],
    )
    w3, w1, x, c, *vecs, w2, w2t, w3t, same, pick = pl.pallas_call(
        functools.partial(load_kernel, inner=inner, group_ch=group_ch),
        out_shape=tuple(shape(v.shape, v.dtype) for v in sources)
        + (shape((12 * inner, 2 * inner), BF), shape((12 * inner, 2 * inner), BF), shape((chans, inner), BF))
        + (shape((inner, 3 * inner), F32), shape((9 * inner, inner), BF)),
        in_specs=[pl.BlockSpec(memory_space=pltpu.HBM)] * 11,
        out_specs=(vmem,) * 15,
        scratch_shapes=[pltpu.VMEM(group_weight.shape, BF), pltpu.SemaphoreType.DMA((11,))],
        compiler_params=params,
        name="load",
    )(*(pltpu.with_memory_space_constraint(v, pltpu.HBM) for v in (group_weight, *sources)))
    shared = (w1, *vecs, w2, w2t, w3, w3t)
    col_odd, col_even, shared, x, c = lax.optimization_barrier((col_odd, col_even, shared, x, c))
    w1, *vecs = shared[:7]
    message = 2 * wide + wide * inner // chans
    strip, to_odd, to_even = pl.pallas_call(
        functools.partial(edges_kernel, rows=rows, cols=cols),
        out_shape=(shape((2 * rows, STRIP, chans), BF),) + (shape((message, chans), BF),) * 2,
        in_specs=[vmem] * 7,
        out_specs=(vmem,) * 3,
        compiler_params=params,
        name="edges",
    )(x, c, col_odd, col_even, w1, *vecs[:2])
    row_even, row_odd = swap_edges(to_even, to_odd, "row")
    acts, gcat, d1, back_in, g1_in, gw3, full, gw1, xt = pl.pallas_call(
        functools.partial(inner_kernel, inner=inner, **sizes),
        out_shape=(
            shape((rows, wide, 3 * inner), BF),
            shape((rows - 2, wide, 3 * inner), BF),
            shape((rows * cols, inner), F32),
            shape(((rows - 2) * cols, chans), F32),
            shape(((rows - 4) * cols, inner), BF),
            shape((inner, chans), F32),
            shape((3, inner, 3 * inner), F32),
            shape((chans, inner), F32),
            shape((chans, 4 * cols), BF),
        ),
        in_specs=[vmem] * 14,
        out_specs=(vmem,) * 9,
        scratch_shapes=[pltpu.VMEM((rows, wide, chans), BF), pltpu.VMEM((rows, wide, chans), BF)],
        compiler_params=params,
        name="inner",
    )(x, c, strip, *shared)
    shares, g1_rim, back_rim = pl.pallas_call(
        functools.partial(rim_kernel, inner=inner, group_ch=group_ch, **sizes),
        out_shape=(
            shape((2, n_dp, half_rows, inner), F32),
            shape((4 * cols, inner), BF),
            shape((2 * cols, chans), F32),
        ),
        in_specs=[vmem] * 25,
        out_specs=(vmem,) * 3,
        scratch_shapes=[pltpu.VMEM((4, wide, 3 * inner), BF)] * 2 + [pltpu.VMEM((2, message, chans), BF)],
        compiler_params=params,
        name="rim",
    )(x, c, strip, row_even, row_odd, *shared, acts, gcat, d1, gw3, full, gw1, xt, same, pick)
    near = [(i, i ^ 1) for i in range(n_row)]
    shares = (shares[0] + lax.ppermute(shares[1], "row", near)).astype(BF)
    g1_rim, shares = lax.optimization_barrier((g1_rim, shares))
    input_grad = pl.pallas_call(
        functools.partial(out_kernel, **sizes),
        out_shape=shape((rows, cols, chans), BF),
        in_specs=[vmem] * 5,
        out_specs=vmem,
        compiler_params=params,
        name="out",
    )(g1_in, g1_rim, back_in, back_rim, w1)
    held = n_dp
    while held > 1:
        held //= 2
        other = crossed(shares[held:], ("dp", held), ("dp", held))
        shares = (shares[:held].astype(F32) + other.astype(F32)).astype(BF)
    total = shares[0]
    steps = [("row", 1 << k) for k in range(1, n_row.bit_length() - 1)]
    steps += [("col", 1 << k) for k in reversed(range(n_col.bit_length() - 1))]
    for i, step in enumerate(steps):
        other = crossed(total, step, steps[(i + 1) % len(steps)])
        if i == 0:
            input_grad, other = lax.optimization_barrier((input_grad, other))
        summed = total.astype(F32) + other.astype(F32)
        total = summed.astype(BF)
    pixels = rows * cols * n_dp * n_row * n_col
    reduce_grad, group_grad, expand_grad = pl.pallas_call(
        functools.partial(
            last_kernel, scale=pixels**-0.5, one=one, three=three, chans=chans, inner=inner, group_ch=group_ch
        ),
        out_shape=(
            jax.ShapeDtypeStruct((one, inner), F32),
            jax.ShapeDtypeStruct((3, 3, group_ch, three), F32),
            jax.ShapeDtypeStruct((three, chans), F32),
        ),
        in_specs=[vmem, vmem],
        out_specs=(pl.BlockSpec(memory_space=pl.ANY),) * 3,
        scratch_shapes=[
            pltpu.VMEM((one, inner), F32),
            pltpu.VMEM((3, 3, group_ch, three), F32),
            pltpu.VMEM((three, chans), F32),
            pltpu.SemaphoreType.DMA((3,)),
        ],
        compiler_params=pltpu.CompilerParams(vmem_limit_bytes=2 << 20),
        name="last",
    )(summed, lax.ppermute(summed, "row", near))
    return input_grad[None], reduce_grad, jnp.transpose(group_grad, (3, 0, 1, 2)), expand_grad


def solution(mesh):
    image = P("dp", "row", "col", None)
    return jax.shard_map(
        body,
        mesh=mesh,
        in_specs=(image,) + (P(),) * 9 + (image,),
        out_specs=(image, P("dp", None), P("dp", None, None, None), P("dp", None)),
        check_vma=False,
    )
```

```python
import functools
import itertools

import jax
import jax.numpy as jnp
from jax import lax
from jax.experimental import pallas as pl
from jax.experimental.pallas import tpu as pltpu
from jax.sharding import PartitionSpec as P

BF = jnp.bfloat16
F32 = jnp.float32
EDGE = 2
STRIP = 16
GROUP_ROWS = 24


def swap_edges(to_even, to_odd, axis):
    count, bands = lax.axis_size(axis), lax.axis_size("dp")
    got_even = lax.ppermute(to_even, axis, [(i, i ^ 1) for i in range(count)])
    names = ("dp", "row", "col")
    sizes = [lax.axis_size(a) for a in names]
    which = names.index(axis)
    perm = []
    for at in itertools.product(*(range(n) for n in sizes)):
        to = list(at)
        if 0 < at[which] < count - 1:
            to[which] = ((at[which] - 1) ^ 1) + 1
        elif axis == "col":
            to[1] ^= 1
        elif bands > 1:
            to[0] ^= 1
        perm.append(tuple(functools.reduce(lambda v, k: v * sizes[k] + p[k], range(3), 0) for p in (at, to)))
    got_odd = lax.ppermute(to_odd, names, perm)
    return got_even, got_odd


def dot(a, b):
    return jnp.dot(a, b, preferred_element_type=F32)


def gate(v):
    return 0.5 + 0.5 * jnp.tanh(0.5 * v)


def parity_of_place():
    bits = 0
    for axis in ("dp", "row", "col"):
        at = lax.axis_index(axis)
        for k in range((lax.axis_size(axis) - 1).bit_length()):
            bits = bits + (at >> k)
    return bits % 2


def has_neighbours(axis):
    at = lax.axis_index(axis)
    return jnp.where(at > 0, 1.0, 0.0).astype(F32), jnp.where(at < lax.axis_size(axis) - 1, 1.0, 0.0).astype(F32)


def column_mask(wide, cols, inner):
    spot = lax.broadcasted_iota(jnp.int32, (wide, inner), 0)
    has_low, has_high = has_neighbours("col")
    return jnp.where(spot < cols, 1.0, jnp.where(spot < cols + STRIP // 2, has_high, has_low))


def spread(ref, r, v):
    wide, inner = v.shape
    ref[r, :, 0:inner] = pltpu.roll(v, 1, 0).astype(BF)
    ref[r, :, inner : 2 * inner] = v.astype(BF)
    ref[r, :, 2 * inner :] = pltpu.roll(v, wide - 1, 0).astype(BF)


def conv_pairs(row, starts, w_ref):
    left = [jnp.concatenate([row(i + j) for j in range(4)], axis=1) for i in starts]
    out = dot(jnp.concatenate(left, axis=0), w_ref[...])
    n, inner = left[0].shape[0], w_ref.shape[1] // 2
    return [out[i * n : (i + 1) * n, k * inner : (k + 1) * inner] for i in range(len(starts)) for k in range(2)]


def reduce_act(x, w1, s1, b1):
    pre = dot(x, w1) * s1 + b1
    sg = gate(pre)
    return pre * sg, sg


def through(conv, skip, ct, s2, b2, w3, w3t, s3, b3):
    pre2 = conv * s2 + b2
    sg2 = gate(pre2)
    silu2 = pre2 * sg2
    a2 = silu2.astype(BF)
    pre3 = dot(a2, w3) * s3 + b3 + skip.astype(F32)
    sg3 = gate(pre3)
    back3 = ct.astype(F32) * (sg3 + pre3 * sg3 * (1.0 - sg3))
    grad3 = (back3 * s3).astype(BF)
    grad2 = dot(grad3, w3t) * ((sg2 + silu2 * (1.0 - sg2)) * s2)
    return a2, grad3, back3, grad2


def cut_kernel(x_hbm, c_hbm, odd_ref, even_ref, low_ref, high_ref, sems, *, rows, cols):
    copies = []
    for i, src in enumerate((x_hbm, c_hbm)):
        at = slice(i * rows, (i + 1) * rows)
        copies.append(pltpu.make_async_copy(src.at[:, 0:8, :], low_ref.at[at], sems.at[2 * i]))
        copies.append(pltpu.make_async_copy(src.at[:, cols - 8 : cols, :], high_ref.at[at], sems.at[2 * i + 1]))
    for copy in copies:
        copy.start()
    is_odd = lax.axis_index("col") % 2 == 1
    for copy in copies:
        copy.wait()
    for r in range(2 * rows):
        low = low_ref[r].astype(F32)[0:EDGE]
        high = high_ref[r].astype(F32)[8 - EDGE : 8]
        even_ref[r] = jnp.where(is_odd, low, high).astype(BF)
        odd_ref[r] = jnp.where(is_odd, high, low).astype(BF)


def load_kernel(*refs, inner, group_ch):
    sources, targets, (w2, w2t, w3t, same, pick, gw_ref, sems) = refs[:11], refs[11:21], refs[21:]
    gw_hbm, sources = sources[0], sources[1:]
    copies = [pltpu.make_async_copy(gw_hbm, gw_ref, sems.at[10])]
    copies += [pltpu.make_async_copy(src, dst, sems.at[i]) for i, (src, dst) in enumerate(zip(sources, targets))]
    for copy in copies:
        copy.start()
    copies[0].wait()
    sub = lax.broadcasted_iota(jnp.int32, (inner, inner), 0)
    lane = lax.broadcasted_iota(jnp.int32, (inner, inner), 1)
    diag = jnp.where(sub // group_ch == lane // group_ch, 1.0, 0.0).astype(F32)
    for t in range(9):
        four = gw_ref[t // 3, t % 3].astype(F32)
        eight = jnp.concatenate([four, four], axis=0)
        tiled = jnp.broadcast_to(eight[None], (inner // 8, 8, inner)).reshape(inner, inner)
        dense = tiled * diag
        for ref, tap, block in ((w2, t, dense.astype(BF)), (w2t, 8 - t, dense.T.astype(BF))):
            ref[tap * inner : (tap + 1) * inner, 0:inner] = block
            ref[(tap + 3) * inner : (tap + 4) * inner, inner:] = block
    for ref in (w2, w2t):
        ref[9 * inner :, 0:inner] = jnp.zeros((3 * inner, inner), BF)
        ref[0 : 3 * inner, inner:] = jnp.zeros((3 * inner, inner), BF)
    for k in range(3):
        same[:, k * inner : (k + 1) * inner] = diag
    for t in range(9):
        place = t * group_ch + sub % group_ch
        pick[t * inner : (t + 1) * inner, :] = jnp.where(lane == place, 1.0, 0.0).astype(BF)
    copies[1].wait()
    w3t[...] = targets[0][...].T
    for copy in copies[2:]:
        copy.wait()


def edges_kernel(
    x_ref, c_ref, col_odd, col_even, w1_ref, s1_ref, b1_ref, strip, odd_ref, even_ref, *, rows, cols
):
    col_is_odd = lax.axis_index("col") % 2 == 1
    row_is_odd = lax.axis_index("row") % 2
    chans, inner = w1_ref.shape
    wide = cols + STRIP
    gap = jnp.zeros((STRIP - 2 * EDGE, chans), F32)
    for r in range(2 * rows):
        a, b = col_even[r].astype(F32), col_odd[r].astype(F32)
        high, low = jnp.where(col_is_odd, b, a), jnp.where(col_is_odd, a, b)
        strip[r] = jnp.concatenate([high, gap, low], axis=0).astype(BF)
    behind = [v for r in (1, rows - 2) for v in (x_ref[r], strip[r])]
    act, _ = reduce_act(jnp.concatenate(behind, axis=0), w1_ref[...], s1_ref[...], b1_ref[...])
    col_ok = column_mask(wide, cols, inner)
    act_low, act_high = act[0:wide] * col_ok, act[wide:] * col_ok
    for ref, sends_high in ((even_ref, row_is_odd == 0), (odd_ref, row_is_odd == 1)):
        at = jnp.where(sends_high, rows - 1, 0)
        ref[0:cols, :] = x_ref[at]
        ref[cols:wide, :] = strip[at]
        ref[wide : wide + cols, :] = c_ref[at]
        ref[wide + cols : 2 * wide, :] = strip[rows + at]
        sent = jnp.where(sends_high, act_high, act_low)
        ref[2 * wide :, 0:inner] = sent[0 : wide // 2].astype(BF)
        ref[2 * wide :, inner:] = sent[wide // 2 :].astype(BF)


def inner_kernel(
    x_ref, c_ref, strip_ref, w1_ref, s1_ref, b1_ref, s2_ref, b2_ref, s3_ref, b3_ref, w2, w2t, w3_ref, w3t_ref,
    acts, gcat, d1, back, g1, gw3_ref, full_ref, gw1_ref, xt, xs, cs,
    *, rows, cols, chans, inner,
):
    wide = cols + STRIP
    step = 2
    col_ok = column_mask(wide, cols, inner)
    s1, b1, s2, b2, s3, b3 = (v[...] for v in (s1_ref, b1_ref, s2_ref, b2_ref, s3_ref, b3_ref))
    w1 = w1_ref[...]
    for r in range(rows):
        xs[r, 0:cols, :] = x_ref[r]
        xs[r, cols:wide, :] = strip_ref[r]
        cs[r, 0:cols, :] = c_ref[r]
        cs[r, cols:wide, :] = strip_ref[rows + r]
    for r0 in range(0, rows, step):
        act, sg = reduce_act(xs[r0 : r0 + step].reshape(step * wide, chans), w1, s1, b1)
        slope = (sg + act * (1.0 - sg)) * s1
        for k in range(step):
            r = r0 + k
            spread(acts, r, act[k * wide : (k + 1) * wide] * col_ok)
            d1[r * cols : (r + 1) * cols, :] = slope[k * wide : k * wide + cols]
    rest = (s2, b2, w3_ref[...], w3t_ref[...], s3, b3)
    gw3 = jnp.zeros((inner, chans), F32)
    convs = conv_pairs(lambda r: acts[r], range(0, rows - 2, step), w2)
    for p0 in range(1, rows - 1, step):
        conv = jnp.concatenate(convs[p0 - 1 : p0 - 1 + step], axis=0)
        skip = xs[p0 : p0 + step].reshape(step * wide, chans)
        ct = cs[p0 : p0 + step].reshape(step * wide, chans)
        a2, grad3, back3, grad2 = through(conv, skip, ct, *rest)
        for k in range(step):
            spread(gcat, p0 - 1 + k, grad2[k * wide : (k + 1) * wide] * col_ok)
            back[(p0 - 1 + k) * cols : (p0 + k) * cols, :] = back3[k * wide : k * wide + cols]
        own = [slice(k * wide, k * wide + cols) for k in range(step)]
        gw3 = gw3 + dot(
            jnp.concatenate([a2[at] for at in own], axis=0).T, jnp.concatenate([grad3[at] for at in own], axis=0)
        )
    gw3_ref[...] = gw3
    n = (rows - 2) * cols
    own_gt = gcat[:, 0:cols, inner : 2 * inner].reshape(n, inner).T
    for dh in range(3):
        full_ref[dh] = dot(own_gt, acts[dh : dh + rows - 2, 0:cols, :].reshape(n, 3 * inner))
    gw1t = jnp.zeros((inner, chans), F32)
    convs = conv_pairs(lambda r: gcat[r, 0:cols, :], range(0, rows - 4, step), w2t)
    for p0 in range(2, rows - 2, step):
        conv = jnp.concatenate(convs[p0 - 2 : p0 - 2 + step], axis=0)
        g = (conv * d1[p0 * cols : (p0 + step) * cols, :]).astype(BF)
        g1[(p0 - 2) * cols : (p0 - 2 + step) * cols, :] = g
        gw1t = gw1t + dot(g.T, x_ref[p0 : p0 + step].reshape(step * cols, chans))
    gw1_ref[...] = gw1t.T
    for k, p in enumerate((0, 1, rows - 2, rows - 1)):
        xt[:, k * cols : (k + 1) * cols] = x_ref[p].T


def rim_kernel(
    x_ref, c_ref, strip_ref, row_even, row_odd, w1_ref, s1_ref, b1_ref, s2_ref, b2_ref, s3_ref, b3_ref, w2, w2t, w3_ref, w3t_ref,
    acts, gcat, d1, gw3_ref, full_ref, gw1_ref, xt, same, pick,
    share_ref, g1, back, hacts, hgrad, far_ref,
    *, rows, cols, chans, inner, group_ch,
):
    wide = cols + STRIP
    col_ok = column_mask(wide, cols, inner)
    s1, b1, s2, b2, s3, b3 = (v[...] for v in (s1_ref, b1_ref, s2_ref, b2_ref, s3_ref, b3_ref))
    row_is_odd = lax.axis_index("row") % 2
    has_low, has_high = has_neighbours("row")

    @pl.when(row_is_odd == 0)
    def _():
        far_ref[0] = row_odd[...]
        far_ref[1] = row_even[...]

    @pl.when(row_is_odd == 1)
    def _():
        far_ref[0] = row_even[...]
        far_ref[1] = row_odd[...]

    def wider(ref, r, base):
        return jnp.concatenate([ref[r], strip_ref[base + r]], axis=0)

    near = [far_ref[i, 0:wide, :] for i in range(2)]
    near_cot = [far_ref[i, wide : 2 * wide, :] for i in range(2)]
    act, _ = reduce_act(jnp.concatenate(near, axis=0), w1_ref[...], s1, b1)
    for k, has in ((0, has_low), (1, has_high)):
        sent = far_ref[k, 2 * wide :, :].astype(F32)
        spread(hacts, 3 * k, jnp.concatenate([sent[:, 0:inner], sent[:, inner:]], axis=0) * has)
        spread(hacts, 1 + k, act[k * wide : (k + 1) * wide] * (col_ok * has))
    def act_row(r):
        return hacts[r] if r < 2 else acts[r - 2] if r < rows + 2 else hacts[r - rows]

    conv = jnp.concatenate(conv_pairs(act_row, (0, rows), w2), axis=0)
    skip = jnp.concatenate([near[0], wider(x_ref, 0, 0), wider(x_ref, rows - 1, 0), near[1]], axis=0)
    ct = jnp.concatenate([near_cot[0], wider(c_ref, 0, rows), wider(c_ref, rows - 1, rows), near_cot[1]], axis=0)
    a2, grad3, back3, grad2 = through(conv, skip, ct, s2, b2, w3_ref[...], w3t_ref[...], s3, b3)
    for k in range(4):
        g = grad2[k * wide : (k + 1) * wide] * col_ok
        spread(hgrad, k, g * has_low if k == 0 else g * has_high if k == 3 else g)
    own = [slice(k * wide, k * wide + cols) for k in (1, 2)]
    for k in range(2):
        back[k * cols : (k + 1) * cols, :] = back3[own[k]]
    def grad_row(q):
        return (hgrad[q] if q < 2 else gcat[q - 2] if q < rows else hgrad[q - rows + 2])[0:cols]

    outs = (0, 1, rows - 2, rows - 1)
    conv = jnp.concatenate(conv_pairs(grad_row, (0, rows - 2), w2t), axis=0)
    slope = jnp.concatenate([d1[0 : 2 * cols, :], d1[(rows - 2) * cols :, :]], axis=0)
    g = (conv * slope).astype(BF)
    g1[...] = g
    own_gt = jnp.concatenate([hgrad[k, 0:cols, inner : 2 * inner] for k in (1, 2)], axis=0).T
    around = jnp.concatenate(
        [jnp.concatenate([act_row(q + dh)[0:cols] for q in (1, rows)], axis=0) for dh in range(3)], axis=1
    )
    full = dot(own_gt, around)
    full = jnp.concatenate(
        [(full_ref[dh] + full[:, dh * 3 * inner : (dh + 1) * 3 * inner]) * same[...] for dh in range(3)], axis=1
    )
    compact = dot(full.astype(BF), pick[...])
    gw2 = compact.T

    gw1 = gw1_ref[...] + dot(xt[...], g)
    gw3 = gw3_ref[...] + dot(
        jnp.concatenate([a2[at] for at in own], axis=0).T, jnp.concatenate([grad3[at] for at in own], axis=0)
    )
    n_dp = share_ref.shape[1]
    one, three = chans // n_dp, inner // n_dp
    parity = parity_of_place()
    at = (parity, 1 - parity)
    for h in range(n_dp):
        slot = h ^ lax.axis_index("dp")
        share_ref[at[0], slot, 0:one, :] = gw1[h * one : (h + 1) * one]
        for k in range(chans // inner):
            share_ref[at[1], slot, k * three : (k + 1) * three, :] = gw3[
                h * three : (h + 1) * three, k * inner : (k + 1) * inner
            ]
        group = gw2 if h == 0 else pltpu.roll(gw2, inner - h * three, 1)
        share_ref[at[0], slot, one : one + GROUP_ROWS, :] = group[0:GROUP_ROWS]
        share_ref[at[1], slot, one : one + GROUP_ROWS, :] = group[GROUP_ROWS : 2 * GROUP_ROWS]


def out_kernel(g1_in, g1_rim, back_in, back_rim, w1_ref, out_ref, *, rows, cols, chans):
    w1t = w1_ref[...].T
    for p in range(rows):
        if 2 <= p < rows - 2:
            g = g1_in[(p - 2) * cols : (p - 1) * cols, :]
        else:
            k = p if p < 2 else p - rows + 4
            g = g1_rim[k * cols : (k + 1) * cols, :]
        if 1 <= p < rows - 1:
            b = back_in[(p - 1) * cols : p * cols, :]
        else:
            b = back_rim[0:cols, :] if p == 0 else back_rim[cols:, :]
        out_ref[p] = (dot(g, w1t) + b).astype(BF)


def last_kernel(
    a_ref, b_ref, r_out, g_out, e_out, r_ref, g_ref, e_ref, sems, *, scale, one, three, chans, inner, group_ch
):
    other_first = parity_of_place() == 1
    copies = [
        pltpu.make_async_copy(src, dst, sems.at[i])
        for i, (src, dst) in enumerate(((r_ref, r_out), (e_ref, e_out), (g_ref, g_out)))
    ]
    first = jnp.where(other_first, b_ref[...], a_ref[...]) * scale
    r_ref[...] = first[0:one]
    copies[0].start()
    second = jnp.where(other_first, a_ref[...], b_ref[...]) * scale
    for k in range(chans // inner):
        e_ref[:, k * inner : (k + 1) * inner] = second[k * three : (k + 1) * three]
    copies[1].start()
    for t in range(9):
        at = t * group_ch
        part = first[one + at : one + at + group_ch] if at < GROUP_ROWS else second[
            one + at - GROUP_ROWS : one + at - GROUP_ROWS + group_ch]
        g_ref[t // 3, t % 3] = part[:, 0:three]
    copies[2].start()
    for copy in copies:
        copy.wait()


def crossed(value, move, other_move):
    names = ("dp", "row", "col")
    sizes = [lax.axis_size(a) for a in names]
    perm = []
    for at in itertools.product(*(range(n) for n in sizes)):
        axis, bit = other_move if sum(i.bit_count() for i in at) % 2 else move
        to = list(at)
        to[names.index(axis)] ^= bit
        to[1] ^= 1
        perm.append(tuple(functools.reduce(lambda v, k: v * sizes[k] + p[k], range(3), 0) for p in (at, to)))
    return lax.ppermute(value, names, perm)


def body(
    features, reduce_weight, scale_one, shift_one, group_weight, scale_two, shift_two, expand_weight, scale_three,
    shift_three, cotangent,
):
    _, rows, cols, chans = features.shape
    inner = reduce_weight.shape[1]
    group_ch = group_weight.shape[2]
    x, c = features[0], cotangent[0]
    n_dp, n_row, n_col = (lax.axis_size(a) for a in ("dp", "row", "col"))

    wide = cols + STRIP
    one, three = chans // n_dp, inner // n_dp
    half_rows = one + GROUP_ROWS
    vmem = pl.BlockSpec(memory_space=pltpu.VMEM)
    params = pltpu.CompilerParams(vmem_limit_bytes=8 << 20)
    sizes = dict(rows=rows, cols=cols, chans=chans)
    shape = jax.ShapeDtypeStruct

    x, c = (pltpu.with_memory_space_constraint(v, pltpu.HBM) for v in (x, c))
    to_odd, to_even = pl.pallas_call(
        functools.partial(cut_kernel, rows=rows, cols=cols),
        out_shape=(shape((2 * rows, EDGE, chans), BF),) * 2,
        in_specs=[pl.BlockSpec(memory_space=pltpu.HBM)] * 2,
        out_specs=(vmem,) * 2,
        scratch_shapes=[pltpu.VMEM((2 * rows, 8, chans), BF)] * 2 + [pltpu.SemaphoreType.DMA((4,))],
        compiler_params=params,
        name="cut",
    )(x, c)
    col_even, col_odd = swap_edges(to_even, to_odd, "col")
    sources = (
        expand_weight, reduce_weight, x, c, scale_one[None], shift_one[None], scale_two[None], shift_two[None],
        scale_three[None], shift_three[None],
    )
    w3, w1, x, c, *vecs, w2, w2t, w3t, same, pick = pl.pallas_call(
        functools.partial(load_kernel, inner=inner, group_ch=group_ch),
        out_shape=tuple(shape(v.shape, v.dtype) for v in sources)
        + (shape((12 * inner, 2 * inner), BF), shape((12 * inner, 2 * inner), BF), shape((chans, inner), BF))
        + (shape((inner, 3 * inner), F32), shape((9 * inner, inner), BF)),
        in_specs=[pl.BlockSpec(memory_space=pltpu.HBM)] * 11,
        out_specs=(vmem,) * 15,
        scratch_shapes=[pltpu.VMEM(group_weight.shape, BF), pltpu.SemaphoreType.DMA((11,))],
        compiler_params=params,
        name="load",
    )(*(pltpu.with_memory_space_constraint(v, pltpu.HBM) for v in (group_weight, *sources)))
    shared = (w1, *vecs, w2, w2t, w3, w3t)
    col_odd, col_even, shared, x, c = lax.optimization_barrier((col_odd, col_even, shared, x, c))
    w1, *vecs = shared[:7]
    message = 2 * wide + wide * inner // chans
    strip, to_odd, to_even = pl.pallas_call(
        functools.partial(edges_kernel, rows=rows, cols=cols),
        out_shape=(shape((2 * rows, STRIP, chans), BF),) + (shape((message, chans), BF),) * 2,
        in_specs=[vmem] * 7,
        out_specs=(vmem,) * 3,
        compiler_params=params,
        name="edges",
    )(x, c, col_odd, col_even, w1, *vecs[:2])
    row_even, row_odd = swap_edges(to_even, to_odd, "row")
    acts, gcat, d1, back_in, g1_in, gw3, full, gw1, xt = pl.pallas_call(
        functools.partial(inner_kernel, inner=inner, **sizes),
        out_shape=(
            shape((rows, wide, 3 * inner), BF),
            shape((rows - 2, wide, 3 * inner), BF),
            shape((rows * cols, inner), F32),
            shape(((rows - 2) * cols, chans), F32),
            shape(((rows - 4) * cols, inner), BF),
            shape((inner, chans), F32),
            shape((3, inner, 3 * inner), F32),
            shape((chans, inner), F32),
            shape((chans, 4 * cols), BF),
        ),
        in_specs=[vmem] * 14,
        out_specs=(vmem,) * 9,
        scratch_shapes=[pltpu.VMEM((rows, wide, chans), BF), pltpu.VMEM((rows, wide, chans), BF)],
        compiler_params=params,
        name="inner",
    )(x, c, strip, *shared)
    shares, g1_rim, back_rim = pl.pallas_call(
        functools.partial(rim_kernel, inner=inner, group_ch=group_ch, **sizes),
        out_shape=(
            shape((2, n_dp, half_rows, inner), F32),
            shape((4 * cols, inner), BF),
            shape((2 * cols, chans), F32),
        ),
        in_specs=[vmem] * 25,
        out_specs=(vmem,) * 3,
        scratch_shapes=[pltpu.VMEM((4, wide, 3 * inner), BF)] * 2 + [pltpu.VMEM((2, message, chans), BF)],
        compiler_params=params,
        name="rim",
    )(x, c, strip, row_even, row_odd, *shared, acts, gcat, d1, gw3, full, gw1, xt, same, pick)
    near = [(i, i ^ 1) for i in range(n_row)]
    shares = (shares[0] + lax.ppermute(shares[1], "row", near)).astype(BF)
    g1_rim, shares = lax.optimization_barrier((g1_rim, shares))
    input_grad = pl.pallas_call(
        functools.partial(out_kernel, **sizes),
        out_shape=shape((rows, cols, chans), BF),
        in_specs=[vmem] * 5,
        out_specs=vmem,
        compiler_params=params,
        name="out",
    )(g1_in, g1_rim, back_in, back_rim, w1)
    held = n_dp
    while held > 1:
        held //= 2
        other = crossed(shares[held:], ("dp", held), ("dp", held))
        shares = (shares[:held].astype(F32) + other.astype(F32)).astype(BF)
    total = shares[0]
    steps = [("row", 1 << k) for k in range(1, n_row.bit_length() - 1)]
    steps += [("col", 1 << k) for k in reversed(range(n_col.bit_length() - 1))]
    for i, step in enumerate(steps):
        other = crossed(total, step, steps[(i + 1) % len(steps)])
        if i == 0:
            input_grad, other = lax.optimization_barrier((input_grad, other))
        summed = total.astype(F32) + other.astype(F32)
        total = summed.astype(BF)
    pixels = rows * cols * n_dp * n_row * n_col
    reduce_grad, group_grad, expand_grad = pl.pallas_call(
        functools.partial(
            last_kernel, scale=pixels**-0.5, one=one, three=three, chans=chans, inner=inner, group_ch=group_ch
        ),
        out_shape=(
            jax.ShapeDtypeStruct((one, inner), F32),
            jax.ShapeDtypeStruct((3, 3, group_ch, three), F32),
            jax.ShapeDtypeStruct((three, chans), F32),
        ),
        in_specs=[vmem, vmem],
        out_specs=(pl.BlockSpec(memory_space=pl.ANY),) * 3,
        scratch_shapes=[
            pltpu.VMEM((one, inner), F32),
            pltpu.VMEM((3, 3, group_ch, three), F32),
            pltpu.VMEM((three, chans), F32),
            pltpu.SemaphoreType.DMA((3,)),
        ],
        compiler_params=pltpu.CompilerParams(vmem_limit_bytes=2 << 20),
        name="last",
    )(summed, lax.ppermute(summed, "row", near))
    return input_grad[None], reduce_grad, jnp.transpose(group_grad, (3, 0, 1, 2)), expand_grad


def solution(mesh):
    image = P("dp", "row", "col", None)
    return jax.shard_map(
        body,
        mesh=mesh,
        in_specs=(image,) + (P(),) * 9 + (image,),
        out_specs=(image, P("dp", None), P("dp", None, None, None), P("dp", None)),
        check_vma=False,
    )
```

```python
import functools
import itertools

import jax
import jax.numpy as jnp
from jax import lax
from jax.experimental import pallas as pl
from jax.experimental.pallas import tpu as pltpu
from jax.sharding import PartitionSpec as P

BF = jnp.bfloat16
F32 = jnp.float32
EDGE = 2
STRIP = 16
GROUP_ROWS = 16


def swap_edges(to_even, to_odd, axis):
    count, bands = lax.axis_size(axis), lax.axis_size("dp")
    got_even = lax.ppermute(to_even, axis, [(i, i ^ 1) for i in range(count)])
    names = ("dp", "row", "col")
    sizes = [lax.axis_size(a) for a in names]
    which = names.index(axis)
    perm = []
    for at in itertools.product(*(range(n) for n in sizes)):
        to = list(at)
        if 0 < at[which] < count - 1:
            to[which] = ((at[which] - 1) ^ 1) + 1
        elif axis == "col":
            to[1] ^= 1
        elif bands > 1:
            to[0] ^= 1
        perm.append(tuple(functools.reduce(lambda v, k: v * sizes[k] + p[k], range(3), 0) for p in (at, to)))
    got_odd = lax.ppermute(to_odd, names, perm)
    return got_even, got_odd


def dot(a, b):
    return jnp.dot(a, b, preferred_element_type=F32)


def gate(v):
    return 0.5 + 0.5 * jnp.tanh(0.5 * v)


def parity_of_place():
    bits = 0
    for axis in ("dp", "row", "col"):
        at = lax.axis_index(axis)
        for k in range((lax.axis_size(axis) - 1).bit_length()):
            bits = bits + (at >> k)
    return bits % 2


def has_neighbours(axis):
    at = lax.axis_index(axis)
    return jnp.where(at > 0, 1.0, 0.0).astype(F32), jnp.where(at < lax.axis_size(axis) - 1, 1.0, 0.0).astype(F32)


def column_mask(wide, cols, inner):
    spot = lax.broadcasted_iota(jnp.int32, (wide, inner), 0)
    has_low, has_high = has_neighbours("col")
    return jnp.where(spot < cols, 1.0, jnp.where(spot < cols + STRIP // 2, has_high, has_low))


def spread(ref, r, v):
    wide, inner = v.shape
    ref[r, :, 0:inner] = pltpu.roll(v, 1, 0).astype(BF)
    ref[r, :, inner : 2 * inner] = v.astype(BF)
    ref[r, :, 2 * inner :] = pltpu.roll(v, wide - 1, 0).astype(BF)


def conv_pairs(row, starts, w_ref):
    left = [jnp.concatenate([row(i + j) for j in range(4)], axis=1) for i in starts]
    out = dot(jnp.concatenate(left, axis=0), w_ref[...])
    n, inner = left[0].shape[0], w_ref.shape[1] // 2
    return [out[i * n : (i + 1) * n, k * inner : (k + 1) * inner] for i in range(len(starts)) for k in range(2)]


def reduce_act(x, w1, s1, b1):
    pre = dot(x, w1) * s1 + b1
    sg = gate(pre)
    return pre * sg, sg


def through(conv, skip, ct, s2, b2, w3, w3t, s3, b3):
    pre2 = conv * s2 + b2
    sg2 = gate(pre2)
    silu2 = pre2 * sg2
    a2 = silu2.astype(BF)
    pre3 = dot(a2, w3) * s3 + b3 + skip.astype(F32)
    sg3 = gate(pre3)
    back3 = ct.astype(F32) * (sg3 + pre3 * sg3 * (1.0 - sg3))
    grad3 = (back3 * s3).astype(BF)
    grad2 = dot(grad3, w3t) * ((sg2 + silu2 * (1.0 - sg2)) * s2)
    return a2, grad3, back3, grad2


def cut_kernel(x_hbm, c_hbm, odd_ref, even_ref, low_ref, high_ref, sems, *, rows, cols):
    copies = []
    for i, src in enumerate((x_hbm, c_hbm)):
        at = slice(i * rows, (i + 1) * rows)
        copies.append(pltpu.make_async_copy(src.at[:, 0:8, :], low_ref.at[at], sems.at[2 * i]))
        copies.append(pltpu.make_async_copy(src.at[:, cols - 8 : cols, :], high_ref.at[at], sems.at[2 * i + 1]))
    for copy in copies:
        copy.start()
    is_odd = lax.axis_index("col") % 2 == 1
    for copy in copies:
        copy.wait()
    for r in range(2 * rows):
        low = low_ref[r].astype(F32)[0:EDGE]
        high = high_ref[r].astype(F32)[8 - EDGE : 8]
        even_ref[r] = jnp.where(is_odd, low, high).astype(BF)
        odd_ref[r] = jnp.where(is_odd, high, low).astype(BF)


def load_kernel(*refs, inner, group_ch):
    sources, targets, (w2, w2t, w3t, same, pick, gw_ref, sems) = refs[:11], refs[11:21], refs[21:]
    gw_hbm, sources = sources[0], sources[1:]
    copies = [pltpu.make_async_copy(gw_hbm, gw_ref, sems.at[10])]
    copies += [pltpu.make_async_copy(src, dst, sems.at[i]) for i, (src, dst) in enumerate(zip(sources, targets))]
    for copy in copies:
        copy.start()
    copies[0].wait()
    sub = lax.broadcasted_iota(jnp.int32, (inner, inner), 0)
    lane = lax.broadcasted_iota(jnp.int32, (inner, inner), 1)
    diag = jnp.where(sub // group_ch == lane // group_ch, 1.0, 0.0).astype(F32)
    for t in range(9):
        four = gw_ref[t // 3, t % 3].astype(F32)
        eight = jnp.concatenate([four, four], axis=0)
        tiled = jnp.broadcast_to(eight[None], (inner // 8, 8, inner)).reshape(inner, inner)
        dense = tiled * diag
        for ref, tap, block in ((w2, t, dense.astype(BF)), (w2t, 8 - t, dense.T.astype(BF))):
            ref[tap * inner : (tap + 1) * inner, 0:inner] = block
            ref[(tap + 3) * inner : (tap + 4) * inner, inner:] = block
    for ref in (w2, w2t):
        ref[9 * inner :, 0:inner] = jnp.zeros((3 * inner, inner), BF)
        ref[0 : 3 * inner, inner:] = jnp.zeros((3 * inner, inner), BF)
    for k in range(3):
        same[:, k * inner : (k + 1) * inner] = diag
    for t in range(9):
        place = t * group_ch + sub % group_ch
        pick[t * inner : (t + 1) * inner, :] = jnp.where(lane == place, 1.0, 0.0).astype(BF)
    copies[1].wait()
    w3t[...] = targets[0][...].T
    for copy in copies[2:]:
        copy.wait()


def edges_kernel(
    x_ref, c_ref, col_odd, col_even, w1_ref, s1_ref, b1_ref, strip, odd_ref, even_ref, *, rows, cols
):
    col_is_odd = lax.axis_index("col") % 2 == 1
    row_is_odd = lax.axis_index("row") % 2
    chans, inner = w1_ref.shape
    wide = cols + STRIP
    gap = jnp.zeros((STRIP - 2 * EDGE, chans), F32)
    for r in range(2 * rows):
        a, b = col_even[r].astype(F32), col_odd[r].astype(F32)
        high, low = jnp.where(col_is_odd, b, a), jnp.where(col_is_odd, a, b)
        strip[r] = jnp.concatenate([high, gap, low], axis=0).astype(BF)
    behind = [v for r in (1, rows - 2) for v in (x_ref[r], strip[r])]
    act, _ = reduce_act(jnp.concatenate(behind, axis=0), w1_ref[...], s1_ref[...], b1_ref[...])
    col_ok = column_mask(wide, cols, inner)
    act_low, act_high = act[0:wide] * col_ok, act[wide:] * col_ok
    for ref, sends_high in ((even_ref, row_is_odd == 0), (odd_ref, row_is_odd == 1)):
        at = jnp.where(sends_high, rows - 1, 0)
        ref[0:cols, :] = x_ref[at]
        ref[cols:wide, :] = strip[at]
        ref[wide : wide + cols, :] = c_ref[at]
        ref[wide + cols : 2 * wide, :] = strip[rows + at]
        sent = jnp.where(sends_high, act_high, act_low)
        ref[2 * wide :, 0:inner] = sent[0 : wide // 2].astype(BF)
        ref[2 * wide :, inner:] = sent[wide // 2 :].astype(BF)


def inner_kernel(
    x_ref, c_ref, strip_ref, w1_ref, s1_ref, b1_ref, s2_ref, b2_ref, s3_ref, b3_ref, w2, w2t, w3_ref, w3t_ref,
    acts, gcat, d1, back, g1, gw3_ref, full_ref, gw1_ref, xt, xs, cs,
    *, rows, cols, chans, inner,
):
    wide = cols + STRIP
    step = 2
    col_ok = column_mask(wide, cols, inner)
    s1, b1, s2, b2, s3, b3 = (v[...] for v in (s1_ref, b1_ref, s2_ref, b2_ref, s3_ref, b3_ref))
    w1 = w1_ref[...]
    for r in range(rows):
        xs[r, 0:cols, :] = x_ref[r]
        xs[r, cols:wide, :] = strip_ref[r]
        cs[r, 0:cols, :] = c_ref[r]
        cs[r, cols:wide, :] = strip_ref[rows + r]
    for r0 in range(0, rows, step):
        act, sg = reduce_act(xs[r0 : r0 + step].reshape(step * wide, chans), w1, s1, b1)
        slope = (sg + act * (1.0 - sg)) * s1
        for k in range(step):
            r = r0 + k
            spread(acts, r, act[k * wide : (k + 1) * wide] * col_ok)
            d1[r * cols : (r + 1) * cols, :] = slope[k * wide : k * wide + cols]
    rest = (s2, b2, w3_ref[...], w3t_ref[...], s3, b3)
    gw3 = jnp.zeros((inner, chans), F32)
    convs = conv_pairs(lambda r: acts[r], range(0, rows - 2, step), w2)
    for p0 in range(1, rows - 1, step):
        conv = jnp.concatenate(convs[p0 - 1 : p0 - 1 + step], axis=0)
        skip = xs[p0 : p0 + step].reshape(step * wide, chans)
        ct = cs[p0 : p0 + step].reshape(step * wide, chans)
        a2, grad3, back3, grad2 = through(conv, skip, ct, *rest)
        for k in range(step):
            spread(gcat, p0 - 1 + k, grad2[k * wide : (k + 1) * wide] * col_ok)
            back[(p0 - 1 + k) * cols : (p0 + k) * cols, :] = back3[k * wide : k * wide + cols]
        own = [slice(k * wide, k * wide + cols) for k in range(step)]
        gw3 = gw3 + dot(
            jnp.concatenate([a2[at] for at in own], axis=0).T, jnp.concatenate([grad3[at] for at in own], axis=0)
        )
    gw3_ref[...] = gw3
    n = (rows - 2) * cols
    own_gt = gcat[:, 0:cols, inner : 2 * inner].reshape(n, inner).T
    for dh in range(3):
        full_ref[dh] = dot(own_gt, acts[dh : dh + rows - 2, 0:cols, :].reshape(n, 3 * inner))
    gw1t = jnp.zeros((inner, chans), F32)
    convs = conv_pairs(lambda r: gcat[r, 0:cols, :], range(0, rows - 4, step), w2t)
    for p0 in range(2, rows - 2, step):
        conv = jnp.concatenate(convs[p0 - 2 : p0 - 2 + step], axis=0)
        g = (conv * d1[p0 * cols : (p0 + step) * cols, :]).astype(BF)
        g1[(p0 - 2) * cols : (p0 - 2 + step) * cols, :] = g
        gw1t = gw1t + dot(g.T, x_ref[p0 : p0 + step].reshape(step * cols, chans))
    gw1_ref[...] = gw1t.T
    for k, p in enumerate((0, 1, rows - 2, rows - 1)):
        xt[:, k * cols : (k + 1) * cols] = x_ref[p].T


def rim_kernel(
    x_ref, c_ref, strip_ref, row_even, row_odd, w1_ref, s1_ref, b1_ref, s2_ref, b2_ref, s3_ref, b3_ref, w2, w2t, w3_ref, w3t_ref,
    acts, gcat, d1, gw3_ref, full_ref, gw1_ref, xt, same, pick,
    share_ref, g1, back, hacts, hgrad, far_ref,
    *, rows, cols, chans, inner, group_ch,
):
    wide = cols + STRIP
    col_ok = column_mask(wide, cols, inner)
    s1, b1, s2, b2, s3, b3 = (v[...] for v in (s1_ref, b1_ref, s2_ref, b2_ref, s3_ref, b3_ref))
    row_is_odd = lax.axis_index("row") % 2
    has_low, has_high = has_neighbours("row")

    @pl.when(row_is_odd == 0)
    def _():
        far_ref[0] = row_odd[...]
        far_ref[1] = row_even[...]

    @pl.when(row_is_odd == 1)
    def _():
        far_ref[0] = row_even[...]
        far_ref[1] = row_odd[...]

    def wider(ref, r, base):
        return jnp.concatenate([ref[r], strip_ref[base + r]], axis=0)

    near = [far_ref[i, 0:wide, :] for i in range(2)]
    near_cot = [far_ref[i, wide : 2 * wide, :] for i in range(2)]
    act, _ = reduce_act(jnp.concatenate(near, axis=0), w1_ref[...], s1, b1)
    for k, has in ((0, has_low), (1, has_high)):
        sent = far_ref[k, 2 * wide :, :].astype(F32)
        spread(hacts, 3 * k, jnp.concatenate([sent[:, 0:inner], sent[:, inner:]], axis=0) * has)
        spread(hacts, 1 + k, act[k * wide : (k + 1) * wide] * (col_ok * has))
    def act_row(r):
        return hacts[r] if r < 2 else acts[r - 2] if r < rows + 2 else hacts[r - rows]

    conv = jnp.concatenate(conv_pairs(act_row, (0, rows), w2), axis=0)
    skip = jnp.concatenate([near[0], wider(x_ref, 0, 0), wider(x_ref, rows - 1, 0), near[1]], axis=0)
    ct = jnp.concatenate([near_cot[0], wider(c_ref, 0, rows), wider(c_ref, rows - 1, rows), near_cot[1]], axis=0)
    a2, grad3, back3, grad2 = through(conv, skip, ct, s2, b2, w3_ref[...], w3t_ref[...], s3, b3)
    for k in range(4):
        g = grad2[k * wide : (k + 1) * wide] * col_ok
        spread(hgrad, k, g * has_low if k == 0 else g * has_high if k == 3 else g)
    own = [slice(k * wide, k * wide + cols) for k in (1, 2)]
    for k in range(2):
        back[k * cols : (k + 1) * cols, :] = back3[own[k]]
    def grad_row(q):
        return (hgrad[q] if q < 2 else gcat[q - 2] if q < rows else hgrad[q - rows + 2])[0:cols]

    outs = (0, 1, rows - 2, rows - 1)
    conv = jnp.concatenate(conv_pairs(grad_row, (0, rows - 2), w2t), axis=0)
    slope = jnp.concatenate([d1[0 : 2 * cols, :], d1[(rows - 2) * cols :, :]], axis=0)
    g = (conv * slope).astype(BF)
    g1[...] = g
    own_gt = jnp.concatenate([hgrad[k, 0:cols, inner : 2 * inner] for k in (1, 2)], axis=0).T
    around = jnp.concatenate(
        [jnp.concatenate([act_row(q + dh)[0:cols] for q in (1, rows)], axis=0) for dh in range(3)], axis=1
    )
    full = dot(own_gt, around)
    full = jnp.concatenate(
        [(full_ref[dh] + full[:, dh * 3 * inner : (dh + 1) * 3 * inner]) * same[...] for dh in range(3)], axis=1
    )
    compact = dot(full.astype(BF), pick[...])
    gw2 = compact.T

    gw1 = gw1_ref[...] + dot(xt[...], g)
    gw3 = gw3_ref[...] + dot(
        jnp.concatenate([a2[at] for at in own], axis=0).T, jnp.concatenate([grad3[at] for at in own], axis=0)
    )
    n_dp = share_ref.shape[1]
    one, three = chans // n_dp, inner // n_dp
    parity = parity_of_place()
    at = (parity, 1 - parity)
    for h in range(n_dp):
        slot = h ^ lax.axis_index("dp")
        share_ref[at[0], slot, 0:one, :] = gw1[h * one : (h + 1) * one]
        for k in range(chans // inner):
            share_ref[at[1], slot, k * three : (k + 1) * three, :] = gw3[
                h * three : (h + 1) * three, k * inner : (k + 1) * inner
            ]
        group = gw2 if h == 0 else pltpu.roll(gw2, inner - h * three, 1)
        part, half = 3 * group_ch, inner // 2
        left = lax.broadcasted_iota(jnp.int32, (GROUP_ROWS, inner), 1) < half
        beside = pltpu.roll(group, half, 1)[part : part + GROUP_ROWS]
        share_ref[at[0], slot, one : one + GROUP_ROWS, :] = jnp.where(left, group[0:GROUP_ROWS], beside)
        share_ref[at[1], slot, one : one + GROUP_ROWS, :] = group[2 * part : 2 * part + GROUP_ROWS]


def out_kernel(g1_in, g1_rim, back_in, back_rim, w1_ref, out_ref, *, rows, cols, chans):
    w1t = w1_ref[...].T
    for p in range(rows):
        if 2 <= p < rows - 2:
            g = g1_in[(p - 2) * cols : (p - 1) * cols, :]
        else:
            k = p if p < 2 else p - rows + 4
            g = g1_rim[k * cols : (k + 1) * cols, :]
        if 1 <= p < rows - 1:
            b = back_in[(p - 1) * cols : p * cols, :]
        else:
            b = back_rim[0:cols, :] if p == 0 else back_rim[cols:, :]
        out_ref[p] = (dot(g, w1t) + b).astype(BF)


def last_kernel(
    a_ref, b_ref, r_out, g_out, e_out, r_ref, g_ref, e_ref, sems, *, scale, one, three, chans, inner, group_ch
):
    other_first = parity_of_place() == 1
    copies = [
        pltpu.make_async_copy(src, dst, sems.at[i])
        for i, (src, dst) in enumerate(((r_ref, r_out), (e_ref, e_out), (g_ref, g_out)))
    ]
    first = jnp.where(other_first, b_ref[...], a_ref[...]) * scale
    r_ref[...] = first[0:one]
    copies[0].start()
    second = jnp.where(other_first, a_ref[...], b_ref[...]) * scale
    for k in range(chans // inner):
        e_ref[:, k * inner : (k + 1) * inner] = second[k * three : (k + 1) * three]
    copies[1].start()
    for t in range(9):
        at = one + t % 3 * group_ch
        side = inner // 2 if t // 3 == 1 else 0
        part = (second if t // 3 == 2 else first)[at : at + group_ch]
        g_ref[t // 3, t % 3] = part[:, side : side + three]
    copies[2].start()
    for copy in copies:
        copy.wait()


def crossed(value, move, other_move):
    names = ("dp", "row", "col")
    sizes = [lax.axis_size(a) for a in names]
    perm = []
    for at in itertools.product(*(range(n) for n in sizes)):
        axis, bit = other_move if sum(i.bit_count() for i in at) % 2 else move
        to = list(at)
        to[names.index(axis)] ^= bit
        to[1] ^= 1
        perm.append(tuple(functools.reduce(lambda v, k: v * sizes[k] + p[k], range(3), 0) for p in (at, to)))
    return lax.ppermute(value, names, perm)


def body(
    features, reduce_weight, scale_one, shift_one, group_weight, scale_two, shift_two, expand_weight, scale_three,
    shift_three, cotangent,
):
    _, rows, cols, chans = features.shape
    inner = reduce_weight.shape[1]
    group_ch = group_weight.shape[2]
    x, c = features[0], cotangent[0]
    n_dp, n_row, n_col = (lax.axis_size(a) for a in ("dp", "row", "col"))

    wide = cols + STRIP
    one, three = chans // n_dp, inner // n_dp
    half_rows = one + GROUP_ROWS
    vmem = pl.BlockSpec(memory_space=pltpu.VMEM)
    params = pltpu.CompilerParams(vmem_limit_bytes=8 << 20)
    sizes = dict(rows=rows, cols=cols, chans=chans)
    shape = jax.ShapeDtypeStruct

    x, c = (pltpu.with_memory_space_constraint(v, pltpu.HBM) for v in (x, c))
    to_odd, to_even = pl.pallas_call(
        functools.partial(cut_kernel, rows=rows, cols=cols),
        out_shape=(shape((2 * rows, EDGE, chans), BF),) * 2,
        in_specs=[pl.BlockSpec(memory_space=pltpu.HBM)] * 2,
        out_specs=(vmem,) * 2,
        scratch_shapes=[pltpu.VMEM((2 * rows, 8, chans), BF)] * 2 + [pltpu.SemaphoreType.DMA((4,))],
        compiler_params=params,
        name="cut",
    )(x, c)
    col_even, col_odd = swap_edges(to_even, to_odd, "col")
    sources = (
        expand_weight, reduce_weight, x, c, scale_one[None], shift_one[None], scale_two[None], shift_two[None],
        scale_three[None], shift_three[None],
    )
    w3, w1, x, c, *vecs, w2, w2t, w3t, same, pick = pl.pallas_call(
        functools.partial(load_kernel, inner=inner, group_ch=group_ch),
        out_shape=tuple(shape(v.shape, v.dtype) for v in sources)
        + (shape((12 * inner, 2 * inner), BF), shape((12 * inner, 2 * inner), BF), shape((chans, inner), BF))
        + (shape((inner, 3 * inner), F32), shape((9 * inner, inner), BF)),
        in_specs=[pl.BlockSpec(memory_space=pltpu.HBM)] * 11,
        out_specs=(vmem,) * 15,
        scratch_shapes=[pltpu.VMEM(group_weight.shape, BF), pltpu.SemaphoreType.DMA((11,))],
        compiler_params=params,
        name="load",
    )(*(pltpu.with_memory_space_constraint(v, pltpu.HBM) for v in (group_weight, *sources)))
    shared = (w1, *vecs, w2, w2t, w3, w3t)
    col_odd, col_even, shared, x, c = lax.optimization_barrier((col_odd, col_even, shared, x, c))
    w1, *vecs = shared[:7]
    message = 2 * wide + wide * inner // chans
    strip, to_odd, to_even = pl.pallas_call(
        functools.partial(edges_kernel, rows=rows, cols=cols),
        out_shape=(shape((2 * rows, STRIP, chans), BF),) + (shape((message, chans), BF),) * 2,
        in_specs=[vmem] * 7,
        out_specs=(vmem,) * 3,
        compiler_params=params,
        name="edges",
    )(x, c, col_odd, col_even, w1, *vecs[:2])
    row_even, row_odd = swap_edges(to_even, to_odd, "row")
    acts, gcat, d1, back_in, g1_in, gw3, full, gw1, xt = pl.pallas_call(
        functools.partial(inner_kernel, inner=inner, **sizes),
        out_shape=(
            shape((rows, wide, 3 * inner), BF),
            shape((rows - 2, wide, 3 * inner), BF),
            shape((rows * cols, inner), F32),
            shape(((rows - 2) * cols, chans), F32),
            shape(((rows - 4) * cols, inner), BF),
            shape((inner, chans), F32),
            shape((3, inner, 3 * inner), F32),
            shape((chans, inner), F32),
            shape((chans, 4 * cols), BF),
        ),
        in_specs=[vmem] * 14,
        out_specs=(vmem,) * 9,
        scratch_shapes=[pltpu.VMEM((rows, wide, chans), BF), pltpu.VMEM((rows, wide, chans), BF)],
        compiler_params=params,
        name="inner",
    )(x, c, strip, *shared)
    shares, g1_rim, back_rim = pl.pallas_call(
        functools.partial(rim_kernel, inner=inner, group_ch=group_ch, **sizes),
        out_shape=(
            shape((2, n_dp, half_rows, inner), F32),
            shape((4 * cols, inner), BF),
            shape((2 * cols, chans), F32),
        ),
        in_specs=[vmem] * 25,
        out_specs=(vmem,) * 3,
        scratch_shapes=[pltpu.VMEM((4, wide, 3 * inner), BF)] * 2 + [pltpu.VMEM((2, message, chans), BF)],
        compiler_params=params,
        name="rim",
    )(x, c, strip, row_even, row_odd, *shared, acts, gcat, d1, gw3, full, gw1, xt, same, pick)
    near = [(i, i ^ 1) for i in range(n_row)]
    shares = (shares[0] + lax.ppermute(shares[1], "row", near)).astype(BF)
    g1_rim, shares = lax.optimization_barrier((g1_rim, shares))
    input_grad = pl.pallas_call(
        functools.partial(out_kernel, **sizes),
        out_shape=shape((rows, cols, chans), BF),
        in_specs=[vmem] * 5,
        out_specs=vmem,
        compiler_params=params,
        name="out",
    )(g1_in, g1_rim, back_in, back_rim, w1)
    held = n_dp
    while held > 1:
        held //= 2
        other = crossed(shares[held:], ("dp", held), ("dp", held))
        shares = (shares[:held].astype(F32) + other.astype(F32)).astype(BF)
    total = shares[0]
    steps = [("row", 1 << k) for k in range(1, n_row.bit_length() - 1)]
    steps += [("col", 1 << k) for k in reversed(range(n_col.bit_length() - 1))]
    for i, step in enumerate(steps):
        other = crossed(total, step, steps[(i + 1) % len(steps)])
        if i == 0:
            input_grad, other = lax.optimization_barrier((input_grad, other))
        summed = total.astype(F32) + other.astype(F32)
        total = summed.astype(BF)
    pixels = rows * cols * n_dp * n_row * n_col
    reduce_grad, group_grad, expand_grad = pl.pallas_call(
        functools.partial(
            last_kernel, scale=pixels**-0.5, one=one, three=three, chans=chans, inner=inner, group_ch=group_ch
        ),
        out_shape=(
            jax.ShapeDtypeStruct((one, inner), F32),
            jax.ShapeDtypeStruct((3, 3, group_ch, three), F32),
            jax.ShapeDtypeStruct((three, chans), F32),
        ),
        in_specs=[vmem, vmem],
        out_specs=(pl.BlockSpec(memory_space=pl.ANY),) * 3,
        scratch_shapes=[
            pltpu.VMEM((one, inner), F32),
            pltpu.VMEM((3, 3, group_ch, three), F32),
            pltpu.VMEM((three, chans), F32),
            pltpu.SemaphoreType.DMA((3,)),
        ],
        compiler_params=pltpu.CompilerParams(vmem_limit_bytes=2 << 20),
        name="last",
    )(summed, lax.ppermute(summed, "row", near))
    return input_grad[None], reduce_grad, jnp.transpose(group_grad, (3, 0, 1, 2)), expand_grad


def solution(mesh):
    image = P("dp", "row", "col", None)
    return jax.shard_map(
        body,
        mesh=mesh,
        in_specs=(image,) + (P(),) * 9 + (image,),
        out_specs=(image, P("dp", None), P("dp", None, None, None), P("dp", None)),
        check_vma=False,
    )
```

```python
import functools
import itertools

import jax
import jax.numpy as jnp
from jax import lax
from jax.experimental import pallas as pl
from jax.experimental.pallas import tpu as pltpu
from jax.sharding import PartitionSpec as P

BF = jnp.bfloat16
F32 = jnp.float32
EDGE = 2
STRIP = 16
GROUP_ROWS = 24


def swap_edges(to_even, to_odd, axis):
    count, bands = lax.axis_size(axis), lax.axis_size("dp")
    got_even = lax.ppermute(to_even, axis, [(i, i ^ 1) for i in range(count)])
    names = ("dp", "row", "col")
    sizes = [lax.axis_size(a) for a in names]
    which = names.index(axis)
    perm = []
    for at in itertools.product(*(range(n) for n in sizes)):
        to = list(at)
        if 0 < at[which] < count - 1:
            to[which] = ((at[which] - 1) ^ 1) + 1
        elif axis == "col":
            to[1] ^= 1
        elif bands > 1:
            to[0] ^= 1
        perm.append(tuple(functools.reduce(lambda v, k: v * sizes[k] + p[k], range(3), 0) for p in (at, to)))
    got_odd = lax.ppermute(to_odd, names, perm)
    return got_even, got_odd


def dot(a, b):
    return jnp.dot(a, b, preferred_element_type=F32)


def gate(v):
    return 0.5 + 0.5 * jnp.tanh(0.5 * v)


def parity_of_place():
    bits = 0
    for axis in ("dp", "row", "col"):
        at = lax.axis_index(axis)
        for k in range((lax.axis_size(axis) - 1).bit_length()):
            bits = bits + (at >> k)
    return bits % 2


def has_neighbours(axis):
    at = lax.axis_index(axis)
    return jnp.where(at > 0, 1.0, 0.0).astype(F32), jnp.where(at < lax.axis_size(axis) - 1, 1.0, 0.0).astype(F32)


def column_mask(wide, cols, inner):
    spot = lax.broadcasted_iota(jnp.int32, (wide, inner), 0)
    has_low, has_high = has_neighbours("col")
    return jnp.where(spot < cols, 1.0, jnp.where(spot < cols + STRIP // 2, has_high, has_low))


def spread(ref, r, v):
    wide, inner = v.shape
    ref[r, :, 0:inner] = pltpu.roll(v, 1, 0).astype(BF)
    ref[r, :, inner : 2 * inner] = v.astype(BF)
    ref[r, :, 2 * inner :] = pltpu.roll(v, wide - 1, 0).astype(BF)


def conv_pairs(row, starts, w_ref):
    left = [jnp.concatenate([row(i + j) for j in range(4)], axis=1) for i in starts]
    out = dot(jnp.concatenate(left, axis=0), w_ref[...])
    n, inner = left[0].shape[0], w_ref.shape[1] // 2
    return [out[i * n : (i + 1) * n, k * inner : (k + 1) * inner] for i in range(len(starts)) for k in range(2)]


def reduce_act(x, w1, s1, b1):
    pre = dot(x, w1) * s1 + b1
    sg = gate(pre)
    return pre * sg, sg


def through(conv, skip, ct, s2, b2, w3, w3t, s3, b3):
    pre2 = conv * s2 + b2
    sg2 = gate(pre2)
    silu2 = pre2 * sg2
    a2 = silu2.astype(BF)
    pre3 = dot(a2, w3) * s3 + b3 + skip.astype(F32)
    sg3 = gate(pre3)
    back3 = ct.astype(F32) * (sg3 + pre3 * sg3 * (1.0 - sg3))
    grad3 = (back3 * s3).astype(BF)
    grad2 = dot(grad3, w3t) * ((sg2 + silu2 * (1.0 - sg2)) * s2)
    return a2, grad3, back3, grad2


def cut_kernel(x_hbm, c_hbm, odd_ref, even_ref, low_ref, high_ref, sems, *, rows, cols):
    copies = []
    for i, src in enumerate((x_hbm, c_hbm)):
        at = slice(i * rows, (i + 1) * rows)
        copies.append(pltpu.make_async_copy(src.at[:, 0:8, :], low_ref.at[at], sems.at[2 * i]))
        copies.append(pltpu.make_async_copy(src.at[:, cols - 8 : cols, :], high_ref.at[at], sems.at[2 * i + 1]))
    for copy in copies:
        copy.start()
    is_odd = lax.axis_index("col") % 2 == 1
    for copy in copies:
        copy.wait()
    for r in range(2 * rows):
        low = low_ref[r].astype(F32)[0:EDGE]
        high = high_ref[r].astype(F32)[8 - EDGE : 8]
        even_ref[r] = jnp.where(is_odd, low, high).astype(BF)
        odd_ref[r] = jnp.where(is_odd, high, low).astype(BF)


def load_kernel(*refs, inner, group_ch):
    sources, targets, (w2, w2t, w3t, same, pick, gw_ref, sems) = refs[:11], refs[11:21], refs[21:]
    gw_hbm, sources = sources[0], sources[1:]
    copies = [pltpu.make_async_copy(gw_hbm, gw_ref, sems.at[10])]
    copies += [pltpu.make_async_copy(src, dst, sems.at[i]) for i, (src, dst) in enumerate(zip(sources, targets))]
    for copy in copies:
        copy.start()
    copies[0].wait()
    sub = lax.broadcasted_iota(jnp.int32, (inner, inner), 0)
    lane = lax.broadcasted_iota(jnp.int32, (inner, inner), 1)
    diag = jnp.where(sub // group_ch == lane // group_ch, 1.0, 0.0).astype(F32)
    for t in range(9):
        four = gw_ref[t // 3, t % 3].astype(F32)
        eight = jnp.concatenate([four, four], axis=0)
        tiled = jnp.broadcast_to(eight[None], (inner // 8, 8, inner)).reshape(inner, inner)
        dense = tiled * diag
        for ref, tap, block in ((w2, t, dense.astype(BF)), (w2t, 8 - t, dense.T.astype(BF))):
            ref[tap * inner : (tap + 1) * inner, 0:inner] = block
            ref[(tap + 3) * inner : (tap + 4) * inner, inner:] = block
    for ref in (w2, w2t):
        ref[9 * inner :, 0:inner] = jnp.zeros((3 * inner, inner), BF)
        ref[0 : 3 * inner, inner:] = jnp.zeros((3 * inner, inner), BF)
    for k in range(3):
        same[:, k * inner : (k + 1) * inner] = diag
    for t in range(9):
        place = t * group_ch + sub % group_ch
        pick[t * inner : (t + 1) * inner, :] = jnp.where(lane == place, 1.0, 0.0).astype(BF)
    copies[1].wait()
    w3t[...] = targets[0][...].T
    for copy in copies[2:]:
        copy.wait()


def edges_kernel(
    x_ref, c_ref, col_odd, col_even, w1_ref, s1_ref, b1_ref, strip, odd_ref, even_ref, *, rows, cols
):
    col_is_odd = lax.axis_index("col") % 2 == 1
    row_is_odd = lax.axis_index("row") % 2
    chans, inner = w1_ref.shape
    wide = cols + STRIP
    gap = jnp.zeros((STRIP - 2 * EDGE, chans), F32)
    for r in range(2 * rows):
        a, b = col_even[r].astype(F32), col_odd[r].astype(F32)
        high, low = jnp.where(col_is_odd, b, a), jnp.where(col_is_odd, a, b)
        strip[r] = jnp.concatenate([high, gap, low], axis=0).astype(BF)
    behind = [v for r in (1, rows - 2) for v in (x_ref[r], strip[r])]
    act, _ = reduce_act(jnp.concatenate(behind, axis=0), w1_ref[...], s1_ref[...], b1_ref[...])
    col_ok = column_mask(wide, cols, inner)
    act_low, act_high = act[0:wide] * col_ok, act[wide:] * col_ok
    for ref, sends_high in ((even_ref, row_is_odd == 0), (odd_ref, row_is_odd == 1)):
        at = jnp.where(sends_high, rows - 1, 0)
        ref[0:cols, :] = x_ref[at]
        ref[cols:wide, :] = strip[at]
        ref[wide : wide + cols, :] = c_ref[at]
        ref[wide + cols : 2 * wide, :] = strip[rows + at]
        sent = jnp.where(sends_high, act_high, act_low)
        ref[2 * wide :, 0:inner] = sent[0 : wide // 2].astype(BF)
        ref[2 * wide :, inner:] = sent[wide // 2 :].astype(BF)


def inner_kernel(
    x_ref, c_ref, strip_ref, w1_ref, s1_ref, b1_ref, s2_ref, b2_ref, s3_ref, b3_ref, w2, w2t, w3_ref, w3t_ref,
    acts, gcat, d1, back, g1, gw3_ref, full_ref, gw1_ref, xt, xs, cs,
    *, rows, cols, chans, inner,
):
    wide = cols + STRIP
    step = 2
    col_ok = column_mask(wide, cols, inner)
    s1, b1, s2, b2, s3, b3 = (v[...] for v in (s1_ref, b1_ref, s2_ref, b2_ref, s3_ref, b3_ref))
    w1 = w1_ref[...]
    for r in range(rows):
        xs[r, 0:cols, :] = x_ref[r]
        xs[r, cols:wide, :] = strip_ref[r]
        cs[r, 0:cols, :] = c_ref[r]
        cs[r, cols:wide, :] = strip_ref[rows + r]
    for r0 in range(0, rows, step):
        act, sg = reduce_act(xs[r0 : r0 + step].reshape(step * wide, chans), w1, s1, b1)
        slope = (sg + act * (1.0 - sg)) * s1
        for k in range(step):
            r = r0 + k
            spread(acts, r, act[k * wide : (k + 1) * wide] * col_ok)
            d1[r * cols : (r + 1) * cols, :] = slope[k * wide : k * wide + cols]
    rest = (s2, b2, w3_ref[...], w3t_ref[...], s3, b3)
    gw3 = jnp.zeros((inner, chans), F32)
    convs = conv_pairs(lambda r: acts[r], range(0, rows - 2, step), w2)
    for p0 in range(1, rows - 1, step):
        conv = jnp.concatenate(convs[p0 - 1 : p0 - 1 + step], axis=0)
        skip = xs[p0 : p0 + step].reshape(step * wide, chans)
        ct = cs[p0 : p0 + step].reshape(step * wide, chans)
        a2, grad3, back3, grad2 = through(conv, skip, ct, *rest)
        for k in range(step):
            spread(gcat, p0 - 1 + k, grad2[k * wide : (k + 1) * wide] * col_ok)
            back[(p0 - 1 + k) * cols : (p0 + k) * cols, :] = back3[k * wide : k * wide + cols]
        own = [slice(k * wide, k * wide + cols) for k in range(step)]
        gw3 = gw3 + dot(
            jnp.concatenate([a2[at] for at in own], axis=0).T, jnp.concatenate([grad3[at] for at in own], axis=0)
        )
    gw3_ref[...] = gw3
    n = (rows - 2) * cols
    own_gt = gcat[:, 0:cols, inner : 2 * inner].reshape(n, inner).T
    for dh in range(3):
        full_ref[dh] = dot(own_gt, acts[dh : dh + rows - 2, 0:cols, :].reshape(n, 3 * inner))
    gw1t = jnp.zeros((inner, chans), F32)
    convs = conv_pairs(lambda r: gcat[r, 0:cols, :], range(0, rows - 4, step), w2t)
    for p0 in range(2, rows - 2, step):
        conv = jnp.concatenate(convs[p0 - 2 : p0 - 2 + step], axis=0)
        g = (conv * d1[p0 * cols : (p0 + step) * cols, :]).astype(BF)
        g1[(p0 - 2) * cols : (p0 - 2 + step) * cols, :] = g
        gw1t = gw1t + dot(g.T, x_ref[p0 : p0 + step].reshape(step * cols, chans))
    gw1_ref[...] = gw1t.T
    for k, p in enumerate((0, 1, rows - 2, rows - 1)):
        xt[:, k * cols : (k + 1) * cols] = x_ref[p].T


def rim_kernel(
    x_ref, c_ref, strip_ref, row_even, row_odd, w1_ref, s1_ref, b1_ref, s2_ref, b2_ref, s3_ref, b3_ref, w2, w2t, w3_ref, w3t_ref,
    acts, gcat, d1, gw3_ref, full_ref, gw1_ref, xt, same, pick,
    share_ref, g1, back, hacts, hgrad, far_ref,
    *, rows, cols, chans, inner, group_ch,
):
    wide = cols + STRIP
    col_ok = column_mask(wide, cols, inner)
    s1, b1, s2, b2, s3, b3 = (v[...] for v in (s1_ref, b1_ref, s2_ref, b2_ref, s3_ref, b3_ref))
    row_is_odd = lax.axis_index("row") % 2
    has_low, has_high = has_neighbours("row")

    @pl.when(row_is_odd == 0)
    def _():
        far_ref[0] = row_odd[...]
        far_ref[1] = row_even[...]

    @pl.when(row_is_odd == 1)
    def _():
        far_ref[0] = row_even[...]
        far_ref[1] = row_odd[...]

    def wider(ref, r, base):
        return jnp.concatenate([ref[r], strip_ref[base + r]], axis=0)

    near = [far_ref[i, 0:wide, :] for i in range(2)]
    near_cot = [far_ref[i, wide : 2 * wide, :] for i in range(2)]
    act, _ = reduce_act(jnp.concatenate(near, axis=0), w1_ref[...], s1, b1)
    for k, has in ((0, has_low), (1, has_high)):
        sent = far_ref[k, 2 * wide :, :].astype(F32)
        spread(hacts, 3 * k, jnp.concatenate([sent[:, 0:inner], sent[:, inner:]], axis=0) * has)
        spread(hacts, 1 + k, act[k * wide : (k + 1) * wide] * (col_ok * has))
    def act_row(r):
        return hacts[r] if r < 2 else acts[r - 2] if r < rows + 2 else hacts[r - rows]

    conv = jnp.concatenate(conv_pairs(act_row, (0, rows), w2), axis=0)
    skip = jnp.concatenate([near[0], wider(x_ref, 0, 0), wider(x_ref, rows - 1, 0), near[1]], axis=0)
    ct = jnp.concatenate([near_cot[0], wider(c_ref, 0, rows), wider(c_ref, rows - 1, rows), near_cot[1]], axis=0)
    a2, grad3, back3, grad2 = through(conv, skip, ct, s2, b2, w3_ref[...], w3t_ref[...], s3, b3)
    for k in range(4):
        g = grad2[k * wide : (k + 1) * wide] * col_ok
        spread(hgrad, k, g * has_low if k == 0 else g * has_high if k == 3 else g)
    own = [slice(k * wide, k * wide + cols) for k in (1, 2)]
    for k in range(2):
        back[k * cols : (k + 1) * cols, :] = back3[own[k]]
    def grad_row(q):
        return (hgrad[q] if q < 2 else gcat[q - 2] if q < rows else hgrad[q - rows + 2])[0:cols]

    outs = (0, 1, rows - 2, rows - 1)
    conv = jnp.concatenate(conv_pairs(grad_row, (0, rows - 2), w2t), axis=0)
    slope = jnp.concatenate([d1[0 : 2 * cols, :], d1[(rows - 2) * cols :, :]], axis=0)
    g = (conv * slope).astype(BF)
    g1[...] = g
    own_gt = jnp.concatenate([hgrad[k, 0:cols, inner : 2 * inner] for k in (1, 2)], axis=0).T
    around = jnp.concatenate(
        [jnp.concatenate([act_row(q + dh)[0:cols] for q in (1, rows)], axis=0) for dh in range(3)], axis=1
    )
    full = dot(own_gt, around)
    full = jnp.concatenate(
        [(full_ref[dh] + full[:, dh * 3 * inner : (dh + 1) * 3 * inner]) * same[...] for dh in range(3)], axis=1
    )
    compact = dot(full.astype(BF), pick[...])
    gw2 = compact.T

    gw1 = gw1_ref[...] + dot(xt[...], g)
    gw3 = gw3_ref[...] + dot(
        jnp.concatenate([a2[at] for at in own], axis=0).T, jnp.concatenate([grad3[at] for at in own], axis=0)
    )
    n_dp = share_ref.shape[1]
    one, three = chans // n_dp, inner // n_dp
    parity = parity_of_place()
    at = (parity, 1 - parity)
    for h in range(n_dp):
        slot = h ^ lax.axis_index("dp")
        share_ref[at[0], slot, 0:one, :] = gw1[h * one : (h + 1) * one]
        for k in range(chans // inner):
            share_ref[at[1], slot, k * three : (k + 1) * three, :] = gw3[
                h * three : (h + 1) * three, k * inner : (k + 1) * inner
            ]
        group = gw2 if h == 0 else pltpu.roll(gw2, inner - h * three, 1)
        share_ref[at[0], slot, one : one + GROUP_ROWS, :] = group[0:GROUP_ROWS]
        share_ref[at[1], slot, one : one + GROUP_ROWS, :] = group[GROUP_ROWS : 2 * GROUP_ROWS]


def out_kernel(g1_in, g1_rim, back_in, back_rim, w1_ref, out_ref, *, rows, cols, chans):
    w1t = w1_ref[...].T
    for p in range(rows):
        if 2 <= p < rows - 2:
            g = g1_in[(p - 2) * cols : (p - 1) * cols, :]
        else:
            k = p if p < 2 else p - rows + 4
            g = g1_rim[k * cols : (k + 1) * cols, :]
        if 1 <= p < rows - 1:
            b = back_in[(p - 1) * cols : p * cols, :]
        else:
            b = back_rim[0:cols, :] if p == 0 else back_rim[cols:, :]
        out_ref[p] = (dot(g, w1t) + b).astype(BF)


def last_kernel(
    a_ref, b_ref, r_out, g_out, e_out, r_ref, g_ref, e_ref, sems, *, scale, one, three, chans, inner, group_ch
):
    other_first = parity_of_place() == 1
    copies = [
        pltpu.make_async_copy(src, dst, sems.at[i])
        for i, (src, dst) in enumerate(((r_ref, r_out), (e_ref, e_out), (g_ref, g_out)))
    ]
    first = jnp.where(other_first, b_ref[...], a_ref[...]) * scale
    r_ref[...] = first[0:one]
    copies[0].start()
    second = jnp.where(other_first, a_ref[...], b_ref[...]) * scale
    for k in range(chans // inner):
        e_ref[:, k * inner : (k + 1) * inner] = second[k * three : (k + 1) * three]
    copies[1].start()
    for t in range(9):
        at = t * group_ch
        part = first[one + at : one + at + group_ch] if at < GROUP_ROWS else second[
            one + at - GROUP_ROWS : one + at - GROUP_ROWS + group_ch]
        g_ref[t // 3, t % 3] = part[:, 0:three]
    copies[2].start()
    for copy in copies:
        copy.wait()


def crossed(value, move, other_move):
    names = ("dp", "row", "col")
    sizes = [lax.axis_size(a) for a in names]
    perm = []
    for at in itertools.product(*(range(n) for n in sizes)):
        axis, bit = other_move if sum(i.bit_count() for i in at) % 2 else move
        to = list(at)
        to[names.index(axis)] ^= bit
        to[1] ^= 1
        perm.append(tuple(functools.reduce(lambda v, k: v * sizes[k] + p[k], range(3), 0) for p in (at, to)))
    return lax.ppermute(value, names, perm)


def body(
    features, reduce_weight, scale_one, shift_one, group_weight, scale_two, shift_two, expand_weight, scale_three,
    shift_three, cotangent,
):
    _, rows, cols, chans = features.shape
    inner = reduce_weight.shape[1]
    group_ch = group_weight.shape[2]
    x, c = features[0], cotangent[0]
    n_dp, n_row, n_col = (lax.axis_size(a) for a in ("dp", "row", "col"))

    wide = cols + STRIP
    one, three = chans // n_dp, inner // n_dp
    half_rows = one + GROUP_ROWS
    vmem = pl.BlockSpec(memory_space=pltpu.VMEM)
    params = pltpu.CompilerParams(vmem_limit_bytes=8 << 20)
    sizes = dict(rows=rows, cols=cols, chans=chans)
    shape = jax.ShapeDtypeStruct

    x, c = (pltpu.with_memory_space_constraint(v, pltpu.HBM) for v in (x, c))
    to_odd, to_even = pl.pallas_call(
        functools.partial(cut_kernel, rows=rows, cols=cols),
        out_shape=(shape((2 * rows, EDGE, chans), BF),) * 2,
        in_specs=[pl.BlockSpec(memory_space=pltpu.HBM)] * 2,
        out_specs=(vmem,) * 2,
        scratch_shapes=[pltpu.VMEM((2 * rows, 8, chans), BF)] * 2 + [pltpu.SemaphoreType.DMA((4,))],
        compiler_params=params,
        name="cut",
    )(x, c)
    col_even, col_odd = swap_edges(to_even, to_odd, "col")
    sources = (
        expand_weight, reduce_weight, x, c, scale_one[None], shift_one[None], scale_two[None], shift_two[None],
        scale_three[None], shift_three[None],
    )
    w3, w1, x, c, *vecs, w2, w2t, w3t, same, pick = pl.pallas_call(
        functools.partial(load_kernel, inner=inner, group_ch=group_ch),
        out_shape=tuple(shape(v.shape, v.dtype) for v in sources)
        + (shape((12 * inner, 2 * inner), BF), shape((12 * inner, 2 * inner), BF), shape((chans, inner), BF))
        + (shape((inner, 3 * inner), F32), shape((9 * inner, inner), BF)),
        in_specs=[pl.BlockSpec(memory_space=pltpu.HBM)] * 11,
        out_specs=(vmem,) * 15,
        scratch_shapes=[pltpu.VMEM(group_weight.shape, BF), pltpu.SemaphoreType.DMA((11,))],
        compiler_params=params,
        name="load",
    )(*(pltpu.with_memory_space_constraint(v, pltpu.HBM) for v in (group_weight, *sources)))
    shared = (w1, *vecs, w2, w2t, w3, w3t)
    col_odd, col_even, shared, x, c = lax.optimization_barrier((col_odd, col_even, shared, x, c))
    w1, *vecs = shared[:7]
    message = 2 * wide + wide * inner // chans
    strip, to_odd, to_even = pl.pallas_call(
        functools.partial(edges_kernel, rows=rows, cols=cols),
        out_shape=(shape((2 * rows, STRIP, chans), BF),) + (shape((message, chans), BF),) * 2,
        in_specs=[vmem] * 7,
        out_specs=(vmem,) * 3,
        compiler_params=params,
        name="edges",
    )(x, c, col_odd, col_even, w1, *vecs[:2])
    row_even, row_odd = swap_edges(to_even, to_odd, "row")
    acts, gcat, d1, back_in, g1_in, gw3, full, gw1, xt = pl.pallas_call(
        functools.partial(inner_kernel, inner=inner, **sizes),
        out_shape=(
            shape((rows, wide, 3 * inner), BF),
            shape((rows - 2, wide, 3 * inner), BF),
            shape((rows * cols, inner), F32),
            shape(((rows - 2) * cols, chans), F32),
            shape(((rows - 4) * cols, inner), BF),
            shape((inner, chans), F32),
            shape((3, inner, 3 * inner), F32),
            shape((chans, inner), F32),
            shape((chans, 4 * cols), BF),
        ),
        in_specs=[vmem] * 14,
        out_specs=(vmem,) * 9,
        scratch_shapes=[pltpu.VMEM((rows, wide, chans), BF), pltpu.VMEM((rows, wide, chans), BF)],
        compiler_params=params,
        name="inner",
    )(x, c, strip, *shared)
    shares, g1_rim, back_rim = pl.pallas_call(
        functools.partial(rim_kernel, inner=inner, group_ch=group_ch, **sizes),
        out_shape=(
            shape((2, n_dp, half_rows, inner), F32),
            shape((4 * cols, inner), BF),
            shape((2 * cols, chans), F32),
        ),
        in_specs=[vmem] * 25,
        out_specs=(vmem,) * 3,
        scratch_shapes=[pltpu.VMEM((4, wide, 3 * inner), BF)] * 2 + [pltpu.VMEM((2, message, chans), BF)],
        compiler_params=params,
        name="rim",
    )(x, c, strip, row_even, row_odd, *shared, acts, gcat, d1, gw3, full, gw1, xt, same, pick)
    near = [(i, i ^ 1) for i in range(n_row)]
    shares = (shares[0] + lax.ppermute(shares[1].astype(BF), "row", near).astype(F32)).astype(BF)
    g1_rim, shares = lax.optimization_barrier((g1_rim, shares))
    input_grad = pl.pallas_call(
        functools.partial(out_kernel, **sizes),
        out_shape=shape((rows, cols, chans), BF),
        in_specs=[vmem] * 5,
        out_specs=vmem,
        compiler_params=params,
        name="out",
    )(g1_in, g1_rim, back_in, back_rim, w1)
    held = n_dp
    while held > 1:
        held //= 2
        other = crossed(shares[held:], ("dp", held), ("dp", held))
        shares = (shares[:held].astype(F32) + other.astype(F32)).astype(BF)
    total = shares[0]
    steps = [("row", 1 << k) for k in range(1, n_row.bit_length() - 1)]
    steps += [("col", 1 << k) for k in reversed(range(n_col.bit_length() - 1))]
    for i, step in enumerate(steps):
        other = crossed(total, step, steps[(i + 1) % len(steps)])
        if i == 0:
            input_grad, other = lax.optimization_barrier((input_grad, other))
        summed = total.astype(F32) + other.astype(F32)
        total = summed.astype(BF)
    pixels = rows * cols * n_dp * n_row * n_col
    reduce_grad, group_grad, expand_grad = pl.pallas_call(
        functools.partial(
            last_kernel, scale=pixels**-0.5, one=one, three=three, chans=chans, inner=inner, group_ch=group_ch
        ),
        out_shape=(
            jax.ShapeDtypeStruct((one, inner), F32),
            jax.ShapeDtypeStruct((3, 3, group_ch, three), F32),
            jax.ShapeDtypeStruct((three, chans), F32),
        ),
        in_specs=[vmem, vmem],
        out_specs=(pl.BlockSpec(memory_space=pl.ANY),) * 3,
        scratch_shapes=[
            pltpu.VMEM((one, inner), F32),
            pltpu.VMEM((3, 3, group_ch, three), F32),
            pltpu.VMEM((three, chans), F32),
            pltpu.SemaphoreType.DMA((3,)),
        ],
        compiler_params=pltpu.CompilerParams(vmem_limit_bytes=2 << 20),
        name="last",
    )(summed, lax.ppermute(summed, "row", near))
    return input_grad[None], reduce_grad, jnp.transpose(group_grad, (3, 0, 1, 2)), expand_grad


def solution(mesh):
    image = P("dp", "row", "col", None)
    return jax.shard_map(
        body,
        mesh=mesh,
        in_specs=(image,) + (P(),) * 9 + (image,),
        out_specs=(image, P("dp", None), P("dp", None, None, None), P("dp", None)),
        check_vma=False,
    )
```
